256 devices in a mesh: read: 32 (over z_lo, x, core), pos: 8 (over y, z_hi).
Axes of the slice: x: 4, y: 4, z: 8 (z_hi: 2, z_lo: 4; z = z_hi * 4 + z_lo), core: 2. Of those that a mesh axis runs over, the one named last changes fastest.
Arguments:
- features: bfloat16 [128, 256, 768], P('read', 'pos'), may hold values from -6 to 6
- grad_out: bfloat16 [128, 256, 768], P('read', 'pos'), may hold values from -16 to 16
- weights: bfloat16 [4, 768, 768], replicated, may hold values from -0.21875 to 0.21875
- read_start: int32 [128], replicated, may hold values from 0 to 127
- read_end: int32 [128], replicated, may hold values from 129 to 256
Outputs:
- grad_input: bfloat16 [128, 256, 768], P('read', 'pos')
- weight_grads: float32 [768, 3072], P(('read', 'pos'))
The draws below stay inside these ranges and needn't reach their ends.
Inputs may be any that keep to these rules, and one draw needn't show every extreme that they name: read_end is above read_start for every read.
All inputs are finite; a program needn't handle non-finite values.
Results may differ from the reference program's by a relative error of at most 0.0086.
Values may be sent and summed in bfloat16 or wider, within the bound.
A program may use at most 128 MiB of HBM per device.

```python
import math
import jax
import jax.numpy as jnp
from jax import lax

D = 768
HEADS = 12
HEAD_DIM = 64
READS = 128
COLS = 256


def touch_ends(values, stream_key, least, high):
    dims = values.shape
    spot = [jax.random.randint(jax.random.fold_in(stream_key, axis), (), 0, dims[axis]) for axis in range(len(dims))]
    values = values.at[tuple(spot)].set(least)
    longest = dims.index(max(dims))
    spot[longest] = (spot[longest] + 1) % dims[longest]
    return values.at[tuple(spot)].set(high)


def raised(result, stream_key, source, target, parts, factor):
    owner, partner = [(jnp.arange(result.shape[axis_at]) // (result.shape[axis_at] // parts)).reshape([-1 if axis == axis_at else 1 for axis in range(result.ndim)]) for axis_at in (source, target)]
    chosen = jax.random.permutation(stream_key, parts)[partner]
    strong = (owner == chosen) | (owner == (partner + parts // 2) % parts)
    return jnp.where(strong, factor * result, result)


def block_levels(key, dims, cuts, least, largest):
    def one(position, parts):
        steps = jax.random.uniform(jax.random.fold_in(jax.random.fold_in(key, 6), position), (parts,), jnp.float32, least / len(cuts), largest / len(cuts))
        return jnp.repeat(jnp.exp(steps), dims[position] // parts).reshape((-1,) + (1,) * (len(dims) - position - 1))

    loudness = one(*cuts[0])
    for cut in cuts[1:]:
        loudness = loudness * one(*cut)
    return loudness


def scatter_about(own_key, shape, spread, most, pieces=(), kind=jnp.bfloat16):
    result = jax.random.normal(own_key, shape, jnp.float32) * spread
    if len(pieces) > 0:
        result = block_levels(own_key, shape, pieces, -0.22, 0.18) * result
    return jnp.clip(result, min=-most, max=most).astype(kind)


def bell_draw_with(stream_key, extent, scale, reach, shards, heavy, held_as=jnp.bfloat16):
    array = scale * jax.random.normal(stream_key, extent, jnp.float32)
    if shards:
        array = array * block_levels(stream_key, extent, shards, -0.22, 0.18)
    return jnp.clip(raised(array, jax.random.fold_in(stream_key, 3), *heavy), -reach, reach).astype(held_as)


def setup_inputs(seed: int = 0) -> dict:
    arg_keys = jax.random.split(jax.random.key(seed), 6)
    return {
        "features": bell_draw_with(arg_keys[0], (READS, COLS, D), 1.0, 6.0, ((0, 32), (1, 8)), (0, 2, 32, 2.75)),
        "grad_out": scatter_about(arg_keys[1], (READS, COLS, D), 4.0, 16.0, ((0, 32), (1, 8))),
        "weights": scatter_about(arg_keys[2], (4, D, D), D ** -0.5, 0.21875),
        "read_start": touch_ends(jax.random.randint(arg_keys[3], (READS,), 0, COLS // 2), jax.random.fold_in(arg_keys[3], 1), 0, (COLS // 2) - 1).astype(jnp.int32),
        "read_end": touch_ends(jax.random.randint(arg_keys[4], (READS,), COLS // 2 + 1, COLS + 1), jax.random.fold_in(arg_keys[4], 1), COLS // 2 + 1, COLS).astype(jnp.int32),
    }


def reference(features, grad_out, weights, read_start, read_end):
    reads, cols, width = features.shape
    columns = jnp.arange(cols, dtype=jnp.int32)
    covered = ((columns[None, :] >= read_start[:, None]) & (columns[None, :] < read_end[:, None])).astype(jnp.float32)
    values32 = features.reshape(-1, width).astype(jnp.float32)
    inverse = lax.rsqrt(lax.optimization_barrier(jnp.mean(values32 * values32, -1, keepdims=True)) + 1e-05)
    normed = values32 * inverse
    normed_b = normed.astype(jnp.bfloat16)
    keep_mask = covered.reshape(-1, 1)
    query = (jnp.dot(normed_b, weights[0], preferred_element_type=jnp.float32) * keep_mask).astype(jnp.bfloat16)
    keys = (jnp.dot(normed_b, weights[1], preferred_element_type=jnp.float32) * keep_mask).astype(jnp.bfloat16)
    vals = (jnp.dot(normed_b, weights[2], preferred_element_type=jnp.float32) * keep_mask).astype(jnp.bfloat16)
    grad_flat = grad_out.reshape(-1, width)
    back_out = jnp.dot(grad_flat, weights[3].T, preferred_element_type=jnp.float32).astype(jnp.bfloat16)
    shape4 = (reads, cols, HEADS, HEAD_DIM)
    query4 = query.reshape(shape4).astype(jnp.float32)
    keys4 = keys.reshape(shape4).astype(jnp.float32)
    vals4 = vals.reshape(shape4).astype(jnp.float32)
    back4 = back_out.reshape(shape4).astype(jnp.float32)
    scale = 1.0 / math.sqrt(HEAD_DIM * COLS)
    logits = jnp.einsum('rchd,schd->hrs', query4, keys4) * scale
    expon = jnp.exp(logits)
    probs = expon / lax.optimization_barrier(jnp.sum(expon, -1, keepdims=True))
    probs_b = probs.astype(jnp.bfloat16).astype(jnp.float32)
    output = jnp.einsum('hrs,schd->rchd', probs_b, vals4).astype(jnp.bfloat16)
    slopes = jnp.einsum('rchd,schd->hrs', back4, vals4)
    mixed = (scale * probs * (slopes - lax.optimization_barrier(jnp.sum(probs * slopes, -1, keepdims=True)))).astype(jnp.bfloat16).astype(jnp.float32)
    keep4 = covered[:, :, None, None]
    grad_query = (jnp.einsum('hrs,schd->rchd', mixed, keys4) * keep4).astype(jnp.bfloat16).reshape(-1, width)
    grad_keys = (jnp.einsum('hrs,rchd->schd', mixed, query4) * keep4).astype(jnp.bfloat16).reshape(-1, width)
    grad_values = (jnp.einsum('hrs,rchd->schd', probs_b, back4) * keep4).astype(jnp.bfloat16).reshape(-1, width)
    output_flat = output.reshape(-1, width)
    blocks = [jnp.dot(normed_b.T, grad_query, preferred_element_type=jnp.float32), jnp.dot(normed_b.T, grad_keys, preferred_element_type=jnp.float32), jnp.dot(normed_b.T, grad_values, preferred_element_type=jnp.float32), jnp.dot(output_flat.T, grad_flat, preferred_element_type=jnp.float32)]
    weight_grads = jnp.concatenate(blocks, axis=1)
    grad_norm = jnp.dot(grad_query, weights[0].T, preferred_element_type=jnp.float32)
    grad_norm = grad_norm + jnp.dot(grad_keys, weights[1].T, preferred_element_type=jnp.float32)
    grad_norm = grad_norm + jnp.dot(grad_values, weights[2].T, preferred_element_type=jnp.float32)
    grad_input = inverse * (grad_norm - normed * lax.optimization_barrier(jnp.mean(grad_norm * normed, -1, keepdims=True)))
    return (grad_input.astype(jnp.bfloat16).reshape(reads, cols, width), weight_grads)
```

```python
import math

import jax
import jax.numpy as jnp
from jax import lax
from jax.experimental import pallas as pl
from jax.experimental.pallas import tpu as pltpu
from jax.sharding import PartitionSpec as P

F32, BF16, I32 = jnp.float32, jnp.bfloat16, jnp.int32
D = 768
WIN = 256
READS = 128
SCALE = 1.0 / 128.0
EPS = 1e-05
OWNERS = (0, 3, 5)


def nt(a, b):
    return lax.dot_general(a, b, (((1,), (1,)), ((), ())), preferred_element_type=F32)


def nn(a, b):
    return jnp.dot(a, b, preferred_element_type=F32)


def iota(shape, dim):
    return lax.broadcasted_iota(I32, shape, dim)


def hot(cond):
    return jnp.where(cond, 1.0, 0.0).astype(BF16)


def read_of(g, m):
    zl, xp = lax.div(g, 2), lax.rem(g, 2)
    xi, c = lax.div(m, 2), lax.rem(m, 2)
    return zl * 8 + (xi + xp * (3 - 2 * xi)) * 2 + c


def kernel(
    feat, gout, starts, ends, w_hbm, gin_out, wj_out, w3_out,
    wv, ww, w3, a_buf, fg, fp, gp, nb, heads, lbuf, rl, acc, rz, pm, gr, ob, rg,
    nbt, obt, wg, rw, wz, rwz, fd, rj, r3, gi, ogi,
    s_w, sa_s, sa_r, sc_s, sc_r, sx_s, sx_r, sf_s, sf_r, sl_s, sl_r, sz_s, sz_r,
    sq_s, sq_r, sp_s, sp_r, sg_s, sg_r, sd_s, sd_r, se_s, se_r, sj_s, sj_r, s3_s, s3_r, si_s, si_r,
):
    ri, pi = lax.axis_index("read"), lax.axis_index("pos")
    zl, x, c = lax.div(ri, 8), lax.rem(lax.div(ri, 2), 4), lax.rem(ri, 2)
    xp = lax.div(x, 2)
    xi = x + xp * (3 - 2 * x)
    y, zh = lax.div(pi, 2), lax.rem(pi, 2)
    g, m = zl * 2 + xp, xi * 2 + c
    e, ze = y * 2 + xp, zh * 4 + zl
    par = lax.rem(m, 2)
    off = pl.multiple_of(128 * lax.div(3 * m, 2), 128)
    core_m = xi * 2 + (1 - c)
    side_m = (1 - xi) * 2 + c
    far_m = (1 - xi) * 2 + (1 - c)

    def remote(src, dst, ss, rs, dev):
        return pltpu.make_async_remote_copy(
            src_ref=src, dst_ref=dst, send_sem=ss, recv_sem=rs,
            device_id=dev, device_id_type=pl.DeviceIdType.MESH,
        )

    def mate(mm):
        return (read_of(g, mm), pi)

    def over_g(gg):
        return (read_of(gg, m), pi)

    def over_e(ee):
        return (read_of(zl * 2 + lax.rem(ee, 2), m), lax.div(ee, 2) * 2 + zh)

    def over_z(zz):
        return (read_of(lax.rem(zz, 4) * 2 + xp, m), y * 2 + lax.div(zz, 4))

    def ahead(v, d):
        return lax.rem(v + d, 8)

    def behind(v, d):
        return lax.rem(v + 8 - d, 8)

    turned = (read_of(m * 2 + xp, zl), pi)
    sends = []

    win_copies = [
        pltpu.make_async_copy(w_hbm.at[j, :, pl.ds(off, WIN)], ww.at[j], s_w.at[j]) for j in range(3)
    ]
    win_copies.append(pltpu.make_async_copy(w_hbm.at[3, pl.ds(off, WIN), :], w3, s_w.at[3]))
    full_copies = [pltpu.make_async_copy(w_hbm.at[j], wv.at[j], s_w.at[4 + j]) for j in range(3)]
    for copy in win_copies + full_copies:
        copy.start()

    barrier = pltpu.get_barrier_semaphore()

    def greet(dev):
        pl.semaphore_signal(barrier, inc=1, device_id=dev, device_id_type=pl.DeviceIdType.MESH)

    for d in range(1, 8):
        greet(over_g(ahead(g, d)))
        greet(over_e(ahead(e, d)))
        greet(over_z(ahead(ze, d)))
    for mm in (core_m, side_m, far_m):
        greet(mate(mm))

    @pl.when(zl != m)
    def _():
        greet(turned)

    ro, co = iota((128, 128), 0), iota((128, 128), 1)
    to_groups = hot(co == ((ro >> 2) & 3) * 32 + (ro >> 4) * 4 + (ro & 3))
    for t, ref in ((0, feat), (1, gout)):
        a_buf[t] = nn(to_groups, ref[...].reshape(128, D)).astype(BF16).reshape(8, 16, D)

    @pl.when(zl == m)
    def _():
        pl.semaphore_wait(barrier, 24)

    @pl.when(zl != m)
    def _():
        pl.semaphore_wait(barrier, 25)

    for t in range(2):
        for d in range(1, 8):
            gg = ahead(g, d)
            copy = remote(a_buf.at[t, gg], fg.at[t, m, g], sa_s.at[t, d], sa_r.at[t, d], over_g(gg))
            copy.start()
            sends.append(copy)
        fg[t, m, g] = a_buf[t, g]

    def first(t, d):
        gs = behind(g, d)
        slot = fg.at[t, m, gs]
        if d > 0:
            remote(slot, slot, sa_s.at[t, d], sa_r.at[t, d], over_g(gs)).wait_recv()
        for ss, rs, mm in ((sx_s, sx_r, side_m), (sc_s, sc_r, core_m)):
            copy = remote(slot, slot, ss.at[t, d], rs.at[t, d], mate(mm))
            copy.start()
            sends.append(copy)

    def second(t, d):
        slot = fg.at[t, side_m, behind(g, d)]
        remote(slot, slot, sx_s.at[t, d], sx_r.at[t, d], mate(side_m)).wait_recv()
        copy = remote(slot, slot, sf_s.at[t, d], sf_r.at[t, d], mate(core_m))
        copy.start()
        sends.append(copy)

    def third(t, d):
        slot = fg.at[t, core_m, behind(g, d)]
        remote(slot, slot, sc_s.at[t, d], sc_r.at[t, d], mate(core_m)).wait_recv()
        slot = fg.at[t, far_m, behind(g, d)]
        remote(slot, slot, sf_s.at[t, d], sf_r.at[t, d], mate(core_m)).wait_recv()

    nat = iota((READS, READS), 0)
    gs_v, ms_v, r_v = (nat >> 2) & 7, nat >> 5, nat & 3
    xi_v, xp_v = ms_v >> 1, gs_v & 1
    nat = 4 * ((gs_v >> 1) * 8 + (xi_v + xp_v * (3 - 2 * xi_v)) * 2 + (ms_v & 1)) + r_v
    pick = iota((READS, READS), 1) == nat
    begin = jnp.sum(jnp.where(pick, starts[...].astype(F32), 0.0), axis=1, keepdims=True)
    close = jnp.sum(jnp.where(pick, ends[...].astype(F32), 0.0), axis=1, keepdims=True)

    def cover(k):
        col = (32 * pi + 4 * g + k).astype(F32)
        return jnp.where(col >= begin, 1.0, 0.0) * jnp.where(col < close, 1.0, 0.0)

    def to_columns(k):
        return hot(iota((READS, 512), 1) == iota((READS, 512), 0) * 4 + k)

    for d in range(8):
        first(0, d)
        if d > 0:
            second(0, d - 1)
    second(0, 7)
    for d in range(8):
        third(0, d)
    for copy in win_copies:
        copy.wait()

    for k in range(4):
        f32 = nn(to_columns(k), fg[0].reshape(512, D))
        fp[k] = f32.astype(BF16)
        inverse = lax.rsqrt(jnp.mean(f32 * f32, -1, keepdims=True) + EPS)
        normed_b = (f32 * inverse).astype(BF16)
        nb[k] = normed_b
        keep = cover(k)
        for j in range(3):
            part = (nn(normed_b, ww[j]) * keep).astype(BF16)
            heads[j, 0, :, k * 128 : (k + 1) * 128] = part[:, :128]
            heads[j, 1, :, k * 128 : (k + 1) * 128] = part[:, 128:]
        first(1, 2 * k)
        if k > 0:
            second(1, 2 * k - 1)
        first(1, 2 * k + 1)
        second(1, 2 * k)

    low = jnp.where((iota((1, 512), 1) & 127) < 64, 1.0, 0.0)
    high = 1.0 - low
    par_f = par.astype(F32)
    own = low * (1.0 - par_f) + high * par_f
    plan = ((0, high), (1, low), (par, own))

    def scores(which, left, right):
        for h, (t, mask) in enumerate(plan):
            lbuf[which, h * 128 : (h + 1) * 128, :] = nt(heads[left, t] * mask.astype(BF16), heads[right, t])
        for d in range(1, 8):
            ee = ahead(e, d)
            copy = remote(
                lbuf.at[which, pl.ds(pl.multiple_of(48 * ee, 16), 48), :], rl.at[which, d],
                sl_s.at[which, d], sl_r.at[which, d], over_e(ee),
            )
            copy.start()
            sends.append(copy)

    scores(0, 0, 1)
    second(1, 7)
    for d in range(8):
        third(1, d)
    for k in range(4):
        col_grad = nn(to_columns(k), fg[1].reshape(512, D)).astype(BF16)
        gp[k] = col_grad
        part = nt(col_grad, w3[...]).astype(BF16)
        heads[3, 0, :, k * 128 : (k + 1) * 128] = part[:, :128]
        heads[3, 1, :, k * 128 : (k + 1) * 128] = part[:, 128:]
    scores(1, 3, 2)

    def turn(i, carry):
        w, col = iota((96, D), 0), iota((96, D), 1)
        yy, xx = lax.div(i, 2), lax.rem(i, 2)
        xi2 = (w >> 1) & 1
        row = (
            ((w >> 3) & 3) * 192 + (xi2 + xx * (3 - 2 * xi2)) * 48 + (w & 1) * 24
            + yy * 6 + ((w >> 2) & 1) * 3 + (w >> 5)
        )
        nbt[pl.ds(pl.multiple_of(i * 96, 16), 96), :] = nt(hot(col == row), nb[...].reshape(512, D)).astype(BF16)
        return carry

    lax.fori_loop(0, 8, turn, 0)

    for which in range(2):
        total = lbuf[which, pl.ds(pl.multiple_of(48 * e, 16), 48), :]
        for d in range(1, 8):
            remote(
                rl.at[which, d], rl.at[which, d], sl_s.at[which, d], sl_r.at[which, d], over_e(behind(e, d))
            ).wait_recv()
            total = total + rl[which, d]
        acc[:, which * 128 : (which + 1) * 128] = total

    late = []
    for o, place in enumerate(OWNERS):
        dev = over_z(place)
        copy = remote(acc.at[pl.ds(16 * o, 16), :], rz.at[ze], sz_s.at[o], sz_r.at[ze], dev)

        @pl.when(ze != place)
        def _():
            copy.start()

        late.append((place, copy))

    for o, place in enumerate(OWNERS):
        rows = pl.ds(pl.multiple_of(48 * e + 16 * o, 16), 16)

        @pl.when(ze == place)
        def _():
            total = acc[16 * o : 16 * o + 16, :]
            for s in range(8):
                if s != place:
                    remote(rz.at[s], rz.at[s], sz_s.at[o], sz_r.at[s], over_z(s)).wait_recv()
                    total = total + rz[s]
            expon = jnp.exp(total[:, :128] * SCALE)
            probs = expon / jnp.sum(expon, -1, keepdims=True)
            slopes = total[:, 128:]
            mixed = SCALE * probs * (slopes - jnp.sum(probs * slopes, -1, keepdims=True))
            pm[rows, 0:128] = probs.astype(BF16)
            pm[rows, 128:256] = mixed.astype(BF16)
            out = []
            for s in range(8):
                if s != place:
                    copy = remote(pm.at[rows, :], pm.at[rows, :], sq_s.at[s], sq_r.at[o], over_z(s))
                    copy.start()
                    out.append(copy)
            for copy in out:
                copy.wait_send()

    for o, place in enumerate(OWNERS):
        rows = pl.ds(pl.multiple_of(48 * e + 16 * o, 16), 16)

        @pl.when(ze != place)
        def _():
            remote(pm.at[rows, :], pm.at[rows, :], sq_s.at[0], sq_r.at[o], over_z(place)).wait_recv()

    def chunk(ee):
        return pm.at[pl.ds(pl.multiple_of(48 * ee, 16), 48), :]

    for d in range(1, 8):
        copy = remote(chunk(e), chunk(e), sp_s.at[d], sp_r.at[d], over_e(ahead(e, d)))
        copy.start()
        sends.append(copy)
    keeps = jnp.concatenate([jnp.broadcast_to(cover(k), (READS, 128)) for k in range(4)], axis=1)
    for d in range(1, 8):
        ee = behind(e, d)
        remote(chunk(ee), chunk(ee), sp_s.at[d], sp_r.at[d], over_e(ee)).wait_recv()

    eye = hot(ro == co)
    made = []
    for h, (t, _) in enumerate(plan):
        probs_b = pm[h * 128 : (h + 1) * 128, 0:128]
        mixed = pm[h * 128 : (h + 1) * 128, 128:256]
        made.append(
            (
                nn(mixed, heads[1, t]),
                nn(nt(eye, mixed).astype(BF16), heads[0, t]),
                nn(nt(eye, probs_b).astype(BF16), heads[3, t]),
                nn(probs_b, heads[2, t]),
            )
        )
    for j in range(4):
        tile0 = made[0][j] * high + made[2][j] * (low * (1.0 - par_f))
        tile1 = made[1][j] * low + made[2][j] * (high * par_f)
        for t, tile in ((0, tile0), (1, tile1)):
            if j < 3:
                tile = tile * keeps
            tile = tile.astype(BF16)
            for k in range(4):
                if j < 3:
                    gr[j, k, :, t * 128 : (t + 1) * 128] = tile[:, k * 128 : (k + 1) * 128]
                else:
                    ob[k, :, t * 128 : (t + 1) * 128] = tile[:, k * 128 : (k + 1) * 128]

    def rows_of(mm):
        return pl.ds(pl.multiple_of(32 * mm, 32), 32)

    for d, mm in ((1, side_m), (2, far_m), (3, core_m)):
        copy = remote(gr.at[:, :, rows_of(mm), :], rg.at[m], sg_s.at[d], sg_r.at[d], mate(mm))
        copy.start()
        sends.append(copy)
    rg[m] = gr[:, :, rows_of(m), :]

    ow, cw = iota((256, 256), 0), iota((256, 256), 1)
    u, yy, xx = ow & 31, ow >> 6, (ow >> 5) & 1
    xi2 = (u >> 1) & 1
    local = (
        64 * par + (xi2 + xx * (3 - 2 * xi2)) * 48 + (u & 1) * 24 + yy * 6 + ((u >> 2) & 1) * 3 + (u >> 3)
    )
    obt[...] = nt(hot(jnp.where(u < 24, local, -1) == cw), ob[...].reshape(512, WIN)).astype(BF16)

    def wgrad_copy(d):
        ee = ahead(e, d)
        return remote(wg.at[ee], rw.at[d], sd_s.at[d], sd_r.at[d], over_e(ee))

    def wgrad(d, carry):
        ee = ahead(e, d)
        left = nbt[pl.ds(pl.multiple_of(ee * 96, 16), 96), :]
        for j in range(3):
            wg[ee, 0:96, j * WIN : (j + 1) * WIN] = nn(left, gr[j].reshape(512, WIN)).astype(BF16)
        last = obt[pl.ds(pl.multiple_of(ee * 32, 32), 32), :]
        wg[ee, 96:128, :] = nn(last, gp[...].reshape(512, D)).astype(BF16)

        @pl.when(d < 8)
        def _():
            wgrad_copy(d).start()

        return carry

    lax.fori_loop(1, 9, wgrad, 0)

    for d, mm in ((1, side_m), (2, far_m), (3, core_m)):
        remote(gr.at[:, :, rows_of(mm), :], rg.at[mm], sg_s.at[d], sg_r.at[d], mate(mm)).wait_recv()
    for copy in full_copies:
        copy.wait()
    grad_norm = jnp.zeros((128, D), F32)
    for mm in range(4):
        lane = 128 * ((3 * mm) // 2)
        for j in range(3):
            grad_norm = grad_norm + nt(rg[mm, j].reshape(128, WIN), wv[j, :, lane : lane + WIN])
    mine = fp[:, rows_of(m), :].reshape(128, D).astype(F32)
    inverse = lax.rsqrt(jnp.mean(mine * mine, -1, keepdims=True) + EPS)
    normed = mine * inverse
    result = (inverse * (grad_norm - normed * jnp.mean(grad_norm * normed, -1, keepdims=True))).astype(BF16)
    to_sources = hot(co == (ro & 3) * 32 + (ro >> 2))
    gi[...] = nn(to_sources, result).astype(BF16).reshape(8, 16, D)
    for d in range(1, 8):
        gg = ahead(g, d)
        copy = remote(gi.at[gg], ogi.at[g], si_s.at[d], si_r.at[d], over_g(gg))
        copy.start()
        sends.append(copy)
    ogi[g] = gi[g]

    total = wg[e].astype(F32)
    for d in range(1, 8):
        remote(rw.at[d], rw.at[d], sd_s.at[d], sd_r.at[d], over_e(behind(e, d))).wait_recv()
        total = total + rw[d].astype(F32)
    v, zz = ro & 15, ro >> 4
    src = (v >> 2) * 32 + (zz & 3) * 8 + (zz >> 2) * 4 + (v & 3)
    src = jnp.where(v < 12, src, jnp.where(v < 15, 96 + (v - 12) * 8 + zz, -1))
    wz[...] = nn(hot(co == src), total.astype(BF16)).astype(BF16).reshape(8, 16, D)
    for d in range(1, 8):
        zz2 = ahead(ze, d)
        copy = remote(wz.at[zz2], rwz.at[d], se_s.at[d], se_r.at[d], over_z(zz2))
        copy.start()
        sends.append(copy)

    for d in range(1, 8):
        slot = ogi.at[behind(g, d)]
        remote(slot, slot, si_s.at[d], si_r.at[d], over_g(behind(g, d))).wait_recv()
    from_groups = hot(co == ((ro >> 2) & 7) * 16 + (ro >> 5) * 4 + (ro & 3))
    gin_out[...] = nn(from_groups, ogi[...].reshape(128, D)).astype(BF16).reshape(4, 32, D)

    total = wz[ze].astype(F32)
    for d in range(1, 8):
        remote(rwz.at[d], rwz.at[d], se_s.at[d], se_r.at[d], over_z(behind(ze, d))).wait_recv()
        total = total + rwz[d].astype(F32)
    for mm in range(4):
        for t in range(3):
            fd[mm, t : t + 1, :] = total[t * 4 + mm : t * 4 + mm + 1, :]
        fd[mm, 3:8, :] = jnp.zeros((5, D), F32)
    fd[4, 0:3, :] = total[12:15, :]
    fd[4, 3:8, :] = jnp.zeros((5, D), F32)
    for d, mm in ((1, side_m), (2, far_m), (3, core_m)):
        copy = remote(fd.at[mm], rj.at[m], sj_s.at[d], sj_r.at[d], mate(mm))
        copy.start()
        sends.append(copy)
    rj[m] = fd[m]
    last = remote(fd.at[4], r3, s3_s.at[0], s3_r.at[0], turned)

    @pl.when(zl != m)
    def _():
        last.start()
        last.wait()

    @pl.when(zl == m)
    def _():
        r3[...] = fd[4]

    for d, mm in ((1, side_m), (2, far_m), (3, core_m)):
        remote(fd.at[mm], rj.at[mm], sj_s.at[d], sj_r.at[d], mate(mm)).wait_recv()
    wj_out[...] = rj[...]
    w3_out[...] = r3[...]

    for copy in sends:
        copy.wait_send()
    for d in range(1, 8):
        wgrad_copy(d).wait_send()
    for place, copy in late:

        @pl.when(ze != place)
        def _():
            copy.wait_send()


def shards(features, grad_out, weights, read_start, read_end):
    vm = pl.BlockSpec(memory_space=pltpu.VMEM)
    dma = pltpu.SemaphoreType.DMA
    grad_input, wj, w3 = pl.pallas_call(
        kernel,
        name="tied_rows",
        out_shape=(
            jax.ShapeDtypeStruct((4, 32, D), BF16),
            jax.ShapeDtypeStruct((4, 8, D), F32),
            jax.ShapeDtypeStruct((8, D), F32),
        ),
        in_specs=[vm, vm, vm, vm, pl.BlockSpec(memory_space=pl.ANY)],
        out_specs=(vm, vm, vm),
        scratch_shapes=[
            pltpu.VMEM((3, D, D), BF16),
            pltpu.VMEM((3, D, WIN), BF16),
            pltpu.VMEM((WIN, D), BF16),
            pltpu.VMEM((2, 8, 16, D), BF16),
            pltpu.VMEM((2, 4, 8, 16, D), BF16),
            pltpu.VMEM((4, READS, D), BF16),
            pltpu.VMEM((4, READS, D), BF16),
            pltpu.VMEM((4, READS, D), BF16),
            pltpu.VMEM((4, 2, READS, 512), BF16),
            pltpu.VMEM((2, 384, 128), F32),
            pltpu.VMEM((2, 8, 48, 128), F32),
            pltpu.VMEM((48, 256), F32),
            pltpu.VMEM((8, 16, 256), F32),
            pltpu.VMEM((384, 256), BF16),
            pltpu.VMEM((3, 4, READS, WIN), BF16),
            pltpu.VMEM((4, READS, WIN), BF16),
            pltpu.VMEM((4, 3, 4, 32, WIN), BF16),
            pltpu.VMEM((D, 512), BF16),
            pltpu.VMEM((WIN, 512), BF16),
            pltpu.VMEM((8, 128, D), BF16),
            pltpu.VMEM((8, 128, D), BF16),
            pltpu.VMEM((8, 16, D), BF16),
            pltpu.VMEM((8, 16, D), BF16),
            pltpu.VMEM((5, 8, D), F32),
            pltpu.VMEM((4, 8, D), F32),
            pltpu.VMEM((8, D), F32),
            pltpu.VMEM((8, 16, D), BF16),
            pltpu.VMEM((8, 16, D), BF16),
            dma((7,)),
            dma((2, 8)), dma((2, 8)), dma((2, 8)), dma((2, 8)), dma((2, 8)), dma((2, 8)), dma((2, 8)), dma((2, 8)),
            dma((2, 8)), dma((2, 8)),
            dma((3,)), dma((8,)),
            dma((8,)), dma((3,)),
            dma((8,)), dma((8,)),
            dma((4,)), dma((4,)),
            dma((8,)), dma((8,)),
            dma((8,)), dma((8,)),
            dma((4,)), dma((4,)),
            dma((1,)), dma((1,)),
            dma((8,)), dma((8,)),
        ],
        compiler_params=pltpu.CompilerParams(
            collective_id=0, has_side_effects=True, vmem_limit_bytes=56 * 1024 * 1024
        ),
    )(features, grad_out, read_start.reshape(1, READS), read_end.reshape(1, READS), weights)
    blocks = []
    for j in range(3):
        for mm in range(4):
            at = j * WIN + 64 * (mm % 2)
            blocks.append(wj[mm, 0:3, at : at + 192])
    blocks.append(w3[0:3])
    return (grad_input, jnp.concatenate(blocks, axis=1))


def solution(mesh):
    in_specs = (P("read", "pos", None), P("read", "pos", None), P(), P(), P())
    out_specs = (P("read", "pos", None), P(("read", "pos"), None))
    return jax.shard_map(shards, mesh=mesh, in_specs=in_specs, out_specs=out_specs, check_vma=False)
```

```python
import math

import jax
import jax.numpy as jnp
from jax import lax
from jax.experimental import pallas as pl
from jax.experimental.pallas import tpu as pltpu
from jax.sharding import PartitionSpec as P

F32, BF16, I32 = jnp.float32, jnp.bfloat16, jnp.int32
D = 768
WIN = 256
READS = 128
SCALE = 1.0 / 128.0
EPS = 1e-05
OWNERS = (0, 3, 5)


def nt(a, b):
    return lax.dot_general(a, b, (((1,), (1,)), ((), ())), preferred_element_type=F32)


def nn(a, b):
    return jnp.dot(a, b, preferred_element_type=F32)


def iota(shape, dim):
    return lax.broadcasted_iota(I32, shape, dim)


def hot(cond):
    return jnp.where(cond, 1.0, 0.0).astype(BF16)


def read_of(g, m):
    zl, xp = lax.div(g, 2), lax.rem(g, 2)
    xi, c = lax.div(m, 2), lax.rem(m, 2)
    return zl * 8 + (xi + xp * (3 - 2 * xi)) * 2 + c


def kernel(
    feat_hbm, gout_hbm, starts_hbm, ends_hbm, w_hbm, gin_out, wgrad_out,
    feat, gout, starts, ends, gin, wsum, wv, ww, w3, a_buf, fg, fp, gp, nb, heads, lbuf, rl, acc, rz, pm, gr, ob, rg,
    nbt, obt, wg, rw, wz, rwz, fd, rj, r3, gi, ogi,
    s_in, s_w, sa_s, sa_r, sc_s, sc_r, sx_s, sx_r, sf_s, sf_r, sl_s, sl_r, sz_s, sz_r,
    sq_s, sq_r, sp_s, sp_r, sg_s, sg_r, sd_s, sd_r, se_s, se_r, sj_s, sj_r, s3_s, s3_r, si_s, si_r,
):
    ri, pi = lax.axis_index("read"), lax.axis_index("pos")
    zl, x, c = lax.div(ri, 8), lax.rem(lax.div(ri, 2), 4), lax.rem(ri, 2)
    xp = lax.div(x, 2)
    xi = x + xp * (3 - 2 * x)
    y, zh = lax.div(pi, 2), lax.rem(pi, 2)
    g, m = zl * 2 + xp, xi * 2 + c
    e, ze = y * 2 + xp, zh * 4 + zl
    par = lax.rem(m, 2)
    off = pl.multiple_of(128 * lax.div(3 * m, 2), 128)
    core_m = xi * 2 + (1 - c)
    side_m = (1 - xi) * 2 + c
    far_m = (1 - xi) * 2 + (1 - c)

    def remote(src, dst, ss, rs, dev):
        return pltpu.make_async_remote_copy(
            src_ref=src, dst_ref=dst, send_sem=ss, recv_sem=rs,
            device_id=dev, device_id_type=pl.DeviceIdType.MESH,
        )

    def mate(mm):
        return (read_of(g, mm), pi)

    def over_g(gg):
        return (read_of(gg, m), pi)

    def over_e(ee):
        return (read_of(zl * 2 + lax.rem(ee, 2), m), lax.div(ee, 2) * 2 + zh)

    def over_z(zz):
        return (read_of(lax.rem(zz, 4) * 2 + xp, m), y * 2 + lax.div(zz, 4))

    def ahead(v, d):
        return lax.rem(v + d, 8)

    def behind(v, d):
        return lax.rem(v + 8 - d, 8)

    turned = (read_of(m * 2 + xp, zl), pi)
    sends = []

    in_copies = [
        pltpu.make_async_copy(src, dst, s_in.at[i])
        for i, (src, dst) in enumerate(
            ((feat_hbm, feat), (gout_hbm, gout), (starts_hbm, starts), (ends_hbm, ends))
        )
    ]
    for copy in in_copies:
        copy.start()

    barrier = pltpu.get_barrier_semaphore()

    def greet(dev):
        pl.semaphore_signal(barrier, inc=1, device_id=dev, device_id_type=pl.DeviceIdType.MESH)

    for d in range(1, 8):
        greet(over_g(ahead(g, d)))
        greet(over_e(ahead(e, d)))
        greet(over_z(ahead(ze, d)))
    for mm in (core_m, side_m, far_m):
        greet(mate(mm))

    @pl.when(zl != m)
    def _():
        greet(turned)

    win_copies = [
        pltpu.make_async_copy(w_hbm.at[j, :, pl.ds(off, WIN)], ww.at[j], s_w.at[j]) for j in range(3)
    ]
    win_copies.append(pltpu.make_async_copy(w_hbm.at[3, pl.ds(off, WIN), :], w3, s_w.at[3]))
    full_copies = [pltpu.make_async_copy(w_hbm.at[j], wv.at[j], s_w.at[4 + j]) for j in range(3)]
    for copy in win_copies + full_copies:
        copy.start()

    for copy in in_copies:
        copy.wait()

    ro, co = iota((128, 128), 0), iota((128, 128), 1)
    to_groups = hot(co == ((ro >> 2) & 3) * 32 + (ro >> 4) * 4 + (ro & 3))
    for t, ref in ((0, feat), (1, gout)):
        a_buf[t] = nn(to_groups, ref[...].reshape(128, D)).astype(BF16).reshape(8, 16, D)

    @pl.when(zl == m)
    def _():
        pl.semaphore_wait(barrier, 24)

    @pl.when(zl != m)
    def _():
        pl.semaphore_wait(barrier, 25)

    for t in range(2):
        for d in range(1, 8):
            gg = ahead(g, d)
            copy = remote(a_buf.at[t, gg], fg.at[t, m, g], sa_s.at[t, d], sa_r.at[t, d], over_g(gg))
            copy.start()
            sends.append(copy)
        fg[t, m, g] = a_buf[t, g]

    def first(t):
        for d in range(1, 8):
            slot = fg.at[t, m, behind(g, d)]
            remote(slot, slot, sa_s.at[t, d], sa_r.at[t, d], over_g(behind(g, d))).wait_recv()
        for ss, rs, mm in ((sx_s, sx_r, side_m), (sc_s, sc_r, core_m)):
            copy = remote(fg.at[t, m], fg.at[t, m], ss.at[t], rs.at[t], mate(mm))
            copy.start()
            sends.append(copy)

    def second(t):
        slot = fg.at[t, side_m]
        remote(slot, slot, sx_s.at[t], sx_r.at[t], mate(side_m)).wait_recv()
        copy = remote(slot, slot, sf_s.at[t], sf_r.at[t], mate(core_m))
        copy.start()
        sends.append(copy)

    def third(t):
        slot = fg.at[t, core_m]
        remote(slot, slot, sc_s.at[t], sc_r.at[t], mate(core_m)).wait_recv()
        slot = fg.at[t, far_m]
        remote(slot, slot, sf_s.at[t], sf_r.at[t], mate(core_m)).wait_recv()

    nat = iota((READS, READS), 0)
    gs_v, ms_v, r_v = (nat >> 2) & 7, nat >> 5, nat & 3
    xi_v, xp_v = ms_v >> 1, gs_v & 1
    nat = 4 * ((gs_v >> 1) * 8 + (xi_v + xp_v * (3 - 2 * xi_v)) * 2 + (ms_v & 1)) + r_v
    pick = iota((READS, READS), 1) == nat
    begin = jnp.sum(jnp.where(pick, starts[...].astype(F32), 0.0), axis=1, keepdims=True)
    close = jnp.sum(jnp.where(pick, ends[...].astype(F32), 0.0), axis=1, keepdims=True)

    def cover(k):
        col = (32 * pi + 4 * g + k).astype(F32)
        return jnp.where(col >= begin, 1.0, 0.0) * jnp.where(col < close, 1.0, 0.0)

    def to_columns(k):
        return hot(iota((READS, 512), 1) == iota((READS, 512), 0) * 4 + k)

    first(0)
    second(0)
    first(1)
    third(0)
    for copy in win_copies:
        copy.wait()

    for k in range(4):
        f32 = nn(to_columns(k), fg[0].reshape(512, D))
        fp[k] = f32.astype(BF16)
        inverse = lax.rsqrt(jnp.mean(f32 * f32, -1, keepdims=True) + EPS)
        normed_b = (f32 * inverse).astype(BF16)
        nb[k] = normed_b
        keep = cover(k)
        for j in range(3):
            part = (nn(normed_b, ww[j]) * keep).astype(BF16)
            heads[j, 0, :, k * 128 : (k + 1) * 128] = part[:, :128]
            heads[j, 1, :, k * 128 : (k + 1) * 128] = part[:, 128:]
        if k == 2:
            second(1)

    low = jnp.where((iota((1, 512), 1) & 127) < 64, 1.0, 0.0)
    high = 1.0 - low
    par_f = par.astype(F32)
    own = low * (1.0 - par_f) + high * par_f
    plan = ((0, high), (1, low), (par, own))

    def scores(which, left, right):
        for h, (t, mask) in enumerate(plan):
            lbuf[which, h * 128 : (h + 1) * 128, :] = nt(heads[left, t] * mask.astype(BF16), heads[right, t])
        for d in range(1, 8):
            ee = ahead(e, d)
            copy = remote(
                lbuf.at[which, pl.ds(pl.multiple_of(48 * ee, 16), 48), :], rl.at[which, d],
                sl_s.at[which, d], sl_r.at[which, d], over_e(ee),
            )
            copy.start()
            sends.append(copy)

    scores(0, 0, 1)
    third(1)
    for k in range(4):
        col_grad = nn(to_columns(k), fg[1].reshape(512, D)).astype(BF16)
        gp[k] = col_grad
        part = nt(col_grad, w3[...]).astype(BF16)
        heads[3, 0, :, k * 128 : (k + 1) * 128] = part[:, :128]
        heads[3, 1, :, k * 128 : (k + 1) * 128] = part[:, 128:]
    scores(1, 3, 2)

    def turn(i, carry):
        w, col = iota((96, D), 0), iota((96, D), 1)
        yy, xx = lax.div(i, 2), lax.rem(i, 2)
        xi2 = (w >> 1) & 1
        row = (
            ((w >> 3) & 3) * 192 + (xi2 + xx * (3 - 2 * xi2)) * 48 + (w & 1) * 24
            + yy * 6 + ((w >> 2) & 1) * 3 + (w >> 5)
        )
        nbt[pl.ds(pl.multiple_of(i * 96, 16), 96), :] = nt(hot(col == row), nb[...].reshape(512, D)).astype(BF16)
        return carry

    lax.fori_loop(0, 8, turn, 0)

    for which in range(2):
        total = lbuf[which, pl.ds(pl.multiple_of(48 * e, 16), 48), :]
        for d in range(1, 8):
            remote(
                rl.at[which, d], rl.at[which, d], sl_s.at[which, d], sl_r.at[which, d], over_e(behind(e, d))
            ).wait_recv()
            total = total + rl[which, d]
        acc[:, which * 128 : (which + 1) * 128] = total

    late = []
    for o, place in enumerate(OWNERS):
        dev = over_z(place)
        copy = remote(acc.at[pl.ds(16 * o, 16), :], rz.at[ze], sz_s.at[o], sz_r.at[ze], dev)

        @pl.when(ze != place)
        def _():
            copy.start()

        late.append((place, copy))

    for o, place in enumerate(OWNERS):
        rows = pl.ds(pl.multiple_of(48 * e + 16 * o, 16), 16)

        @pl.when(ze == place)
        def _():
            total = acc[16 * o : 16 * o + 16, :]
            for s in range(8):
                if s != place:
                    remote(rz.at[s], rz.at[s], sz_s.at[o], sz_r.at[s], over_z(s)).wait_recv()
                    total = total + rz[s]
            expon = jnp.exp(total[:, :128] * SCALE)
            probs = expon / jnp.sum(expon, -1, keepdims=True)
            slopes = total[:, 128:]
            mixed = SCALE * probs * (slopes - jnp.sum(probs * slopes, -1, keepdims=True))
            pm[rows, 0:128] = probs.astype(BF16)
            pm[rows, 128:256] = mixed.astype(BF16)
            out = []
            for s in range(8):
                if s != place:
                    copy = remote(pm.at[rows, :], pm.at[rows, :], sq_s.at[s], sq_r.at[o], over_z(s))
                    copy.start()
                    out.append(copy)
            for copy in out:
                copy.wait_send()

    for o, place in enumerate(OWNERS):
        rows = pl.ds(pl.multiple_of(48 * e + 16 * o, 16), 16)

        @pl.when(ze != place)
        def _():
            remote(pm.at[rows, :], pm.at[rows, :], sq_s.at[0], sq_r.at[o], over_z(place)).wait_recv()

    def chunk(ee):
        return pm.at[pl.ds(pl.multiple_of(48 * ee, 16), 48), :]

    for d in range(1, 8):
        copy = remote(chunk(e), chunk(e), sp_s.at[d], sp_r.at[d], over_e(ahead(e, d)))
        copy.start()
        sends.append(copy)
    keeps = jnp.concatenate([jnp.broadcast_to(cover(k), (READS, 128)) for k in range(4)], axis=1)
    for d in range(1, 8):
        ee = behind(e, d)
        remote(chunk(ee), chunk(ee), sp_s.at[d], sp_r.at[d], over_e(ee)).wait_recv()

    eye = hot(ro == co)
    made = []
    for h, (t, _) in enumerate(plan):
        probs_b = pm[h * 128 : (h + 1) * 128, 0:128]
        mixed = pm[h * 128 : (h + 1) * 128, 128:256]
        made.append(
            (
                nn(mixed, heads[1, t]),
                nn(nt(eye, mixed).astype(BF16), heads[0, t]),
                nn(nt(eye, probs_b).astype(BF16), heads[3, t]),
                nn(probs_b, heads[2, t]),
            )
        )
    for j in range(4):
        tile0 = made[0][j] * high + made[2][j] * (low * (1.0 - par_f))
        tile1 = made[1][j] * low + made[2][j] * (high * par_f)
        for t, tile in ((0, tile0), (1, tile1)):
            if j < 3:
                tile = tile * keeps
            tile = tile.astype(BF16)
            for k in range(4):
                if j < 3:
                    gr[j, k, :, t * 128 : (t + 1) * 128] = tile[:, k * 128 : (k + 1) * 128]
                else:
                    ob[k, :, t * 128 : (t + 1) * 128] = tile[:, k * 128 : (k + 1) * 128]

    def rows_of(mm):
        return pl.ds(pl.multiple_of(32 * mm, 32), 32)

    for d, mm in ((1, side_m), (2, far_m), (3, core_m)):
        copy = remote(gr.at[:, :, rows_of(mm), :], rg.at[m], sg_s.at[d], sg_r.at[d], mate(mm))
        copy.start()
        sends.append(copy)
    rg[m] = gr[:, :, rows_of(m), :]

    ow, cw = iota((256, 256), 0), iota((256, 256), 1)
    u, yy, xx = ow & 31, ow >> 6, (ow >> 5) & 1
    xi2 = (u >> 1) & 1
    local = (
        64 * par + (xi2 + xx * (3 - 2 * xi2)) * 48 + (u & 1) * 24 + yy * 6 + ((u >> 2) & 1) * 3 + (u >> 3)
    )
    obt[...] = nt(hot(jnp.where(u < 24, local, -1) == cw), ob[...].reshape(512, WIN)).astype(BF16)

    def wgrad_copy(d):
        ee = ahead(e, d)
        return remote(wg.at[ee], rw.at[d], sd_s.at[d], sd_r.at[d], over_e(ee))

    def wgrad(d, carry):
        ee = ahead(e, d)
        left = nbt[pl.ds(pl.multiple_of(ee * 96, 16), 96), :]
        for j in range(3):
            wg[ee, 0:96, j * WIN : (j + 1) * WIN] = nn(left, gr[j].reshape(512, WIN)).astype(BF16)
        last = obt[pl.ds(pl.multiple_of(ee * 32, 32), 32), :]
        wg[ee, 96:128, :] = nn(last, gp[...].reshape(512, D)).astype(BF16)

        @pl.when(d < 8)
        def _():
            wgrad_copy(d).start()

        return carry

    lax.fori_loop(1, 9, wgrad, 0)

    for d, mm in ((1, side_m), (2, far_m), (3, core_m)):
        remote(gr.at[:, :, rows_of(mm), :], rg.at[mm], sg_s.at[d], sg_r.at[d], mate(mm)).wait_recv()
    for copy in full_copies:
        copy.wait()
    grad_norm = jnp.zeros((128, D), F32)
    for mm in range(4):
        lane = 128 * ((3 * mm) // 2)
        for j in range(3):
            grad_norm = grad_norm + nt(rg[mm, j].reshape(128, WIN), wv[j, :, lane : lane + WIN])
    mine = fp[:, rows_of(m), :].reshape(128, D).astype(F32)
    inverse = lax.rsqrt(jnp.mean(mine * mine, -1, keepdims=True) + EPS)
    normed = mine * inverse
    result = (inverse * (grad_norm - normed * jnp.mean(grad_norm * normed, -1, keepdims=True))).astype(BF16)
    to_sources = hot(co == (ro & 3) * 32 + (ro >> 2))
    gi[...] = nn(to_sources, result).astype(BF16).reshape(8, 16, D)
    for d in range(1, 8):
        gg = ahead(g, d)
        copy = remote(gi.at[gg], ogi.at[g], si_s.at[d], si_r.at[d], over_g(gg))
        copy.start()
        sends.append(copy)
    ogi[g] = gi[g]

    total = wg[e].astype(F32)
    for d in range(1, 8):
        remote(rw.at[d], rw.at[d], sd_s.at[d], sd_r.at[d], over_e(behind(e, d))).wait_recv()
        total = total + rw[d].astype(F32)
    v, zz = ro & 15, ro >> 4
    src = (v >> 2) * 32 + (zz & 3) * 8 + (zz >> 2) * 4 + (v & 3)
    src = jnp.where(v < 12, src, jnp.where(v < 15, 96 + (v - 12) * 8 + zz, -1))
    wz[...] = nn(hot(co == src), total.astype(BF16)).astype(BF16).reshape(8, 16, D)
    for d in range(1, 8):
        zz2 = ahead(ze, d)
        copy = remote(wz.at[zz2], rwz.at[d], se_s.at[d], se_r.at[d], over_z(zz2))
        copy.start()
        sends.append(copy)

    for d in range(1, 8):
        slot = ogi.at[behind(g, d)]
        remote(slot, slot, si_s.at[d], si_r.at[d], over_g(behind(g, d))).wait_recv()
    from_groups = hot(co == ((ro >> 2) & 7) * 16 + (ro >> 5) * 4 + (ro & 3))
    gin[...] = nn(from_groups, ogi[...].reshape(128, D)).astype(BF16).reshape(4, 32, D)
    gin_copy = pltpu.make_async_copy(gin, gin_out, s_in.at[0])
    gin_copy.start()

    total = wz[ze].astype(F32)
    for d in range(1, 8):
        remote(rwz.at[d], rwz.at[d], se_s.at[d], se_r.at[d], over_z(behind(ze, d))).wait_recv()
        total = total + rwz[d].astype(F32)
    for mm in range(4):
        for t in range(3):
            fd[mm, t : t + 1, :] = total[t * 4 + mm : t * 4 + mm + 1, :]
        fd[mm, 3:8, :] = jnp.zeros((5, D), F32)
    fd[4, 0:3, :] = total[12:15, :]
    fd[4, 3:8, :] = jnp.zeros((5, D), F32)
    for d, mm in ((1, side_m), (2, far_m), (3, core_m)):
        copy = remote(fd.at[mm], rj.at[m], sj_s.at[d], sj_r.at[d], mate(mm))
        copy.start()
        sends.append(copy)
    rj[m] = fd[m]
    last = remote(fd.at[4], r3, s3_s.at[0], s3_r.at[0], turned)

    @pl.when(zl != m)
    def _():
        last.start()
        last.wait()

    @pl.when(zl == m)
    def _():
        r3[...] = fd[4]

    for d, mm in ((1, side_m), (2, far_m), (3, core_m)):
        remote(fd.at[mm], rj.at[mm], sj_s.at[d], sj_r.at[d], mate(mm)).wait_recv()
    for j in range(3):
        for tile in range(6):
            value = jnp.zeros((3, 128), F32)
            for mm in range(4):
                at = tile - (3 * mm) // 2
                if at in (0, 1):
                    value = value + rj[mm, 0:3, j * WIN + at * 128 : j * WIN + (at + 1) * 128]
            wsum[:, j * D + tile * 128 : j * D + (tile + 1) * 128] = value
    wsum[:, 3 * D : 4 * D] = r3[0:3, :]
    wsum_copy = pltpu.make_async_copy(wsum, wgrad_out, s_in.at[1])
    wsum_copy.start()

    for copy in sends:
        copy.wait_send()
    gin_copy.wait()
    wsum_copy.wait()
    for d in range(1, 8):
        wgrad_copy(d).wait_send()
    for place, copy in late:

        @pl.when(ze != place)
        def _():
            copy.wait_send()


def shards(features, grad_out, weights, read_start, read_end):
    hbm = pl.BlockSpec(memory_space=pl.ANY)
    dma = pltpu.SemaphoreType.DMA
    return pl.pallas_call(
        kernel,
        name="tied_rows",
        out_shape=(
            jax.ShapeDtypeStruct((4, 32, D), BF16),
            jax.ShapeDtypeStruct((3, 4 * D), F32),
        ),
        in_specs=[hbm] * 5,
        out_specs=(hbm, hbm),
        scratch_shapes=[
            pltpu.VMEM((4, 32, D), BF16),
            pltpu.VMEM((4, 32, D), BF16),
            pltpu.VMEM((1, READS), I32),
            pltpu.VMEM((1, READS), I32),
            pltpu.VMEM((4, 32, D), BF16),
            pltpu.VMEM((3, 4 * D), F32),
            pltpu.VMEM((3, D, D), BF16),
            pltpu.VMEM((3, D, WIN), BF16),
            pltpu.VMEM((WIN, D), BF16),
            pltpu.VMEM((2, 8, 16, D), BF16),
            pltpu.VMEM((2, 4, 8, 16, D), BF16),
            pltpu.VMEM((4, READS, D), BF16),
            pltpu.VMEM((4, READS, D), BF16),
            pltpu.VMEM((4, READS, D), BF16),
            pltpu.VMEM((4, 2, READS, 512), BF16),
            pltpu.VMEM((2, 384, 128), F32),
            pltpu.VMEM((2, 8, 48, 128), F32),
            pltpu.VMEM((48, 256), F32),
            pltpu.VMEM((8, 16, 256), F32),
            pltpu.VMEM((384, 256), BF16),
            pltpu.VMEM((3, 4, READS, WIN), BF16),
            pltpu.VMEM((4, READS, WIN), BF16),
            pltpu.VMEM((4, 3, 4, 32, WIN), BF16),
            pltpu.VMEM((D, 512), BF16),
            pltpu.VMEM((WIN, 512), BF16),
            pltpu.VMEM((8, 128, D), BF16),
            pltpu.VMEM((8, 128, D), BF16),
            pltpu.VMEM((8, 16, D), BF16),
            pltpu.VMEM((8, 16, D), BF16),
            pltpu.VMEM((5, 8, D), F32),
            pltpu.VMEM((4, 8, D), F32),
            pltpu.VMEM((8, D), F32),
            pltpu.VMEM((8, 16, D), BF16),
            pltpu.VMEM((8, 16, D), BF16),
            dma((4,)), dma((7,)),
            dma((2, 8)), dma((2, 8)), dma((2,)), dma((2,)), dma((2,)), dma((2,)), dma((2,)), dma((2,)),
            dma((2, 8)), dma((2, 8)),
            dma((3,)), dma((8,)),
            dma((8,)), dma((3,)),
            dma((8,)), dma((8,)),
            dma((4,)), dma((4,)),
            dma((8,)), dma((8,)),
            dma((8,)), dma((8,)),
            dma((4,)), dma((4,)),
            dma((1,)), dma((1,)),
            dma((8,)), dma((8,)),
        ],
        compiler_params=pltpu.CompilerParams(
            collective_id=0, has_side_effects=True, vmem_limit_bytes=56 * 1024 * 1024
        ),
    )(features, grad_out, read_start.reshape(1, READS), read_end.reshape(1, READS), weights)


def solution(mesh):
    in_specs = (P("read", "pos", None), P("read", "pos", None), P(), P(), P())
    out_specs = (P("read", "pos", None), P(("read", "pos"), None))
    return jax.shard_map(shards, mesh=mesh, in_specs=in_specs, out_specs=out_specs, check_vma=False)
```

```python
import math

import jax
import jax.numpy as jnp
from jax import lax
from jax.experimental import pallas as pl
from jax.experimental.pallas import tpu as pltpu
from jax.sharding import PartitionSpec as P

F32, BF16, I32 = jnp.float32, jnp.bfloat16, jnp.int32
D = 768
WIN = 256
PACK = 640
READS = 128
SCALE = 1.0 / 128.0
EPS = 1e-05
OWNERS = (0, 3, 5)


def nt(a, b):
    return lax.dot_general(a, b, (((1,), (1,)), ((), ())), preferred_element_type=F32)


def nn(a, b):
    return jnp.dot(a, b, preferred_element_type=F32)


def iota(shape, dim):
    return lax.broadcasted_iota(I32, shape, dim)


def hot(cond):
    return jnp.where(cond, 1.0, 0.0).astype(BF16)


def read_of(g, m):
    zl, xp = lax.div(g, 2), lax.rem(g, 2)
    xi, c = lax.div(m, 2), lax.rem(m, 2)
    return zl * 8 + (xi + xp * (3 - 2 * xi)) * 2 + c


def kernel(
    feat_hbm, gout_hbm, starts_hbm, ends_hbm, w_hbm, gin_out, wgrad_out,
    feat, gout, starts, ends, gin, wsum, wv, ww, w3, a_buf, fg, fp, gp, nb, heads, lbuf, rl, acc, rz, pm,
    gr, gpk, ob, rg, nbt, obt, wa, ra, wb, rb, za, rza, yb, ryb, fd, rj, f3, r3, gi, ogi,
    s_in, s_w, sa_s, sa_r, sc_s, sc_r, sx_s, sx_r, sf_s, sf_r, sl_s, sl_r, sz_s, sz_r,
    sq_s, sq_r, sp_s, sp_r, sg_s, sg_r, sd_s, sd_r, se_s, se_r, sb_s, sb_r, sy_s, sy_r, sj_s, sj_r, s3_s, s3_r, si_s, si_r,
):
    ri, pi = lax.axis_index("read"), lax.axis_index("pos")
    zl, x, c = lax.div(ri, 8), lax.rem(lax.div(ri, 2), 4), lax.rem(ri, 2)
    xp = lax.div(x, 2)
    xi = x + xp * (3 - 2 * x)
    y, zh = lax.div(pi, 2), lax.rem(pi, 2)
    g, m = zl * 2 + xp, xi * 2 + c
    e, ze = y * 2 + xp, zh * 4 + zl
    par = lax.rem(m, 2)
    off = pl.multiple_of(128 * lax.div(3 * m, 2), 128)
    core_m = xi * 2 + (1 - c)
    side_m = (1 - xi) * 2 + c
    far_m = (1 - xi) * 2 + (1 - c)

    def remote(src, dst, ss, rs, dev):
        return pltpu.make_async_remote_copy(
            src_ref=src, dst_ref=dst, send_sem=ss, recv_sem=rs,
            device_id=dev, device_id_type=pl.DeviceIdType.MESH,
        )

    def mate(mm):
        return (read_of(g, mm), pi)

    def over_g(gg):
        return (read_of(gg, m), pi)

    def over_e(ee):
        return (read_of(zl * 2 + lax.rem(ee, 2), m), lax.div(ee, 2) * 2 + zh)

    def over_z(zz):
        return (read_of(lax.rem(zz, 4) * 2 + xp, m), y * 2 + lax.div(zz, 4))

    def ahead(v, d):
        return lax.rem(v + d, 8)

    def behind(v, d):
        return lax.rem(v + 8 - d, 8)

    turned = (read_of(m * 2 + xp, zl), pi)
    sends = []

    in_copies = [
        pltpu.make_async_copy(src, dst, s_in.at[i])
        for i, (src, dst) in enumerate(
            ((feat_hbm, feat), (gout_hbm, gout), (starts_hbm, starts), (ends_hbm, ends))
        )
    ]
    for copy in in_copies:
        copy.start()

    barrier = pltpu.get_barrier_semaphore()

    def greet(dev):
        pl.semaphore_signal(barrier, inc=1, device_id=dev, device_id_type=pl.DeviceIdType.MESH)

    for d in range(1, 8):
        greet(over_g(ahead(g, d)))
        greet(over_e(ahead(e, d)))
        greet(over_z(ahead(ze, d)))
    for mm in (core_m, side_m, far_m):
        greet(mate(mm))

    @pl.when(zl != m)
    def _():
        greet(turned)

    win_copies = [
        pltpu.make_async_copy(w_hbm.at[j, :, pl.ds(off, WIN)], ww.at[j], s_w.at[j]) for j in range(3)
    ]
    win_copies.append(pltpu.make_async_copy(w_hbm.at[3, pl.ds(off, WIN), :], w3, s_w.at[3]))
    full_copies = [pltpu.make_async_copy(w_hbm.at[j], wv.at[j], s_w.at[4 + j]) for j in range(3)]
    for copy in win_copies + full_copies:
        copy.start()

    for copy in in_copies:
        copy.wait()

    ro, co = iota((128, 128), 0), iota((128, 128), 1)
    to_groups = hot(co == ((ro >> 2) & 3) * 32 + (ro >> 4) * 4 + (ro & 3))
    for t, ref in ((0, feat), (1, gout)):
        a_buf[t] = nn(to_groups, ref[...].reshape(128, D)).astype(BF16).reshape(8, 16, D)

    @pl.when(zl == m)
    def _():
        pl.semaphore_wait(barrier, 24)

    @pl.when(zl != m)
    def _():
        pl.semaphore_wait(barrier, 25)

    for t in range(2):
        for d in range(1, 8):
            gg = ahead(g, d)
            copy = remote(a_buf.at[t, gg], fg.at[t, m, g], sa_s.at[t, d], sa_r.at[t, d], over_g(gg))
            copy.start()
            sends.append(copy)
        fg[t, m, g] = a_buf[t, g]

    def first(t):
        for d in range(1, 8):
            slot = fg.at[t, m, behind(g, d)]
            remote(slot, slot, sa_s.at[t, d], sa_r.at[t, d], over_g(behind(g, d))).wait_recv()
        for ss, rs, mm in ((sx_s, sx_r, side_m), (sc_s, sc_r, core_m)):
            copy = remote(fg.at[t, m], fg.at[t, m], ss.at[t], rs.at[t], mate(mm))
            copy.start()
            sends.append(copy)

    def second(t):
        slot = fg.at[t, side_m]
        remote(slot, slot, sx_s.at[t], sx_r.at[t], mate(side_m)).wait_recv()
        copy = remote(slot, slot, sf_s.at[t], sf_r.at[t], mate(core_m))
        copy.start()
        sends.append(copy)

    def third(t):
        slot = fg.at[t, core_m]
        remote(slot, slot, sc_s.at[t], sc_r.at[t], mate(core_m)).wait_recv()
        slot = fg.at[t, far_m]
        remote(slot, slot, sf_s.at[t], sf_r.at[t], mate(core_m)).wait_recv()

    nat = iota((READS, READS), 0)
    gs_v, ms_v, r_v = (nat >> 2) & 7, nat >> 5, nat & 3
    xi_v, xp_v = ms_v >> 1, gs_v & 1
    nat = 4 * ((gs_v >> 1) * 8 + (xi_v + xp_v * (3 - 2 * xi_v)) * 2 + (ms_v & 1)) + r_v
    pick = iota((READS, READS), 1) == nat
    begin = jnp.sum(jnp.where(pick, starts[...].astype(F32), 0.0), axis=1, keepdims=True)
    close = jnp.sum(jnp.where(pick, ends[...].astype(F32), 0.0), axis=1, keepdims=True)

    def cover(k):
        col = (32 * pi + 4 * g + k).astype(F32)
        return jnp.where(col >= begin, 1.0, 0.0) * jnp.where(col < close, 1.0, 0.0)

    def to_columns(k):
        return hot(iota((READS, 512), 1) == iota((READS, 512), 0) * 4 + k)

    first(0)
    second(0)
    first(1)
    third(0)
    for copy in win_copies:
        copy.wait()

    for k in range(4):
        f32 = nn(to_columns(k), fg[0].reshape(512, D))
        fp[k] = f32.astype(BF16)
        inverse = lax.rsqrt(jnp.mean(f32 * f32, -1, keepdims=True) + EPS)
        normed_b = (f32 * inverse).astype(BF16)
        nb[k] = normed_b
        keep = cover(k)
        for j in range(3):
            part = (nn(normed_b, ww[j]) * keep).astype(BF16)
            heads[j, 0, :, k * 128 : (k + 1) * 128] = part[:, :128]
            heads[j, 1, :, k * 128 : (k + 1) * 128] = part[:, 128:]
        if k == 2:
            second(1)

    low = jnp.where((iota((1, 512), 1) & 127) < 64, 1.0, 0.0)
    high = 1.0 - low
    par_f = par.astype(F32)
    own = low * (1.0 - par_f) + high * par_f
    plan = ((0, high), (1, low), (par, own))

    def scores(which, left, right):
        for h, (t, mask) in enumerate(plan):
            lbuf[which, h * 128 : (h + 1) * 128, :] = nt(heads[left, t] * mask.astype(BF16), heads[right, t])
        for d in range(1, 8):
            ee = ahead(e, d)
            copy = remote(
                lbuf.at[which, pl.ds(pl.multiple_of(48 * ee, 16), 48), :], rl.at[which, d],
                sl_s.at[which, d], sl_r.at[which, d], over_e(ee),
            )
            copy.start()
            sends.append(copy)

    scores(0, 0, 1)
    third(1)
    back = nt(fg[1].reshape(512, D), w3[...]).astype(BF16)
    for k in range(4):
        part = nn(to_columns(k), back).astype(BF16)
        heads[3, 0, :, k * 128 : (k + 1) * 128] = part[:, :128]
        heads[3, 1, :, k * 128 : (k + 1) * 128] = part[:, 128:]
    scores(1, 3, 2)

    def turn(i, carry):
        w, col = iota((96, D), 0), iota((96, D), 1)
        yy, xx = lax.div(ahead(e, i + 1), 2), lax.rem(ahead(e, i + 1), 2)
        xi2 = (w >> 1) & 1
        row = (
            ((w >> 3) & 3) * 192 + (xi2 + xx * (3 - 2 * xi2)) * 48 + (w & 1) * 24
            + yy * 6 + ((w >> 2) & 1) * 3 + (w >> 5)
        )
        nbt[pl.ds(pl.multiple_of(i * 96, 16), 96), :] = nt(hot(col == row), nb[...].reshape(512, D)).astype(BF16)
        return carry

    lax.fori_loop(0, 8, turn, 0)
    for k in range(4):
        gp[k] = nn(to_columns(k), fg[1].reshape(512, D)).astype(BF16)

    for which in range(2):
        total = lbuf[which, pl.ds(pl.multiple_of(48 * e, 16), 48), :]
        for d in range(1, 8):
            remote(
                rl.at[which, d], rl.at[which, d], sl_s.at[which, d], sl_r.at[which, d], over_e(behind(e, d))
            ).wait_recv()
            total = total + rl[which, d]
        acc[:, which * 128 : (which + 1) * 128] = total

    late = []
    for o, place in enumerate(OWNERS):
        dev = over_z(place)
        copy = remote(acc.at[pl.ds(16 * o, 16), :], rz.at[ze], sz_s.at[o], sz_r.at[ze], dev)

        @pl.when(ze != place)
        def _():
            copy.start()

        late.append((place, copy))

    for o, place in enumerate(OWNERS):
        rows = pl.ds(pl.multiple_of(48 * e + 16 * o, 16), 16)

        @pl.when(ze == place)
        def _():
            total = acc[16 * o : 16 * o + 16, :]
            for s in range(8):
                if s != place:
                    remote(rz.at[s], rz.at[s], sz_s.at[o], sz_r.at[s], over_z(s)).wait_recv()
                    total = total + rz[s]
            expon = jnp.exp(total[:, :128] * SCALE)
            probs = expon / jnp.sum(expon, -1, keepdims=True)
            slopes = total[:, 128:]
            mixed = SCALE * probs * (slopes - jnp.sum(probs * slopes, -1, keepdims=True))
            pm[rows, 0:128] = probs.astype(BF16)
            pm[rows, 128:256] = mixed.astype(BF16)
            out = []
            for s in range(8):
                if s != place:
                    copy = remote(pm.at[rows, :], pm.at[rows, :], sq_s.at[s], sq_r.at[o], over_z(s))
                    copy.start()
                    out.append(copy)
            for copy in out:
                copy.wait_send()

    for o, place in enumerate(OWNERS):
        rows = pl.ds(pl.multiple_of(48 * e + 16 * o, 16), 16)

        @pl.when(ze != place)
        def _():
            remote(pm.at[rows, :], pm.at[rows, :], sq_s.at[0], sq_r.at[o], over_z(place)).wait_recv()

    def chunk(ee):
        return pm.at[pl.ds(pl.multiple_of(48 * ee, 16), 48), :]

    for d in range(1, 8):
        copy = remote(chunk(e), chunk(e), sp_s.at[d], sp_r.at[d], over_e(ahead(e, d)))
        copy.start()
        sends.append(copy)
    keeps = jnp.concatenate([jnp.broadcast_to(cover(k), (READS, 128)) for k in range(4)], axis=1)
    for d in range(1, 8):
        ee = behind(e, d)
        remote(chunk(ee), chunk(ee), sp_s.at[d], sp_r.at[d], over_e(ee)).wait_recv()

    eye = hot(ro == co)
    made = []
    for h, (t, _) in enumerate(plan):
        probs_b = pm[h * 128 : (h + 1) * 128, 0:128]
        mixed = pm[h * 128 : (h + 1) * 128, 128:256]
        made.append(
            (
                nn(mixed, heads[1, t]),
                nn(nt(eye, mixed).astype(BF16), heads[0, t]),
                nn(nt(eye, probs_b).astype(BF16), heads[3, t]),
                nn(probs_b, heads[2, t]),
            )
        )
    def lanes(v, k):
        return v[:, k * 128 : (k + 1) * 128]

    spare = []
    for j in range(4):
        tile0 = made[0][j] * high + made[2][j] * (low * (1.0 - par_f))
        tile1 = made[1][j] * low + made[2][j] * (high * par_f)
        if j < 3:
            tile0, tile1 = tile0 * keeps, tile1 * keeps
            full = (tile0 * (1.0 - par_f) + tile1 * par_f).astype(BF16)
            spare.append(tile1 * (1.0 - par_f) + tile0 * par_f)
        for k in range(4):
            for t, tile in ((0, tile0), (1, tile1)):
                if j < 3:
                    gr[j, k, :, t * 128 : (t + 1) * 128] = lanes(tile, k).astype(BF16)
                else:
                    ob[k, :, t * 128 : (t + 1) * 128] = lanes(tile, k).astype(BF16)
            if j < 3:
                gpk[k, :, j * 128 : (j + 1) * 128] = lanes(full, k)
    for k in range(4):
        gpk[k, :, 384:512] = (lanes(spare[0], k) + pltpu.roll(lanes(spare[1], k), 64, axis=1)).astype(BF16)
        gpk[k, :, 512:640] = lanes(spare[2], k).astype(BF16)

    def rows_of(mm):
        return pl.ds(pl.multiple_of(32 * mm, 32), 32)

    for d, mm in ((1, side_m), (2, far_m), (3, core_m)):
        copy = remote(gr.at[:, :, rows_of(mm), :], rg.at[m], sg_s.at[d], sg_r.at[d], mate(mm))
        copy.start()
        sends.append(copy)
    rg[m] = gr[:, :, rows_of(m), :]

    right = gpk[...].reshape(512, PACK)
    for half in range(2):
        part = nn(nbt[half * 384 : (half + 1) * 384, :], right).astype(BF16)
        for q in range(4):
            d = (half * 4 + q + 1) % 8
            wa[d] = part[q * 96 : (q + 1) * 96, :]
        for q in range(4):
            d = (half * 4 + q + 1) % 8
            if d > 0:
                copy = remote(wa.at[d], ra.at[d], sd_s.at[d], sd_r.at[d], over_e(ahead(e, d)))
                copy.start()
                sends.append(copy)

    ow, cw = iota((256, 256), 0), iota((256, 256), 1)
    u, zz = ow & 31, ((ow >> 5) + ze) & 7
    xi2, xx, yy = (zz >> 1) & 1, u & 1, (u >> 1) & 3
    local = 64 * par + (xi2 + xx * (3 - 2 * xi2)) * 48 + (zz & 1) * 24 + yy * 6 + (zz >> 2) * 3 + (u >> 3)
    obt[...] = nt(hot(jnp.where(u < 24, local, -1) == cw), ob[...].reshape(512, WIN)).astype(BF16)
    wb[...] = nn(obt[...], gp[...].reshape(512, D)).astype(BF16).reshape(8, 32, D)
    for d in range(1, 8):
        copy = remote(wb.at[d], rb.at[d], sb_s.at[d], sb_r.at[d], over_z(ahead(ze, d)))
        copy.start()
        sends.append(copy)

    for d, mm in ((1, side_m), (2, far_m), (3, core_m)):
        remote(gr.at[:, :, rows_of(mm), :], rg.at[mm], sg_s.at[d], sg_r.at[d], mate(mm)).wait_recv()
    for copy in full_copies:
        copy.wait()
    grad_norm = jnp.zeros((128, D), F32)
    for mm in range(4):
        lane = 128 * ((3 * mm) // 2)
        for j in range(3):
            grad_norm = grad_norm + nt(rg[mm, j].reshape(128, WIN), wv[j, :, lane : lane + WIN])
    mine = fp[:, rows_of(m), :].reshape(128, D).astype(F32)
    inverse = lax.rsqrt(jnp.mean(mine * mine, -1, keepdims=True) + EPS)
    normed = mine * inverse
    result = (inverse * (grad_norm - normed * jnp.mean(grad_norm * normed, -1, keepdims=True))).astype(BF16)
    to_sources = hot(co == (ro & 3) * 32 + (ro >> 2))
    gi[...] = nn(to_sources, result).astype(BF16).reshape(8, 16, D)
    for d in range(1, 8):
        gg = ahead(g, d)
        copy = remote(gi.at[gg], ogi.at[g], si_s.at[d], si_r.at[d], over_g(gg))
        copy.start()
        sends.append(copy)
    ogi[g] = gi[g]

    total = wb[0].astype(F32)
    for d in range(1, 8):
        remote(rb.at[d], rb.at[d], sb_s.at[d], sb_r.at[d], over_z(behind(ze, d))).wait_recv()
        total = total + rb[d].astype(F32)
    rb_row, rb_col = iota((128, 32), 0), iota((128, 32), 1)
    v = rb_row & 15
    src = jnp.where(v < 3, v * 8 + (((rb_row >> 4) + e) & 7), -1)
    yb[...] = nn(hot(rb_col == src), total.astype(BF16)).astype(BF16).reshape(8, 16, D)
    for d in range(1, 8):
        copy = remote(yb.at[d], ryb.at[d], sy_s.at[d], sy_r.at[d], over_e(ahead(e, d)))
        copy.start()
        sends.append(copy)

    total = wa[0].astype(F32)
    for d in range(1, 8):
        remote(ra.at[d], ra.at[d], sd_s.at[d], sd_r.at[d], over_e(behind(e, d))).wait_recv()
        total = total + ra[d].astype(F32)
    ra_row, ra_col = iota((128, 96), 0), iota((128, 96), 1)
    v, zz = ra_row & 15, ((ra_row >> 4) + ze) & 7
    src = jnp.where(v < 12, (v >> 2) * 32 + (zz & 3) * 8 + (zz >> 2) * 4 + (v & 3), -1)
    za[...] = nn(hot(ra_col == src), total.astype(BF16)).astype(BF16).reshape(8, 16, PACK)
    for d in range(1, 8):
        copy = remote(za.at[d], rza.at[d], se_s.at[d], se_r.at[d], over_z(ahead(ze, d)))
        copy.start()
        sends.append(copy)

    for d in range(1, 8):
        slot = ogi.at[behind(g, d)]
        remote(slot, slot, si_s.at[d], si_r.at[d], over_g(behind(g, d))).wait_recv()
    from_groups = hot(co == ((ro >> 2) & 7) * 16 + (ro >> 5) * 4 + (ro & 3))
    gin[...] = nn(from_groups, ogi[...].reshape(128, D)).astype(BF16).reshape(4, 32, D)
    gin_copy = pltpu.make_async_copy(gin, gin_out, s_in.at[0])
    gin_copy.start()

    total = yb[0].astype(F32)
    for d in range(1, 8):
        remote(ryb.at[d], ryb.at[d], sy_s.at[d], sy_r.at[d], over_e(behind(e, d))).wait_recv()
        total = total + ryb[d].astype(F32)
    f3[...] = total[0:8, :]
    last = remote(f3, r3, s3_s.at[0], s3_r.at[0], turned)

    @pl.when(zl != m)
    def _():
        last.start()

    @pl.when(zl == m)
    def _():
        r3[...] = f3[...]

    total = za[0].astype(F32)
    for d in range(1, 8):
        remote(rza.at[d], rza.at[d], se_s.at[d], se_r.at[d], over_z(behind(ze, d))).wait_recv()
        total = total + rza[d].astype(F32)
    for mm in range(4):
        for t in range(3):
            fd[mm, t : t + 1, :] = total[t * 4 + mm : t * 4 + mm + 1, :]
        fd[mm, 3:8, :] = jnp.zeros((5, PACK), F32)
    for d, mm in ((1, side_m), (2, far_m), (3, core_m)):
        copy = remote(fd.at[mm], rj.at[m], sj_s.at[d], sj_r.at[d], mate(mm))
        copy.start()
        sends.append(copy)
    rj[m] = fd[m]

    @pl.when(zl != m)
    def _():
        last.wait()

    for d, mm in ((1, side_m), (2, far_m), (3, core_m)):
        remote(fd.at[mm], rj.at[mm], sj_s.at[d], sj_r.at[d], mate(mm)).wait_recv()
    for j in range(3):
        tiles = [jnp.zeros((3, 128), F32)] * 6
        for mm in range(4):
            side = (low, high)[mm % 2][:, :128]
            full = rj[mm, :, j * 128 : (j + 1) * 128]
            rest = rj[mm, :, (512 if j == 2 else 384) : (640 if j == 2 else 512)]
            if j == 1:
                rest = pltpu.roll(rest, 64, axis=1)
            pair = (full, rest * side) if mm % 2 == 0 else (rest * side, full)
            for at in range(2):
                tiles[(3 * mm) // 2 + at] = tiles[(3 * mm) // 2 + at] + pair[at][0:3]
        for tile in range(6):
            wsum[:, j * D + tile * 128 : j * D + (tile + 1) * 128] = tiles[tile]
    wsum[:, 3 * D : 4 * D] = r3[0:3, :]
    wsum_copy = pltpu.make_async_copy(wsum, wgrad_out, s_in.at[1])
    wsum_copy.start()

    for copy in sends:
        copy.wait_send()
    gin_copy.wait()
    wsum_copy.wait()
    for place, copy in late:

        @pl.when(ze != place)
        def _():
            copy.wait_send()


def shards(features, grad_out, weights, read_start, read_end):
    hbm = pl.BlockSpec(memory_space=pl.ANY)
    dma = pltpu.SemaphoreType.DMA
    return pl.pallas_call(
        kernel,
        name="tied_rows",
        out_shape=(
            jax.ShapeDtypeStruct((4, 32, D), BF16),
            jax.ShapeDtypeStruct((3, 4 * D), F32),
        ),
        in_specs=[hbm] * 5,
        out_specs=(hbm, hbm),
        scratch_shapes=[
            pltpu.VMEM((4, 32, D), BF16),
            pltpu.VMEM((4, 32, D), BF16),
            pltpu.VMEM((1, READS), I32),
            pltpu.VMEM((1, READS), I32),
            pltpu.VMEM((4, 32, D), BF16),
            pltpu.VMEM((3, 4 * D), F32),
            pltpu.VMEM((3, D, D), BF16),
            pltpu.VMEM((3, D, WIN), BF16),
            pltpu.VMEM((WIN, D), BF16),
            pltpu.VMEM((2, 8, 16, D), BF16),
            pltpu.VMEM((2, 4, 8, 16, D), BF16),
            pltpu.VMEM((4, READS, D), BF16),
            pltpu.VMEM((4, READS, D), BF16),
            pltpu.VMEM((4, READS, D), BF16),
            pltpu.VMEM((4, 2, READS, 512), BF16),
            pltpu.VMEM((2, 384, 128), F32),
            pltpu.VMEM((2, 8, 48, 128), F32),
            pltpu.VMEM((48, 256), F32),
            pltpu.VMEM((8, 16, 256), F32),
            pltpu.VMEM((384, 256), BF16),
            pltpu.VMEM((3, 4, READS, WIN), BF16),
            pltpu.VMEM((4, READS, PACK), BF16),
            pltpu.VMEM((4, READS, WIN), BF16),
            pltpu.VMEM((4, 3, 4, 32, WIN), BF16),
            pltpu.VMEM((D, 512), BF16),
            pltpu.VMEM((WIN, 512), BF16),
            pltpu.VMEM((8, 96, PACK), BF16),
            pltpu.VMEM((8, 96, PACK), BF16),
            pltpu.VMEM((8, 32, D), BF16),
            pltpu.VMEM((8, 32, D), BF16),
            pltpu.VMEM((8, 16, PACK), BF16),
            pltpu.VMEM((8, 16, PACK), BF16),
            pltpu.VMEM((8, 16, D), BF16),
            pltpu.VMEM((8, 16, D), BF16),
            pltpu.VMEM((4, 8, PACK), F32),
            pltpu.VMEM((4, 8, PACK), F32),
            pltpu.VMEM((8, D), F32),
            pltpu.VMEM((8, D), F32),
            pltpu.VMEM((8, 16, D), BF16),
            pltpu.VMEM((8, 16, D), BF16),
            dma((4,)), dma((7,)),
            dma((2, 8)), dma((2, 8)), dma((2,)), dma((2,)), dma((2,)), dma((2,)), dma((2,)), dma((2,)),
            dma((2, 8)), dma((2, 8)),
            dma((3,)), dma((8,)),
            dma((8,)), dma((3,)),
            dma((8,)), dma((8,)),
            dma((4,)), dma((4,)),
            dma((8,)), dma((8,)),
            dma((8,)), dma((8,)),
            dma((8,)), dma((8,)),
            dma((8,)), dma((8,)),
            dma((4,)), dma((4,)),
            dma((1,)), dma((1,)),
            dma((8,)), dma((8,)),
        ],
        compiler_params=pltpu.CompilerParams(
            collective_id=0, has_side_effects=True, vmem_limit_bytes=56 * 1024 * 1024
        ),
    )(features, grad_out, read_start.reshape(1, READS), read_end.reshape(1, READS), weights)


def solution(mesh):
    in_specs = (P("read", "pos", None), P("read", "pos", None), P(), P(), P())
    out_specs = (P("read", "pos", None), P(("read", "pos"), None))
    return jax.shard_map(shards, mesh=mesh, in_specs=in_specs, out_specs=out_specs, check_vma=False)
```

```python
import math

import jax
import jax.numpy as jnp
from jax import lax
from jax.experimental import pallas as pl
from jax.experimental.pallas import tpu as pltpu
from jax.sharding import PartitionSpec as P

F32, BF16, I32 = jnp.float32, jnp.bfloat16, jnp.int32
D = 768
WIN = 256
PACK = 640
READS = 128
SCALE = 1.0 / 128.0
EPS = 1e-05
OWNERS = (0, 3, 5)


def nt(a, b):
    return lax.dot_general(a, b, (((1,), (1,)), ((), ())), preferred_element_type=F32)


def nn(a, b):
    return jnp.dot(a, b, preferred_element_type=F32)


def iota(shape, dim):
    return lax.broadcasted_iota(I32, shape, dim)


def hot(cond):
    return jnp.where(cond, 1.0, 0.0).astype(BF16)


def read_of(g, m):
    zl, xp = lax.div(g, 2), lax.rem(g, 2)
    xi, c = lax.div(m, 2), lax.rem(m, 2)
    return zl * 8 + (xi + xp * (3 - 2 * xi)) * 2 + c


def kernel(
    feat_hbm, gout_hbm, starts_hbm, ends_hbm, w_hbm, gin, wsum,
    feat, gout, starts, ends, wv, ww, w3, a_buf, fg, bg, bx, qa, na, mine, gp, nb, heads, lbuf, rl, acc, rz, pm,
    gr, gpk, ob, rg, nbt, obt, wa, ra, wb, rb, za, rza, yb, ryb, fd, rj, f3, r3, gi, ogi,
    s_in, s_w, sa_s, sa_r, sh_s, sh_r, sc_s, sc_r, sx_s, sx_r, sf_s, sf_r, sl_s, sl_r, sz_s, sz_r,
    sq_s, sq_r, sp_s, sp_r, sg_s, sg_r, sd_s, sd_r, se_s, se_r, sb_s, sb_r, sy_s, sy_r, sj_s, sj_r, s3_s, s3_r, si_s, si_r,
):
    ri, pi = lax.axis_index("read"), lax.axis_index("pos")
    zl, x, c = lax.div(ri, 8), lax.rem(lax.div(ri, 2), 4), lax.rem(ri, 2)
    xp = lax.div(x, 2)
    xi = x + xp * (3 - 2 * x)
    y, zh = lax.div(pi, 2), lax.rem(pi, 2)
    g, m = zl * 2 + xp, xi * 2 + c
    e, ze = y * 2 + xp, zh * 4 + zl
    par = lax.rem(m, 2)
    off = pl.multiple_of(128 * lax.div(3 * m, 2), 128)
    core_m = xi * 2 + (1 - c)
    side_m = (1 - xi) * 2 + c
    far_m = (1 - xi) * 2 + (1 - c)

    def remote(src, dst, ss, rs, dev):
        return pltpu.make_async_remote_copy(
            src_ref=src, dst_ref=dst, send_sem=ss, recv_sem=rs,
            device_id=dev, device_id_type=pl.DeviceIdType.MESH,
        )

    def mate(mm):
        return (read_of(g, mm), pi)

    def over_g(gg):
        return (read_of(gg, m), pi)

    def over_e(ee):
        return (read_of(zl * 2 + lax.rem(ee, 2), m), lax.div(ee, 2) * 2 + zh)

    def over_z(zz):
        return (read_of(lax.rem(zz, 4) * 2 + xp, m), y * 2 + lax.div(zz, 4))

    def ahead(v, d):
        return lax.rem(v + d, 8)

    def behind(v, d):
        return lax.rem(v + 8 - d, 8)

    turned = (read_of(m * 2 + xp, zl), pi)
    sends = []

    in_copies = [
        pltpu.make_async_copy(src, dst, s_in.at[i])
        for i, (src, dst) in enumerate(
            ((feat_hbm, feat), (gout_hbm, gout), (starts_hbm, starts), (ends_hbm, ends))
        )
    ]
    for copy in in_copies:
        copy.start()

    barrier = pltpu.get_barrier_semaphore()

    def greet(dev):
        pl.semaphore_signal(barrier, inc=1, device_id=dev, device_id_type=pl.DeviceIdType.MESH)

    for d in range(1, 8):
        greet(over_g(ahead(g, d)))
        greet(over_e(ahead(e, d)))
        greet(over_z(ahead(ze, d)))
    for mm in (core_m, side_m, far_m):
        greet(mate(mm))

    @pl.when(zl != m)
    def _():
        greet(turned)

    win_copies = [
        pltpu.make_async_copy(w_hbm.at[j, :, pl.ds(off, WIN)], ww.at[j], s_w.at[j]) for j in range(3)
    ]
    w3_copy = pltpu.make_async_copy(w_hbm.at[3], w3, s_w.at[3])
    full_copies = [pltpu.make_async_copy(w_hbm.at[j], wv.at[j], s_w.at[4 + j]) for j in range(3)]
    for copy in [w3_copy] + win_copies + full_copies:
        copy.start()

    ro, co = iota((128, 128), 0), iota((128, 128), 1)
    to_groups = hot(co == ((ro >> 2) & 3) * 32 + (ro >> 4) * 4 + (ro & 3))
    def by_group(ref):
        return nn(to_groups, ref[...].reshape(128, D)).astype(BF16)

    def spread(i, dst):
        for d in range(1, 8):
            gg = ahead(g, d)
            copy = remote(a_buf.at[i, gg], dst.at[g], sa_s.at[i, d], sa_r.at[i, d], over_g(gg))
            copy.start()
            sends.append(copy)
        dst[g] = a_buf[i, g]

    def gathered(i, dst):
        for d in range(1, 8):
            slot = dst.at[behind(g, d)]
            remote(slot, slot, sa_s.at[i, d], sa_r.at[i, d], over_g(behind(g, d))).wait_recv()

    in_copies[0].wait()
    a_buf[0] = by_group(feat).reshape(8, 16, D)

    @pl.when(zl == m)
    def _():
        pl.semaphore_wait(barrier, 24)

    @pl.when(zl != m)
    def _():
        pl.semaphore_wait(barrier, 25)

    spread(0, fg.at[0, m])
    in_copies[1].wait()
    local_grad = by_group(gout)
    a_buf[1] = local_grad.reshape(8, 16, D)
    w3_copy.wait()
    a_buf[2] = nt(local_grad, w3[...]).astype(BF16).reshape(8, 16, D)
    spread(2, bg)
    spread(1, fg.at[1, m])

    def first(t):
        gathered(t, fg.at[t, m])
        for ss, rs, mm in ((sx_s, sx_r, side_m), (sc_s, sc_r, core_m)):
            copy = remote(fg.at[t, m], fg.at[t, m], ss.at[t], rs.at[t], mate(mm))
            copy.start()
            sends.append(copy)

    def second(t):
        slot = fg.at[t, side_m]
        remote(slot, slot, sx_s.at[t], sx_r.at[t], mate(side_m)).wait_recv()
        copy = remote(slot, slot, sf_s.at[t], sf_r.at[t], mate(core_m))
        copy.start()
        sends.append(copy)

    def from_core(t):
        slot = fg.at[t, core_m]
        remote(slot, slot, sc_s.at[t], sc_r.at[t], mate(core_m)).wait_recv()

    def from_far(t):
        slot = fg.at[t, far_m]
        remote(slot, slot, sf_s.at[t], sf_r.at[t], mate(core_m)).wait_recv()

    def project(mm):
        f32 = fg[0, mm].reshape(128, D).astype(F32)
        inverse = lax.rsqrt(jnp.mean(f32 * f32, -1, keepdims=True) + EPS)
        normed_b = (f32 * inverse).astype(BF16)
        na[mm] = normed_b
        for j in range(3):
            qa[j, mm] = nn(normed_b, ww[j]).astype(BF16)

    first(0)
    for copy in in_copies[2:] + win_copies:
        copy.wait()
    project(m)
    from_core(0)
    project(core_m)

    def window(mm):
        return bg.at[:, :, pl.ds(pl.multiple_of(128 * lax.div(3 * mm, 2), 128), WIN)]

    gathered(2, bg)
    for d, mm in ((1, side_m), (2, far_m), (3, core_m)):
        copy = remote(window(mm), bx.at[m], sh_s.at[d], sh_r.at[d], mate(mm))
        copy.start()
        sends.append(copy)
    second(0)

    nat = iota((READS, READS), 0)
    gs_v, ms_v, r_v = (nat >> 2) & 7, nat >> 5, nat & 3
    xi_v, xp_v = ms_v >> 1, gs_v & 1
    nat = 4 * ((gs_v >> 1) * 8 + (xi_v + xp_v * (3 - 2 * xi_v)) * 2 + (ms_v & 1)) + r_v
    pick = iota((READS, READS), 1) == nat
    begin = jnp.sum(jnp.where(pick, starts[...].astype(F32), 0.0), axis=1, keepdims=True)
    close = jnp.sum(jnp.where(pick, ends[...].astype(F32), 0.0), axis=1, keepdims=True)

    def cover(k):
        col = (32 * pi + 4 * g + k).astype(F32)
        return jnp.where(col >= begin, 1.0, 0.0) * jnp.where(col < close, 1.0, 0.0)

    project(side_m)
    bx[m] = bg[:, :, pl.ds(off, WIN)]
    pr, pc = iota((256, 512), 0), iota((256, 512), 1)

    def to_columns(half):
        return hot(pc == (pr & 127) * 4 + (pr >> 7) + 2 * half)

    def set_heads(j, half, part):
        for k in range(2):
            for t in range(2):
                at = (2 * half + k) * 128
                heads[j, t, :, at : at + 128] = part[k * 128 : (k + 1) * 128, t * 128 : (t + 1) * 128]

    from_far(0)
    project(far_m)
    for half in range(2):
        keep = jnp.concatenate([cover(2 * half), cover(2 * half + 1)], axis=0)
        for j in range(3):
            set_heads(j, half, (nn(to_columns(half), qa[j].reshape(512, WIN)) * keep).astype(BF16))

    low = jnp.where((iota((1, 512), 1) & 127) < 64, 1.0, 0.0)
    high = 1.0 - low
    par_f = par.astype(F32)
    own = low * (1.0 - par_f) + high * par_f
    plan = ((0, high), (1, low), (par, own))

    def scores(which, left, right):
        for h, (t, mask) in enumerate(plan):
            lbuf[which, h * 128 : (h + 1) * 128, :] = nt(heads[left, t] * mask.astype(BF16), heads[right, t])
        for d in range(1, 8):
            ee = ahead(e, d)
            copy = remote(
                lbuf.at[which, pl.ds(pl.multiple_of(48 * ee, 16), 48), :], rl.at[which, d],
                sl_s.at[which, d], sl_r.at[which, d], over_e(ee),
            )
            copy.start()
            sends.append(copy)

    scores(0, 0, 1)
    for d, mm in ((1, side_m), (2, far_m), (3, core_m)):
        remote(window(mm), bx.at[mm], sh_s.at[d], sh_r.at[d], mate(mm)).wait_recv()
    for half in range(2):
        set_heads(3, half, nn(to_columns(half), bx[...].reshape(512, WIN)).astype(BF16))
    scores(1, 3, 2)

    first(1)
    for half in range(2):
        nb[2 * half : 2 * half + 2] = nn(to_columns(half), na[...].reshape(512, D)).astype(BF16).reshape(2, READS, D)
    mine[...] = nn(hot(co == (ro & 31) * 4 + (ro >> 5)), fg[0, m].reshape(128, D)).astype(BF16)

    def turn(i, carry):
        w, col = iota((96, D), 0), iota((96, D), 1)
        yy, xx = lax.div(ahead(e, i + 1), 2), lax.rem(ahead(e, i + 1), 2)
        xi2 = (w >> 1) & 1
        row = (
            ((w >> 3) & 3) * 192 + (xi2 + xx * (3 - 2 * xi2)) * 48 + (w & 1) * 24
            + yy * 6 + ((w >> 2) & 1) * 3 + (w >> 5)
        )
        nbt[pl.ds(pl.multiple_of(i * 96, 16), 96), :] = nt(hot(col == row), nb[...].reshape(512, D)).astype(BF16)
        return carry

    lax.fori_loop(0, 8, turn, 0)

    for which in range(2):
        total = lbuf[which, pl.ds(pl.multiple_of(48 * e, 16), 48), :]
        for d in range(1, 8):
            remote(
                rl.at[which, d], rl.at[which, d], sl_s.at[which, d], sl_r.at[which, d], over_e(behind(e, d))
            ).wait_recv()
            total = total + rl[which, d]
        acc[:, which * 128 : (which + 1) * 128] = total

    late = []
    for o, place in enumerate(OWNERS):
        dev = over_z(place)
        copy = remote(acc.at[pl.ds(16 * o, 16), :], rz.at[ze], sz_s.at[o], sz_r.at[ze], dev)

        @pl.when(ze != place)
        def _():
            copy.start()

        late.append((place, copy))

    second(1)
    for o, place in enumerate(OWNERS):
        rows = pl.ds(pl.multiple_of(48 * e + 16 * o, 16), 16)

        @pl.when(ze == place)
        def _():
            total = acc[16 * o : 16 * o + 16, :]
            for s in range(8):
                if s != place:
                    remote(rz.at[s], rz.at[s], sz_s.at[o], sz_r.at[s], over_z(s)).wait_recv()
                    total = total + rz[s]
            expon = jnp.exp(total[:, :128] * SCALE)
            probs = expon / jnp.sum(expon, -1, keepdims=True)
            slopes = total[:, 128:]
            mixed = SCALE * probs * (slopes - jnp.sum(probs * slopes, -1, keepdims=True))
            pm[rows, 0:128] = probs.astype(BF16)
            pm[rows, 128:256] = mixed.astype(BF16)
            out = []
            for s in range(8):
                if s != place:
                    copy = remote(pm.at[rows, :], pm.at[rows, :], sq_s.at[s], sq_r.at[o], over_z(s))
                    copy.start()
                    out.append(copy)
            for copy in out:
                copy.wait_send()

    for o, place in enumerate(OWNERS):
        rows = pl.ds(pl.multiple_of(48 * e + 16 * o, 16), 16)

        @pl.when(ze != place)
        def _():
            remote(pm.at[rows, :], pm.at[rows, :], sq_s.at[0], sq_r.at[o], over_z(place)).wait_recv()

    def chunk(ee):
        return pm.at[pl.ds(pl.multiple_of(48 * ee, 16), 48), :]

    for d in range(1, 8):
        copy = remote(chunk(e), chunk(e), sp_s.at[d], sp_r.at[d], over_e(ahead(e, d)))
        copy.start()
        sends.append(copy)
    keeps = jnp.concatenate([jnp.broadcast_to(cover(k), (READS, 128)) for k in range(4)], axis=1)
    from_core(1)
    from_far(1)
    for half in range(2):
        gp[2 * half : 2 * half + 2] = nn(to_columns(half), fg[1].reshape(512, D)).astype(BF16).reshape(2, READS, D)
    for d in range(1, 8):
        ee = behind(e, d)
        remote(chunk(ee), chunk(ee), sp_s.at[d], sp_r.at[d], over_e(ee)).wait_recv()

    eye = hot(ro == co)
    made = []
    for h, (t, _) in enumerate(plan):
        probs_b = pm[h * 128 : (h + 1) * 128, 0:128]
        mixed = pm[h * 128 : (h + 1) * 128, 128:256]
        made.append(
            (
                nn(mixed, heads[1, t]),
                nn(nt(eye, mixed).astype(BF16), heads[0, t]),
                nn(nt(eye, probs_b).astype(BF16), heads[3, t]),
                nn(probs_b, heads[2, t]),
            )
        )
    def lanes(v, k):
        return v[:, k * 128 : (k + 1) * 128]

    spare = []
    for j in range(4):
        tile0 = made[0][j] * high + made[2][j] * (low * (1.0 - par_f))
        tile1 = made[1][j] * low + made[2][j] * (high * par_f)
        if j < 3:
            tile0, tile1 = tile0 * keeps, tile1 * keeps
            full = (tile0 * (1.0 - par_f) + tile1 * par_f).astype(BF16)
            spare.append(tile1 * (1.0 - par_f) + tile0 * par_f)
        for k in range(4):
            for t, tile in ((0, tile0), (1, tile1)):
                if j < 3:
                    gr[j, k, :, t * 128 : (t + 1) * 128] = lanes(tile, k).astype(BF16)
                else:
                    ob[k, :, t * 128 : (t + 1) * 128] = lanes(tile, k).astype(BF16)
            if j < 3:
                gpk[k, :, j * 128 : (j + 1) * 128] = lanes(full, k)
    for k in range(4):
        gpk[k, :, 384:512] = (lanes(spare[0], k) + pltpu.roll(lanes(spare[1], k), 64, axis=1)).astype(BF16)
        gpk[k, :, 512:640] = lanes(spare[2], k).astype(BF16)

    def rows_of(mm):
        return pl.ds(pl.multiple_of(32 * mm, 32), 32)

    for d, mm in ((1, side_m), (2, far_m), (3, core_m)):
        copy = remote(gr.at[:, :, rows_of(mm), :], rg.at[m], sg_s.at[d], sg_r.at[d], mate(mm))
        copy.start()
        sends.append(copy)
    rg[m] = gr[:, :, rows_of(m), :]

    right = gpk[...].reshape(512, PACK)
    for half in range(2):
        part = nn(nbt[half * 384 : (half + 1) * 384, :], right).astype(BF16)
        for q in range(4):
            d = (half * 4 + q + 1) % 8
            wa[d] = part[q * 96 : (q + 1) * 96, :]
        for q in range(4):
            d = (half * 4 + q + 1) % 8
            if d > 0:
                copy = remote(wa.at[d], ra.at[d], sd_s.at[d], sd_r.at[d], over_e(ahead(e, d)))
                copy.start()
                sends.append(copy)

    ow, cw = iota((256, 256), 0), iota((256, 256), 1)
    u, zz = ow & 31, ((ow >> 5) + ze) & 7
    xi2, xx, yy = (zz >> 1) & 1, u & 1, (u >> 1) & 3
    local = 64 * par + (xi2 + xx * (3 - 2 * xi2)) * 48 + (zz & 1) * 24 + yy * 6 + (zz >> 2) * 3 + (u >> 3)
    obt[...] = nt(hot(jnp.where(u < 24, local, -1) == cw), ob[...].reshape(512, WIN)).astype(BF16)
    wb[...] = nn(obt[...], gp[...].reshape(512, D)).astype(BF16).reshape(8, 32, D)
    for d in range(1, 8):
        copy = remote(wb.at[d], rb.at[d], sb_s.at[d], sb_r.at[d], over_z(ahead(ze, d)))
        copy.start()
        sends.append(copy)

    for d, mm in ((1, side_m), (2, far_m), (3, core_m)):
        remote(gr.at[:, :, rows_of(mm), :], rg.at[mm], sg_s.at[d], sg_r.at[d], mate(mm)).wait_recv()
    for copy in full_copies:
        copy.wait()
    grad_norm = jnp.zeros((128, D), F32)
    for mm in range(4):
        lane = 128 * ((3 * mm) // 2)
        for j in range(3):
            grad_norm = grad_norm + nt(rg[mm, j].reshape(128, WIN), wv[j, :, lane : lane + WIN])
    own_feat = mine[...].astype(F32)
    inverse = lax.rsqrt(jnp.mean(own_feat * own_feat, -1, keepdims=True) + EPS)
    normed = own_feat * inverse
    result = (inverse * (grad_norm - normed * jnp.mean(grad_norm * normed, -1, keepdims=True))).astype(BF16)
    to_sources = hot(co == (ro & 3) * 32 + (ro >> 2))
    gi[...] = nn(to_sources, result).astype(BF16).reshape(8, 16, D)
    for d in range(1, 8):
        gg = ahead(g, d)
        copy = remote(gi.at[gg], ogi.at[g], si_s.at[d], si_r.at[d], over_g(gg))
        copy.start()
        sends.append(copy)
    ogi[g] = gi[g]

    total = wb[0].astype(F32)
    for d in range(1, 8):
        remote(rb.at[d], rb.at[d], sb_s.at[d], sb_r.at[d], over_z(behind(ze, d))).wait_recv()
        total = total + rb[d].astype(F32)
    rb_row, rb_col = iota((128, 32), 0), iota((128, 32), 1)
    v = rb_row & 15
    src = jnp.where(v < 3, v * 8 + (((rb_row >> 4) + e) & 7), -1)
    yb[...] = nn(hot(rb_col == src), total.astype(BF16)).astype(BF16).reshape(8, 16, D)
    for d in range(1, 8):
        copy = remote(yb.at[d], ryb.at[d], sy_s.at[d], sy_r.at[d], over_e(ahead(e, d)))
        copy.start()
        sends.append(copy)

    total = wa[0].astype(F32)
    for d in range(1, 8):
        remote(ra.at[d], ra.at[d], sd_s.at[d], sd_r.at[d], over_e(behind(e, d))).wait_recv()
        total = total + ra[d].astype(F32)
    ra_row, ra_col = iota((128, 96), 0), iota((128, 96), 1)
    v, zz = ra_row & 15, ((ra_row >> 4) + ze) & 7
    src = jnp.where(v < 12, (v >> 2) * 32 + (zz & 3) * 8 + (zz >> 2) * 4 + (v & 3), -1)
    za[...] = nn(hot(ra_col == src), total.astype(BF16)).astype(BF16).reshape(8, 16, PACK)
    for d in range(1, 8):
        copy = remote(za.at[d], rza.at[d], se_s.at[d], se_r.at[d], over_z(ahead(ze, d)))
        copy.start()
        sends.append(copy)

    for d in range(1, 8):
        slot = ogi.at[behind(g, d)]
        remote(slot, slot, si_s.at[d], si_r.at[d], over_g(behind(g, d))).wait_recv()
    from_groups = hot(co == ((ro >> 2) & 7) * 16 + (ro >> 5) * 4 + (ro & 3))
    gin[...] = nn(from_groups, ogi[...].reshape(128, D)).astype(BF16).reshape(4, 32, D)

    total = yb[0].astype(F32)
    for d in range(1, 8):
        remote(ryb.at[d], ryb.at[d], sy_s.at[d], sy_r.at[d], over_e(behind(e, d))).wait_recv()
        total = total + ryb[d].astype(F32)
    f3[...] = total[0:8, :]
    last = remote(f3, r3, s3_s.at[0], s3_r.at[0], turned)

    @pl.when(zl != m)
    def _():
        last.start()

    @pl.when(zl == m)
    def _():
        r3[...] = f3[...]

    total = za[0].astype(F32)
    for d in range(1, 8):
        remote(rza.at[d], rza.at[d], se_s.at[d], se_r.at[d], over_z(behind(ze, d))).wait_recv()
        total = total + rza[d].astype(F32)
    for mm in range(4):
        for t in range(3):
            fd[mm, t : t + 1, :] = total[t * 4 + mm : t * 4 + mm + 1, :]
        fd[mm, 3:8, :] = jnp.zeros((5, PACK), F32)
    for d, mm in ((1, side_m), (2, far_m), (3, core_m)):
        copy = remote(fd.at[mm], rj.at[m], sj_s.at[d], sj_r.at[d], mate(mm))
        copy.start()
        sends.append(copy)
    rj[m] = fd[m]

    @pl.when(zl != m)
    def _():
        last.wait()

    for d, mm in ((1, side_m), (2, far_m), (3, core_m)):
        remote(fd.at[mm], rj.at[mm], sj_s.at[d], sj_r.at[d], mate(mm)).wait_recv()
    for j in range(3):
        tiles = [jnp.zeros((3, 128), F32)] * 6
        for mm in range(4):
            side = (low, high)[mm % 2][:, :128]
            full = rj[mm, :, j * 128 : (j + 1) * 128]
            rest = rj[mm, :, (512 if j == 2 else 384) : (640 if j == 2 else 512)]
            if j == 1:
                rest = pltpu.roll(rest, 64, axis=1)
            pair = (full, rest * side) if mm % 2 == 0 else (rest * side, full)
            for at in range(2):
                tiles[(3 * mm) // 2 + at] = tiles[(3 * mm) // 2 + at] + pair[at][0:3]
        for tile in range(6):
            wsum[:, j * D + tile * 128 : j * D + (tile + 1) * 128] = tiles[tile]
    wsum[:, 3 * D : 4 * D] = r3[0:3, :]

    for copy in sends:
        copy.wait_send()
    for place, copy in late:

        @pl.when(ze != place)
        def _():
            copy.wait_send()


def hand_over(gin, wgrad, gin_out, wgrad_out, sem):
    copies = [pltpu.make_async_copy(gin, gin_out, sem.at[0]), pltpu.make_async_copy(wgrad, wgrad_out, sem.at[1])]
    for copy in copies:
        copy.start()
    for copy in copies:
        copy.wait()


def shards(features, grad_out, weights, read_start, read_end):
    hbm = pl.BlockSpec(memory_space=pl.ANY)
    vm = pl.BlockSpec(memory_space=pltpu.VMEM)
    dma = pltpu.SemaphoreType.DMA
    results = pl.pallas_call(
        kernel,
        name="tied_rows",
        out_shape=(
            pltpu.VMEM((4, 32, D), BF16),
            pltpu.VMEM((3, 4 * D), F32),
        ),
        in_specs=[hbm] * 5,
        out_specs=(vm, vm),
        scratch_shapes=[
            pltpu.VMEM((4, 32, D), BF16),
            pltpu.VMEM((4, 32, D), BF16),
            pltpu.VMEM((1, READS), I32),
            pltpu.VMEM((1, READS), I32),
            pltpu.VMEM((3, D, D), BF16),
            pltpu.VMEM((3, D, WIN), BF16),
            pltpu.VMEM((D, D), BF16),
            pltpu.VMEM((3, 8, 16, D), BF16),
            pltpu.VMEM((2, 4, 8, 16, D), BF16),
            pltpu.VMEM((8, 16, D), BF16),
            pltpu.VMEM((4, 8, 16, WIN), BF16),
            pltpu.VMEM((3, 4, READS, WIN), BF16),
            pltpu.VMEM((4, READS, D), BF16),
            pltpu.VMEM((READS, D), BF16),
            pltpu.VMEM((4, READS, D), BF16),
            pltpu.VMEM((4, READS, D), BF16),
            pltpu.VMEM((4, 2, READS, 512), BF16),
            pltpu.VMEM((2, 384, 128), F32),
            pltpu.VMEM((2, 8, 48, 128), F32),
            pltpu.VMEM((48, 256), F32),
            pltpu.VMEM((8, 16, 256), F32),
            pltpu.VMEM((384, 256), BF16),
            pltpu.VMEM((3, 4, READS, WIN), BF16),
            pltpu.VMEM((4, READS, PACK), BF16),
            pltpu.VMEM((4, READS, WIN), BF16),
            pltpu.VMEM((4, 3, 4, 32, WIN), BF16),
            pltpu.VMEM((D, 512), BF16),
            pltpu.VMEM((WIN, 512), BF16),
            pltpu.VMEM((8, 96, PACK), BF16),
            pltpu.VMEM((8, 96, PACK), BF16),
            pltpu.VMEM((8, 32, D), BF16),
            pltpu.VMEM((8, 32, D), BF16),
            pltpu.VMEM((8, 16, PACK), BF16),
            pltpu.VMEM((8, 16, PACK), BF16),
            pltpu.VMEM((8, 16, D), BF16),
            pltpu.VMEM((8, 16, D), BF16),
            pltpu.VMEM((4, 8, PACK), F32),
            pltpu.VMEM((4, 8, PACK), F32),
            pltpu.VMEM((8, D), F32),
            pltpu.VMEM((8, D), F32),
            pltpu.VMEM((8, 16, D), BF16),
            pltpu.VMEM((8, 16, D), BF16),
            dma((4,)), dma((7,)),
            dma((3, 8)), dma((3, 8)), dma((4,)), dma((4,)), dma((2,)), dma((2,)), dma((2,)), dma((2,)), dma((2,)), dma((2,)),
            dma((2, 8)), dma((2, 8)),
            dma((3,)), dma((8,)),
            dma((8,)), dma((3,)),
            dma((8,)), dma((8,)),
            dma((4,)), dma((4,)),
            dma((8,)), dma((8,)),
            dma((8,)), dma((8,)),
            dma((8,)), dma((8,)),
            dma((8,)), dma((8,)),
            dma((4,)), dma((4,)),
            dma((1,)), dma((1,)),
            dma((8,)), dma((8,)),
        ],
        compiler_params=pltpu.CompilerParams(
            collective_id=0, has_side_effects=True, vmem_limit_bytes=56 * 1024 * 1024
        ),
    )(features, grad_out, read_start.reshape(1, READS), read_end.reshape(1, READS), weights)
    return pl.pallas_call(
        hand_over,
        name="hand_over",
        out_shape=tuple(jax.ShapeDtypeStruct(r.shape, r.dtype) for r in results),
        in_specs=[vm, vm],
        out_specs=(hbm, hbm),
        scratch_shapes=[dma((2,))],
        compiler_params=pltpu.CompilerParams(vmem_limit_bytes=4 * 1024 * 1024),
    )(*results)


def solution(mesh):
    in_specs = (P("read", "pos", None), P("read", "pos", None), P(), P(), P())
    out_specs = (P("read", "pos", None), P(("read", "pos"), None))
    return jax.shard_map(shards, mesh=mesh, in_specs=in_specs, out_specs=out_specs, check_vma=False)
```

```python
import math

import jax
import jax.numpy as jnp
from jax import lax
from jax.experimental import pallas as pl
from jax.experimental.pallas import tpu as pltpu
from jax.sharding import PartitionSpec as P

F32, BF16, I32 = jnp.float32, jnp.bfloat16, jnp.int32
D = 768
WIN = 256
PARTS = ((0, 384), (384, 256))
PACK = 640
READS = 128
SCALE = 1.0 / 128.0
EPS = 1e-05
OWNERS = (0, 3, 5)


def nt(a, b):
    return lax.dot_general(a, b, (((1,), (1,)), ((), ())), preferred_element_type=F32)


def nn(a, b):
    return jnp.dot(a, b, preferred_element_type=F32)


def iota(shape, dim):
    return lax.broadcasted_iota(I32, shape, dim)


def hot(cond):
    return jnp.where(cond, 1.0, 0.0).astype(BF16)


def read_of(g, m):
    zl, xp = lax.div(g, 2), lax.rem(g, 2)
    xi, c = lax.div(m, 2), lax.rem(m, 2)
    return zl * 8 + (xi + xp * (3 - 2 * xi)) * 2 + c


def kernel(
    feat_hbm, gout_hbm, starts_hbm, ends_hbm, w_hbm, gin, wsum,
    feat, gout, starts, ends, wv, ww, w3, a_buf, fg, bg, bx, qa, na, mine, gp, nb, heads, lbuf, rl, acc, rz, pm,
    gr, gpk, ob, rg, nbt, obt, wa0, wa1, ra0, ra1, wb, rb, za0, za1, rza0, rza1, yb, ryb, fd, rj, f3, r3, gi, ogi,
    s_in, s_w, sa_s, sa_r, sh_s, sh_r, sc_s, sc_r, sx_s, sx_r, sf_s, sf_r, sl_s, sl_r, sz_s, sz_r,
    sq_s, sq_r, sp_s, sp_r, sg_s, sg_r, sd_s, sd_r, se_s, se_r, sb_s, sb_r, sy_s, sy_r, sj_s, sj_r, s3_s, s3_r, si_s, si_r,
):
    ri, pi = lax.axis_index("read"), lax.axis_index("pos")
    zl, x, c = lax.div(ri, 8), lax.rem(lax.div(ri, 2), 4), lax.rem(ri, 2)
    xp = lax.div(x, 2)
    xi = x + xp * (3 - 2 * x)
    y, zh = lax.div(pi, 2), lax.rem(pi, 2)
    g, m = zl * 2 + xp, xi * 2 + c
    e, ze = y * 2 + xp, zh * 4 + zl
    par = lax.rem(m, 2)
    off = pl.multiple_of(128 * lax.div(3 * m, 2), 128)
    core_m = xi * 2 + (1 - c)
    side_m = (1 - xi) * 2 + c
    far_m = (1 - xi) * 2 + (1 - c)

    def remote(src, dst, ss, rs, dev):
        return pltpu.make_async_remote_copy(
            src_ref=src, dst_ref=dst, send_sem=ss, recv_sem=rs,
            device_id=dev, device_id_type=pl.DeviceIdType.MESH,
        )

    def mate(mm):
        return (read_of(g, mm), pi)

    def over_g(gg):
        return (read_of(gg, m), pi)

    def over_e(ee):
        return (read_of(zl * 2 + lax.rem(ee, 2), m), lax.div(ee, 2) * 2 + zh)

    def over_z(zz):
        return (read_of(lax.rem(zz, 4) * 2 + xp, m), y * 2 + lax.div(zz, 4))

    def ahead(v, d):
        return lax.rem(v + d, 8)

    def behind(v, d):
        return lax.rem(v + 8 - d, 8)

    z1, z0 = lax.div(zl, 2), lax.rem(zl, 2)

    def twin(d):
        a, b, q = z1, z0, xp
        a = 1 - a if d & 4 else a
        b = 1 - b if d & 2 else b
        q = 1 - q if d & 1 else q
        return a * 4 + b * 2 + q

    NEAR, FAR = (1, 2, 3), (4, 5, 6, 7)

    def side_of(ref, far):
        return ref.at[pl.ds((1 - z1 if far else z1) * 4, 4)]

    turned = (read_of(m * 2 + xp, zl), pi)
    sends = []
    wa, ra, za, rza = (wa0, wa1), (ra0, ra1), (za0, za1), (rza0, rza1)

    in_copies = [
        pltpu.make_async_copy(src, dst, s_in.at[i])
        for i, (src, dst) in enumerate(
            ((feat_hbm, feat), (gout_hbm, gout), (starts_hbm, starts), (ends_hbm, ends))
        )
    ]
    for copy in in_copies:
        copy.start()

    barrier = pltpu.get_barrier_semaphore()

    def greet(dev):
        pl.semaphore_signal(barrier, inc=1, device_id=dev, device_id_type=pl.DeviceIdType.MESH)

    for d in range(1, 8):
        greet(over_g(twin(d)))
        greet(over_e(ahead(e, d)))
        greet(over_z(ahead(ze, d)))
    for mm in (core_m, side_m, far_m):
        greet(mate(mm))

    @pl.when(zl != m)
    def _():
        greet(turned)

    win_copies = [
        pltpu.make_async_copy(w_hbm.at[j, :, pl.ds(off, WIN)], ww.at[j], s_w.at[j]) for j in range(3)
    ]
    w3_copy = pltpu.make_async_copy(w_hbm.at[3], w3, s_w.at[3])
    full_copies = [pltpu.make_async_copy(w_hbm.at[j], wv.at[j], s_w.at[4 + j]) for j in range(3)]
    for copy in [w3_copy] + win_copies + full_copies:
        copy.start()

    ro, co = iota((128, 128), 0), iota((128, 128), 1)
    to_groups = hot(co == ((ro >> 2) & 3) * 32 + (ro >> 4) * 4 + (ro & 3))
    def by_group(ref):
        return nn(to_groups, ref[...].reshape(128, D)).astype(BF16)

    def spread(i, dst):
        dst[g] = a_buf[i, g]
        for d in FAR + NEAR:
            gg = twin(d)
            copy = remote(a_buf.at[i, gg], dst.at[g], sa_s.at[i, d], sa_r.at[i, d], over_g(gg))
            copy.start()
            sends.append(copy)

    def gathered(i, dst, far):
        for d in FAR if far else NEAR:
            slot = dst.at[twin(d)]
            remote(slot, slot, sa_s.at[i, d], sa_r.at[i, d], over_g(twin(d))).wait_recv()

    in_copies[0].wait()
    a_buf[0] = by_group(feat).reshape(8, 16, D)

    @pl.when(zl == m)
    def _():
        pl.semaphore_wait(barrier, 24)

    @pl.when(zl != m)
    def _():
        pl.semaphore_wait(barrier, 25)

    spread(0, fg.at[0, m])
    in_copies[1].wait()
    local_grad = by_group(gout)
    a_buf[1] = local_grad.reshape(8, 16, D)
    w3_copy.wait()
    a_buf[2] = nt(local_grad, w3[...]).astype(BF16).reshape(8, 16, D)
    spread(2, bg)
    spread(1, fg.at[1, m])

    def first(t, far):
        gathered(t, fg.at[t, m], far)
        slot = side_of(fg.at[t, m], far)
        for ss, rs, mm in ((sx_s, sx_r, side_m), (sc_s, sc_r, core_m)):
            copy = remote(slot, slot, ss.at[t, far], rs.at[t, far], mate(mm))
            copy.start()
            sends.append(copy)

    def second(t, far):
        slot = side_of(fg.at[t, side_m], far)
        remote(slot, slot, sx_s.at[t, far], sx_r.at[t, far], mate(side_m)).wait_recv()
        copy = remote(slot, slot, sf_s.at[t, far], sf_r.at[t, far], mate(core_m))
        copy.start()
        sends.append(copy)

    def from_core(t):
        for far in (0, 1):
            slot = side_of(fg.at[t, core_m], far)
            remote(slot, slot, sc_s.at[t, far], sc_r.at[t, far], mate(core_m)).wait_recv()

    def from_far(t):
        for far in (0, 1):
            slot = side_of(fg.at[t, far_m], far)
            remote(slot, slot, sf_s.at[t, far], sf_r.at[t, far], mate(core_m)).wait_recv()

    def project(mm):
        f32 = fg[0, mm].reshape(128, D).astype(F32)
        inverse = lax.rsqrt(jnp.mean(f32 * f32, -1, keepdims=True) + EPS)
        normed_b = (f32 * inverse).astype(BF16)
        na[mm] = normed_b
        for j in range(3):
            qa[j, mm] = nn(normed_b, ww[j]).astype(BF16)

    first(0, 0)
    for copy in in_copies[2:] + win_copies:
        copy.wait()
    first(0, 1)
    second(0, 0)
    project(m)
    from_core(0)
    project(core_m)

    def window(mm, far):
        lane = pl.multiple_of(128 * lax.div(3 * mm, 2), 128)
        return side_of(bg, far).at[:, :, pl.ds(lane, WIN)]

    def trade(far):
        gathered(2, bg, far)
        for d, mm in ((1, side_m), (2, far_m), (3, core_m)):
            copy = remote(window(mm, far), side_of(bx.at[m], far), sh_s.at[far, d], sh_r.at[far, d], mate(mm))
            copy.start()
            sends.append(copy)

    trade(0)
    second(0, 1)
    trade(1)
    nat = iota((READS, READS), 0)
    gs_v, ms_v, r_v = (nat >> 2) & 7, nat >> 5, nat & 3
    xi_v, xp_v = ms_v >> 1, gs_v & 1
    nat = 4 * ((gs_v >> 1) * 8 + (xi_v + xp_v * (3 - 2 * xi_v)) * 2 + (ms_v & 1)) + r_v
    pick = iota((READS, READS), 1) == nat
    begin = jnp.sum(jnp.where(pick, starts[...].astype(F32), 0.0), axis=1, keepdims=True)
    close = jnp.sum(jnp.where(pick, ends[...].astype(F32), 0.0), axis=1, keepdims=True)

    def cover(k):
        col = (32 * pi + 4 * g + k).astype(F32)
        return jnp.where(col >= begin, 1.0, 0.0) * jnp.where(col < close, 1.0, 0.0)

    project(side_m)
    bx[m] = bg[:, :, pl.ds(off, WIN)]
    pr, pc = iota((256, 512), 0), iota((256, 512), 1)

    def to_columns(half):
        return hot(pc == (pr & 127) * 4 + (pr >> 7) + 2 * half)

    def set_heads(j, half, part):
        for k in range(2):
            for t in range(2):
                at = (2 * half + k) * 128
                heads[j, t, :, at : at + 128] = part[k * 128 : (k + 1) * 128, t * 128 : (t + 1) * 128]

    from_far(0)
    project(far_m)
    for half in range(2):
        keep = jnp.concatenate([cover(2 * half), cover(2 * half + 1)], axis=0)
        for j in range(3):
            set_heads(j, half, (nn(to_columns(half), qa[j].reshape(512, WIN)) * keep).astype(BF16))

    low = jnp.where((iota((1, 512), 1) & 127) < 64, 1.0, 0.0)
    high = 1.0 - low
    par_f = par.astype(F32)
    own = low * (1.0 - par_f) + high * par_f
    plan = ((0, high), (1, low), (par, own))

    def scores(which, left, right):
        for h, (t, mask) in enumerate(plan):
            lbuf[which, h * 128 : (h + 1) * 128, :] = nt(heads[left, t] * mask.astype(BF16), heads[right, t])
        for d in range(1, 8):
            ee = ahead(e, d)
            copy = remote(
                lbuf.at[which, pl.ds(pl.multiple_of(48 * ee, 16), 48), :], rl.at[which, d],
                sl_s.at[which, d], sl_r.at[which, d], over_e(ee),
            )
            copy.start()
            sends.append(copy)

    scores(0, 0, 1)
    for far in (0, 1):
        for d, mm in ((1, side_m), (2, far_m), (3, core_m)):
            slot = side_of(bx.at[mm], far)
            remote(slot, slot, sh_s.at[far, d], sh_r.at[far, d], mate(mm)).wait_recv()
    for half in range(2):
        set_heads(3, half, nn(to_columns(half), bx[...].reshape(512, WIN)).astype(BF16))
    scores(1, 3, 2)

    first(1, 0)
    first(1, 1)
    for half in range(2):
        nb[2 * half : 2 * half + 2] = nn(to_columns(half), na[...].reshape(512, D)).astype(BF16).reshape(2, READS, D)
    mine[...] = nn(hot(co == (ro & 31) * 4 + (ro >> 5)), fg[0, m].reshape(128, D)).astype(BF16)

    def turn(half):
        w, col = iota((96, D), 0), iota((96, D), 1)
        xi2 = (w >> 1) & 1
        picks = []
        for q in range(4):
            ee = ahead(e, half * 4 + q + 1)
            yy, xx = lax.div(ee, 2), lax.rem(ee, 2)
            row = (
                ((w >> 3) & 3) * 192 + (xi2 + xx * (3 - 2 * xi2)) * 48 + (w & 1) * 24
                + yy * 6 + ((w >> 2) & 1) * 3 + (w >> 5)
            )
            picks.append(hot(col == row))
        pick = jnp.concatenate(picks, axis=0)
        nbt[half * 384 : (half + 1) * 384, :] = nt(pick, nb[...].reshape(512, D)).astype(BF16)

    for which in range(2):
        total = lbuf[which, pl.ds(pl.multiple_of(48 * e, 16), 48), :]
        for d in range(1, 8):
            remote(
                rl.at[which, d], rl.at[which, d], sl_s.at[which, d], sl_r.at[which, d], over_e(behind(e, d))
            ).wait_recv()
            total = total + rl[which, d]
        acc[:, which * 128 : (which + 1) * 128] = total

    late = []
    for o, place in enumerate(OWNERS):
        dev = over_z(place)
        copy = remote(acc.at[pl.ds(16 * o, 16), :], rz.at[ze], sz_s.at[o], sz_r.at[ze], dev)

        @pl.when(ze != place)
        def _():
            copy.start()

        late.append((place, copy))

    second(1, 0)
    second(1, 1)
    turn(0)
    for o, place in enumerate(OWNERS):
        rows = pl.ds(pl.multiple_of(48 * e + 16 * o, 16), 16)

        @pl.when(ze == place)
        def _():
            total = acc[16 * o : 16 * o + 16, :]
            for s in range(8):
                if s != place:
                    remote(rz.at[s], rz.at[s], sz_s.at[o], sz_r.at[s], over_z(s)).wait_recv()
                    total = total + rz[s]
            expon = jnp.exp(total[:, :128] * SCALE)
            probs = expon / jnp.sum(expon, -1, keepdims=True)
            slopes = total[:, 128:]
            mixed = SCALE * probs * (slopes - jnp.sum(probs * slopes, -1, keepdims=True))
            pm[rows, 0:128] = probs.astype(BF16)
            pm[rows, 128:256] = mixed.astype(BF16)
            out = []
            for s in range(8):
                if s != place:
                    copy = remote(pm.at[rows, :], pm.at[rows, :], sq_s.at[s], sq_r.at[o], over_z(s))
                    copy.start()
                    out.append(copy)
            for copy in out:
                copy.wait_send()

    turn(1)
    for o, place in enumerate(OWNERS):
        rows = pl.ds(pl.multiple_of(48 * e + 16 * o, 16), 16)

        @pl.when(ze != place)
        def _():
            remote(pm.at[rows, :], pm.at[rows, :], sq_s.at[0], sq_r.at[o], over_z(place)).wait_recv()

    def chunk(ee):
        return pm.at[pl.ds(pl.multiple_of(48 * ee, 16), 48), :]

    for d in range(1, 8):
        copy = remote(chunk(e), chunk(e), sp_s.at[d], sp_r.at[d], over_e(ahead(e, d)))
        copy.start()
        sends.append(copy)
    keeps = jnp.concatenate([jnp.broadcast_to(cover(k), (READS, 128)) for k in range(4)], axis=1)
    from_core(1)
    from_far(1)
    for half in range(2):
        gp[2 * half : 2 * half + 2] = nn(to_columns(half), fg[1].reshape(512, D)).astype(BF16).reshape(2, READS, D)
    for d in range(1, 8):
        ee = behind(e, d)
        remote(chunk(ee), chunk(ee), sp_s.at[d], sp_r.at[d], over_e(ee)).wait_recv()

    eye = hot(ro == co)
    made = []
    for h, (t, _) in enumerate(plan):
        probs_b = pm[h * 128 : (h + 1) * 128, 0:128]
        mixed = pm[h * 128 : (h + 1) * 128, 128:256]
        made.append(
            (
                nn(mixed, heads[1, t]),
                nn(nt(eye, mixed).astype(BF16), heads[0, t]),
                nn(nt(eye, probs_b).astype(BF16), heads[3, t]),
                nn(probs_b, heads[2, t]),
            )
        )
    def lanes(v, k):
        return v[:, k * 128 : (k + 1) * 128]

    spare = []
    for j in range(4):
        tile0 = made[0][j] * high + made[2][j] * (low * (1.0 - par_f))
        tile1 = made[1][j] * low + made[2][j] * (high * par_f)
        if j < 3:
            tile0, tile1 = tile0 * keeps, tile1 * keeps
            full = (tile0 * (1.0 - par_f) + tile1 * par_f).astype(BF16)
            spare.append(tile1 * (1.0 - par_f) + tile0 * par_f)
        for k in range(4):
            for t, tile in ((0, tile0), (1, tile1)):
                if j < 3:
                    gr[j, k, :, t * 128 : (t + 1) * 128] = lanes(tile, k).astype(BF16)
                else:
                    ob[k, :, t * 128 : (t + 1) * 128] = lanes(tile, k).astype(BF16)
            if j < 3:
                gpk[k, :, j * 128 : (j + 1) * 128] = lanes(full, k)
    for k in range(4):
        gpk[k, :, 384:512] = (lanes(spare[0], k) + pltpu.roll(lanes(spare[1], k), 64, axis=1)).astype(BF16)
        gpk[k, :, 512:640] = lanes(spare[2], k).astype(BF16)

    def rows_of(mm):
        return pl.ds(pl.multiple_of(32 * mm, 32), 32)

    for d, mm in ((1, side_m), (2, far_m), (3, core_m)):
        copy = remote(gr.at[:, :, rows_of(mm), :], rg.at[m], sg_s.at[d], sg_r.at[d], mate(mm))
        copy.start()
        sends.append(copy)
    rg[m] = gr[:, :, rows_of(m), :]

    def left_parts(p):
        first_lane, count = PARTS[p]
        right = gpk[:, :, first_lane : first_lane + count].reshape(512, count)
        for half in range(2):
            part = nn(nbt[half * 384 : (half + 1) * 384, :], right).astype(BF16)
            for q in range(4):
                wa[p][(half * 4 + q + 1) % 8] = part[q * 96 : (q + 1) * 96, :]
            for q in range(4):
                d = (half * 4 + q + 1) % 8
                if d > 0:
                    copy = remote(wa[p].at[d], ra[p].at[d], sd_s.at[p, d], sd_r.at[p, d], over_e(ahead(e, d)))
                    copy.start()
                    sends.append(copy)

    left_parts(0)
    ow, cw = iota((256, 256), 0), iota((256, 256), 1)
    u, zz = ow & 31, ((ow >> 5) + ze) & 7
    xi2, xx, yy = (zz >> 1) & 1, u & 1, (u >> 1) & 3
    local = 64 * par + (xi2 + xx * (3 - 2 * xi2)) * 48 + (zz & 1) * 24 + yy * 6 + (zz >> 2) * 3 + (u >> 3)
    obt[...] = nt(hot(jnp.where(u < 24, local, -1) == cw), ob[...].reshape(512, WIN)).astype(BF16)
    wb[...] = nn(obt[...], gp[...].reshape(512, D)).astype(BF16).reshape(8, 32, D)
    for d in range(1, 8):
        copy = remote(wb.at[d], rb.at[d], sb_s.at[d], sb_r.at[d], over_z(ahead(ze, d)))
        copy.start()
        sends.append(copy)

    left_parts(1)

    for d, mm in ((1, side_m), (2, far_m), (3, core_m)):
        remote(gr.at[:, :, rows_of(mm), :], rg.at[mm], sg_s.at[d], sg_r.at[d], mate(mm)).wait_recv()
    for copy in full_copies:
        copy.wait()
    grad_norm = jnp.zeros((128, D), F32)
    for mm in range(4):
        lane = 128 * ((3 * mm) // 2)
        for j in range(3):
            grad_norm = grad_norm + nt(rg[mm, j].reshape(128, WIN), wv[j, :, lane : lane + WIN])
    own_feat = mine[...].astype(F32)
    inverse = lax.rsqrt(jnp.mean(own_feat * own_feat, -1, keepdims=True) + EPS)
    normed = own_feat * inverse
    result = (inverse * (grad_norm - normed * jnp.mean(grad_norm * normed, -1, keepdims=True))).astype(BF16)
    to_sources = hot(co == (ro & 3) * 32 + (ro >> 2))
    gi[...] = nn(to_sources, result).astype(BF16).reshape(8, 16, D)
    for d in FAR + NEAR:
        gg = twin(d)
        copy = remote(gi.at[gg], ogi.at[g], si_s.at[d], si_r.at[d], over_g(gg))
        copy.start()
        sends.append(copy)
    ogi[g] = gi[g]

    def second_parts(p):
        count = PARTS[p][1]
        total = wa[p][0].astype(F32)
        for d in range(1, 8):
            remote(ra[p].at[d], ra[p].at[d], sd_s.at[p, d], sd_r.at[p, d], over_e(behind(e, d))).wait_recv()
            total = total + ra[p][d].astype(F32)
        ra_row, ra_col = iota((128, 96), 0), iota((128, 96), 1)
        v, zz = ra_row & 15, ((ra_row >> 4) + ze) & 7
        src = jnp.where(v < 12, (v >> 2) * 32 + (zz & 3) * 8 + (zz >> 2) * 4 + (v & 3), -1)
        za[p][...] = nn(hot(ra_col == src), total.astype(BF16)).astype(BF16).reshape(8, 16, count)
        for d in range(1, 8):
            copy = remote(za[p].at[d], rza[p].at[d], se_s.at[p, d], se_r.at[p, d], over_z(ahead(ze, d)))
            copy.start()
            sends.append(copy)

    second_parts(0)
    total = wb[0].astype(F32)
    for d in range(1, 8):
        remote(rb.at[d], rb.at[d], sb_s.at[d], sb_r.at[d], over_z(behind(ze, d))).wait_recv()
        total = total + rb[d].astype(F32)
    rb_row, rb_col = iota((128, 32), 0), iota((128, 32), 1)
    v = rb_row & 15
    src = jnp.where(v < 3, v * 8 + (((rb_row >> 4) + e) & 7), -1)
    yb[...] = nn(hot(rb_col == src), total.astype(BF16)).astype(BF16).reshape(8, 16, D)
    for d in range(1, 8):
        copy = remote(yb.at[d], ryb.at[d], sy_s.at[d], sy_r.at[d], over_e(ahead(e, d)))
        copy.start()
        sends.append(copy)

    second_parts(1)

    for d in range(1, 8):
        slot = ogi.at[twin(d)]
        remote(slot, slot, si_s.at[d], si_r.at[d], over_g(twin(d))).wait_recv()
    from_groups = hot(co == ((ro >> 2) & 7) * 16 + (ro >> 5) * 4 + (ro & 3))
    gin[...] = nn(from_groups, ogi[...].reshape(128, D)).astype(BF16).reshape(4, 32, D)

    total = yb[0].astype(F32)
    for d in range(1, 8):
        remote(ryb.at[d], ryb.at[d], sy_s.at[d], sy_r.at[d], over_e(behind(e, d))).wait_recv()
        total = total + ryb[d].astype(F32)
    f3[...] = total[0:8, :]
    last = remote(f3, r3, s3_s.at[0], s3_r.at[0], turned)

    @pl.when(zl != m)
    def _():
        last.start()

    @pl.when(zl == m)
    def _():
        r3[...] = f3[...]

    for p, (lane, count) in enumerate(PARTS):
        total = za[p][0].astype(F32)
        for d in range(1, 8):
            remote(rza[p].at[d], rza[p].at[d], se_s.at[p, d], se_r.at[p, d], over_z(behind(ze, d))).wait_recv()
            total = total + rza[p][d].astype(F32)
        for mm in range(4):
            for t in range(3):
                fd[mm, t : t + 1, lane : lane + count] = total[t * 4 + mm : t * 4 + mm + 1, :]
            fd[mm, 3:8, lane : lane + count] = jnp.zeros((5, count), F32)
    for d, mm in ((1, side_m), (2, far_m), (3, core_m)):
        copy = remote(fd.at[mm], rj.at[m], sj_s.at[d], sj_r.at[d], mate(mm))
        copy.start()
        sends.append(copy)
    rj[m] = fd[m]

    @pl.when(zl != m)
    def _():
        last.wait()

    for d, mm in ((1, side_m), (2, far_m), (3, core_m)):
        remote(fd.at[mm], rj.at[mm], sj_s.at[d], sj_r.at[d], mate(mm)).wait_recv()
    for j in range(3):
        tiles = [jnp.zeros((3, 128), F32)] * 6
        for mm in range(4):
            side = (low, high)[mm % 2][:, :128]
            full = rj[mm, :, j * 128 : (j + 1) * 128]
            rest = rj[mm, :, (512 if j == 2 else 384) : (640 if j == 2 else 512)]
            if j == 1:
                rest = pltpu.roll(rest, 64, axis=1)
            pair = (full, rest * side) if mm % 2 == 0 else (rest * side, full)
            for at in range(2):
                tiles[(3 * mm) // 2 + at] = tiles[(3 * mm) // 2 + at] + pair[at][0:3]
        for tile in range(6):
            wsum[:, j * D + tile * 128 : j * D + (tile + 1) * 128] = tiles[tile]
    wsum[:, 3 * D : 4 * D] = r3[0:3, :]

    for copy in sends:
        copy.wait_send()
    for place, copy in late:

        @pl.when(ze != place)
        def _():
            copy.wait_send()


def hand_over(gin, wgrad, gin_out, wgrad_out, sem):
    copies = [pltpu.make_async_copy(gin, gin_out, sem.at[0]), pltpu.make_async_copy(wgrad, wgrad_out, sem.at[1])]
    for copy in copies:
        copy.start()
    for copy in copies:
        copy.wait()


def shards(features, grad_out, weights, read_start, read_end):
    hbm = pl.BlockSpec(memory_space=pl.ANY)
    vm = pl.BlockSpec(memory_space=pltpu.VMEM)
    dma = pltpu.SemaphoreType.DMA
    results = pl.pallas_call(
        kernel,
        name="tied_rows",
        out_shape=(
            pltpu.VMEM((4, 32, D), BF16),
            pltpu.VMEM((3, 4 * D), F32),
        ),
        in_specs=[hbm] * 5,
        out_specs=(vm, vm),
        scratch_shapes=[
            pltpu.VMEM((4, 32, D), BF16),
            pltpu.VMEM((4, 32, D), BF16),
            pltpu.VMEM((1, READS), I32),
            pltpu.VMEM((1, READS), I32),
            pltpu.VMEM((3, D, D), BF16),
            pltpu.VMEM((3, D, WIN), BF16),
            pltpu.VMEM((D, D), BF16),
            pltpu.VMEM((3, 8, 16, D), BF16),
            pltpu.VMEM((2, 4, 8, 16, D), BF16),
            pltpu.VMEM((8, 16, D), BF16),
            pltpu.VMEM((4, 8, 16, WIN), BF16),
            pltpu.VMEM((3, 4, READS, WIN), BF16),
            pltpu.VMEM((4, READS, D), BF16),
            pltpu.VMEM((READS, D), BF16),
            pltpu.VMEM((4, READS, D), BF16),
            pltpu.VMEM((4, READS, D), BF16),
            pltpu.VMEM((4, 2, READS, 512), BF16),
            pltpu.VMEM((2, 384, 128), F32),
            pltpu.VMEM((2, 8, 48, 128), F32),
            pltpu.VMEM((48, 256), F32),
            pltpu.VMEM((8, 16, 256), F32),
            pltpu.VMEM((384, 256), BF16),
            pltpu.VMEM((3, 4, READS, WIN), BF16),
            pltpu.VMEM((4, READS, PACK), BF16),
            pltpu.VMEM((4, READS, WIN), BF16),
            pltpu.VMEM((4, 3, 4, 32, WIN), BF16),
            pltpu.VMEM((D, 512), BF16),
            pltpu.VMEM((WIN, 512), BF16),
            pltpu.VMEM((8, 96, PARTS[0][1]), BF16),
            pltpu.VMEM((8, 96, PARTS[1][1]), BF16),
            pltpu.VMEM((8, 96, PARTS[0][1]), BF16),
            pltpu.VMEM((8, 96, PARTS[1][1]), BF16),
            pltpu.VMEM((8, 32, D), BF16),
            pltpu.VMEM((8, 32, D), BF16),
            pltpu.VMEM((8, 16, PARTS[0][1]), BF16),
            pltpu.VMEM((8, 16, PARTS[1][1]), BF16),
            pltpu.VMEM((8, 16, PARTS[0][1]), BF16),
            pltpu.VMEM((8, 16, PARTS[1][1]), BF16),
            pltpu.VMEM((8, 16, D), BF16),
            pltpu.VMEM((8, 16, D), BF16),
            pltpu.VMEM((4, 8, PACK), F32),
            pltpu.VMEM((4, 8, PACK), F32),
            pltpu.VMEM((8, D), F32),
            pltpu.VMEM((8, D), F32),
            pltpu.VMEM((8, 16, D), BF16),
            pltpu.VMEM((8, 16, D), BF16),
            dma((4,)), dma((7,)),
            dma((3, 8)), dma((3, 8)), dma((2, 4)), dma((2, 4)),
            dma((2, 2)), dma((2, 2)), dma((2, 2)), dma((2, 2)), dma((2, 2)), dma((2, 2)),
            dma((2, 8)), dma((2, 8)),
            dma((3,)), dma((8,)),
            dma((8,)), dma((3,)),
            dma((8,)), dma((8,)),
            dma((4,)), dma((4,)),
            dma((2, 8)), dma((2, 8)),
            dma((2, 8)), dma((2, 8)),
            dma((8,)), dma((8,)),
            dma((8,)), dma((8,)),
            dma((4,)), dma((4,)),
            dma((1,)), dma((1,)),
            dma((8,)), dma((8,)),
        ],
        compiler_params=pltpu.CompilerParams(
            collective_id=0, has_side_effects=True, vmem_limit_bytes=56 * 1024 * 1024
        ),
    )(features, grad_out, read_start.reshape(1, READS), read_end.reshape(1, READS), weights)
    return pl.pallas_call(
        hand_over,
        name="hand_over",
        out_shape=tuple(jax.ShapeDtypeStruct(r.shape, r.dtype) for r in results),
        in_specs=[vm, vm],
        out_specs=(hbm, hbm),
        scratch_shapes=[dma((2,))],
        compiler_params=pltpu.CompilerParams(vmem_limit_bytes=4 * 1024 * 1024),
    )(*results)


def solution(mesh):
    in_specs = (P("read", "pos", None), P("read", "pos", None), P(), P(), P())
    out_specs = (P("read", "pos", None), P(("read", "pos"), None))
    return jax.shard_map(shards, mesh=mesh, in_specs=in_specs, out_specs=out_specs, check_vma=False)
```

```python
import math

import jax
import jax.numpy as jnp
from jax import lax
from jax.experimental import pallas as pl
from jax.experimental.pallas import tpu as pltpu
from jax.sharding import PartitionSpec as P

F32, BF16, I32 = jnp.float32, jnp.bfloat16, jnp.int32
D = 768
WIN = 256
PARTS = ((0, 384), (384, 256))
PACK = 640
READS = 128
SCALE = 1.0 / 128.0
EPS = 1e-05
OWNERS = (0, 3, 5)


def nt(a, b):
    return lax.dot_general(a, b, (((1,), (1,)), ((), ())), preferred_element_type=F32)


def nn(a, b):
    return jnp.dot(a, b, preferred_element_type=F32)


def iota(shape, dim):
    return lax.broadcasted_iota(I32, shape, dim)


def hot(cond):
    return jnp.where(cond, 1.0, 0.0).astype(BF16)


def read_of(g, m):
    zl, xp = lax.div(g, 2), lax.rem(g, 2)
    xi, c = lax.div(m, 2), lax.rem(m, 2)
    return zl * 8 + (xi + xp * (3 - 2 * xi)) * 2 + c


def kernel(
    feat_hbm, gout_hbm, starts_hbm, ends_hbm, w_hbm, gin, wsum,
    feat, gout, starts, ends, wv, ww, w3, a_buf, fg, to_columns, bg, bx, qa, na, mine, gp, nb, heads, lbuf, rl, acc, rz, pm,
    gr, gpk, ob, rg, nbt, obt, wa0, wa1, ra0, ra1, wb, rb, za0, za1, rza0, rza1, yb, ryb, fd, rj, f3, r3, gi, ogi,
    s_in, s_w, sa_s, sa_r, sh_s, sh_r, sc_s, sc_r, sx_s, sx_r, sf_s, sf_r, sl_s, sl_r, sz_s, sz_r,
    sq_s, sq_r, sp_s, sp_r, sg_s, sg_r, sd_s, sd_r, se_s, se_r, sb_s, sb_r, sy_s, sy_r, sj_s, sj_r, s3_s, s3_r, si_s, si_r,
):
    ri, pi = lax.axis_index("read"), lax.axis_index("pos")
    zl, x, c = lax.div(ri, 8), lax.rem(lax.div(ri, 2), 4), lax.rem(ri, 2)
    xp = lax.div(x, 2)
    xi = x + xp * (3 - 2 * x)
    y, zh = lax.div(pi, 2), lax.rem(pi, 2)
    g, m = zl * 2 + xp, xi * 2 + c
    e, ze = y * 2 + xp, zh * 4 + zl
    par = lax.rem(m, 2)
    off = pl.multiple_of(128 * lax.div(3 * m, 2), 128)
    core_m = xi * 2 + (1 - c)
    side_m = (1 - xi) * 2 + c
    far_m = (1 - xi) * 2 + (1 - c)

    def remote(src, dst, ss, rs, dev):
        return pltpu.make_async_remote_copy(
            src_ref=src, dst_ref=dst, send_sem=ss, recv_sem=rs,
            device_id=dev, device_id_type=pl.DeviceIdType.MESH,
        )

    def mate(mm):
        return (read_of(g, mm), pi)

    def over_g(gg):
        return (read_of(gg, m), pi)

    def over_e(ee):
        return (read_of(zl * 2 + lax.rem(ee, 2), m), lax.div(ee, 2) * 2 + zh)

    def over_z(zz):
        return (read_of(lax.rem(zz, 4) * 2 + xp, m), y * 2 + lax.div(zz, 4))

    def ahead(v, d):
        return lax.rem(v + d, 8)

    def behind(v, d):
        return lax.rem(v + 8 - d, 8)

    z1, z0 = lax.div(zl, 2), lax.rem(zl, 2)

    def twin(d):
        a, b, q = z1, z0, xp
        a = 1 - a if d & 4 else a
        b = 1 - b if d & 2 else b
        q = 1 - q if d & 1 else q
        return a * 4 + b * 2 + q

    NEAR, FAR = (1, 2, 3), (4, 5, 6, 7)

    def side_of(ref, far):
        return ref.at[pl.ds((1 - z1 if far else z1) * 4, 4)]

    turned = (read_of(m * 2 + xp, zl), pi)
    sends = []
    wa, ra, za, rza = (wa0, wa1), (ra0, ra1), (za0, za1), (rza0, rza1)

    in_copies = [
        pltpu.make_async_copy(src, dst, s_in.at[i])
        for i, (src, dst) in enumerate(
            ((feat_hbm, feat), (gout_hbm, gout), (starts_hbm, starts), (ends_hbm, ends))
        )
    ]
    for copy in in_copies:
        copy.start()

    barrier = pltpu.get_barrier_semaphore()

    def greet(dev):
        pl.semaphore_signal(barrier, inc=1, device_id=dev, device_id_type=pl.DeviceIdType.MESH)

    for d in range(1, 8):
        greet(over_g(twin(d)))
        greet(over_e(ahead(e, d)))
        greet(over_z(ahead(ze, d)))
    for mm in (core_m, side_m, far_m):
        greet(mate(mm))

    @pl.when(zl != m)
    def _():
        greet(turned)

    win_copies = [
        pltpu.make_async_copy(w_hbm.at[j, :, pl.ds(off, WIN)], ww.at[j], s_w.at[j]) for j in range(3)
    ]
    w3_copy = pltpu.make_async_copy(w_hbm.at[3], w3, s_w.at[3])
    full_copies = [pltpu.make_async_copy(w_hbm.at[j], wv.at[j], s_w.at[4 + j]) for j in range(3)]
    for copy in [w3_copy] + win_copies + full_copies:
        copy.start()

    ro, co = iota((128, 128), 0), iota((128, 128), 1)
    to_groups = hot(co == ((ro >> 2) & 3) * 32 + (ro >> 4) * 4 + (ro & 3))
    def by_group(ref):
        return nn(to_groups, ref[...].reshape(128, D)).astype(BF16)

    def spread(i, dst):
        dst[g] = a_buf[i, g]
        for d in FAR + NEAR:
            gg = twin(d)
            copy = remote(a_buf.at[i, gg], dst.at[g], sa_s.at[i, d], sa_r.at[i, d], over_g(gg))
            copy.start()
            sends.append(copy)

    def gathered(i, dst, far):
        for d in FAR if far else NEAR:
            slot = dst.at[twin(d)]
            remote(slot, slot, sa_s.at[i, d], sa_r.at[i, d], over_g(twin(d))).wait_recv()

    in_copies[0].wait()
    a_buf[0] = by_group(feat).reshape(8, 16, D)

    @pl.when(zl == m)
    def _():
        pl.semaphore_wait(barrier, 24)

    @pl.when(zl != m)
    def _():
        pl.semaphore_wait(barrier, 25)

    spread(0, fg.at[0, m])
    in_copies[1].wait()
    local_grad = by_group(gout)
    a_buf[1] = local_grad.reshape(8, 16, D)
    w3_copy.wait()
    a_buf[2] = nt(local_grad, w3[...]).astype(BF16).reshape(8, 16, D)
    spread(2, bg)
    spread(1, fg.at[1, m])

    def first(t, far):
        gathered(t, fg.at[t, m], far)
        slot = side_of(fg.at[t, m], far)
        for ss, rs, mm in ((sx_s, sx_r, side_m), (sc_s, sc_r, core_m)):
            copy = remote(slot, slot, ss.at[t, far], rs.at[t, far], mate(mm))
            copy.start()
            sends.append(copy)

    def second(t, far):
        slot = side_of(fg.at[t, side_m], far)
        remote(slot, slot, sx_s.at[t, far], sx_r.at[t, far], mate(side_m)).wait_recv()
        copy = remote(slot, slot, sf_s.at[t, far], sf_r.at[t, far], mate(core_m))
        copy.start()
        sends.append(copy)

    def from_core(t):
        for far in (0, 1):
            slot = side_of(fg.at[t, core_m], far)
            remote(slot, slot, sc_s.at[t, far], sc_r.at[t, far], mate(core_m)).wait_recv()

    def from_far(t):
        for far in (0, 1):
            slot = side_of(fg.at[t, far_m], far)
            remote(slot, slot, sf_s.at[t, far], sf_r.at[t, far], mate(core_m)).wait_recv()

    def project(mm):
        f32 = fg[0, mm].reshape(128, D).astype(F32)
        inverse = lax.rsqrt(jnp.mean(f32 * f32, -1, keepdims=True) + EPS)
        normed_b = (f32 * inverse).astype(BF16)
        na[mm] = normed_b
        for j in range(3):
            qa[j, mm] = nn(normed_b, ww[j]).astype(BF16)

    for k in range(4):
        pr, pc = iota((READS, 512), 0), iota((READS, 512), 1)
        to_columns[k * 128 : (k + 1) * 128, :] = hot(pc == pr * 4 + k)
    first(0, 0)
    for copy in in_copies[2:] + win_copies:
        copy.wait()
    first(0, 1)
    second(0, 0)
    project(m)
    from_core(0)
    project(core_m)

    def window(mm, far):
        lane = pl.multiple_of(128 * lax.div(3 * mm, 2), 128)
        return side_of(bg, far).at[:, :, pl.ds(lane, WIN)]

    def trade(far):
        gathered(2, bg, far)
        for d, mm in ((1, side_m), (2, far_m), (3, core_m)):
            copy = remote(window(mm, far), side_of(bx.at[m], far), sh_s.at[far, d], sh_r.at[far, d], mate(mm))
            copy.start()
            sends.append(copy)

    trade(0)
    second(0, 1)
    trade(1)
    nat = iota((READS, READS), 0)
    gs_v, ms_v, r_v = (nat >> 2) & 7, nat >> 5, nat & 3
    xi_v, xp_v = ms_v >> 1, gs_v & 1
    nat = 4 * ((gs_v >> 1) * 8 + (xi_v + xp_v * (3 - 2 * xi_v)) * 2 + (ms_v & 1)) + r_v
    pick = iota((READS, READS), 1) == nat
    begin = jnp.sum(jnp.where(pick, starts[...].astype(F32), 0.0), axis=1, keepdims=True)
    close = jnp.sum(jnp.where(pick, ends[...].astype(F32), 0.0), axis=1, keepdims=True)

    def cover(k):
        col = (32 * pi + 4 * g + k).astype(F32)
        return jnp.where(col >= begin, 1.0, 0.0) * jnp.where(col < close, 1.0, 0.0)

    project(side_m)
    bx[m] = bg[:, :, pl.ds(off, WIN)]
    def set_heads(j, part):
        for k in range(4):
            for t in range(2):
                heads[j, t, :, k * 128 : (k + 1) * 128] = part[k * 128 : (k + 1) * 128, t * 128 : (t + 1) * 128]

    keep = jnp.concatenate([cover(k) for k in range(4)], axis=0)
    from_far(0)
    project(far_m)
    for j in range(3):
        set_heads(j, (nn(to_columns[...], qa[j].reshape(512, WIN)) * keep).astype(BF16))

    low = jnp.where((iota((1, 512), 1) & 127) < 64, 1.0, 0.0)
    high = 1.0 - low
    par_f = par.astype(F32)
    own = low * (1.0 - par_f) + high * par_f
    plan = ((0, high), (1, low), (par, own))

    def scores(which, left, right):
        for h, (t, mask) in enumerate(plan):
            lbuf[which, h * 128 : (h + 1) * 128, :] = nt(heads[left, t] * mask.astype(BF16), heads[right, t])
        for d in range(1, 8):
            ee = ahead(e, d)
            copy = remote(
                lbuf.at[which, pl.ds(pl.multiple_of(48 * ee, 16), 48), :], rl.at[which, d],
                sl_s.at[which, d], sl_r.at[which, d], over_e(ee),
            )
            copy.start()
            sends.append(copy)

    scores(0, 0, 1)
    for far in (0, 1):
        for d, mm in ((1, side_m), (2, far_m), (3, core_m)):
            slot = side_of(bx.at[mm], far)
            remote(slot, slot, sh_s.at[far, d], sh_r.at[far, d], mate(mm)).wait_recv()
    set_heads(3, nn(to_columns[...], bx[...].reshape(512, WIN)).astype(BF16))
    scores(1, 3, 2)

    first(1, 0)
    first(1, 1)
    for half in range(2):
        rows = to_columns[half * 256 : (half + 1) * 256, :]
        nb[2 * half : 2 * half + 2] = nn(rows, na[...].reshape(512, D)).astype(BF16).reshape(2, READS, D)
    mine[...] = nn(hot(co == (ro & 31) * 4 + (ro >> 5)), fg[0, m].reshape(128, D)).astype(BF16)

    def turn(half):
        w, col = iota((96, D), 0), iota((96, D), 1)
        xi2 = (w >> 1) & 1
        picks = []
        for q in range(4):
            ee = ahead(e, half * 4 + q + 1)
            yy, xx = lax.div(ee, 2), lax.rem(ee, 2)
            row = (
                ((w >> 3) & 3) * 192 + (xi2 + xx * (3 - 2 * xi2)) * 48 + (w & 1) * 24
                + yy * 6 + ((w >> 2) & 1) * 3 + (w >> 5)
            )
            picks.append(hot(col == row))
        pick = jnp.concatenate(picks, axis=0)
        nbt[half * 384 : (half + 1) * 384, :] = nt(pick, nb[...].reshape(512, D)).astype(BF16)

    for which in range(2):
        total = lbuf[which, pl.ds(pl.multiple_of(48 * e, 16), 48), :]
        for d in range(1, 8):
            remote(
                rl.at[which, d], rl.at[which, d], sl_s.at[which, d], sl_r.at[which, d], over_e(behind(e, d))
            ).wait_recv()
            total = total + rl[which, d]
        acc[:, which * 128 : (which + 1) * 128] = total

    late = []
    for o, place in enumerate(OWNERS):
        dev = over_z(place)
        copy = remote(acc.at[pl.ds(16 * o, 16), :], rz.at[ze], sz_s.at[o], sz_r.at[ze], dev)

        @pl.when(ze != place)
        def _():
            copy.start()

        late.append((place, copy))

    second(1, 0)
    second(1, 1)
    turn(0)
    for o, place in enumerate(OWNERS):
        rows = pl.ds(pl.multiple_of(48 * e + 16 * o, 16), 16)

        @pl.when(ze == place)
        def _():
            total = acc[16 * o : 16 * o + 16, :]
            for s in range(8):
                if s != place:
                    remote(rz.at[s], rz.at[s], sz_s.at[o], sz_r.at[s], over_z(s)).wait_recv()
                    total = total + rz[s]
            expon = jnp.exp(total[:, :128] * SCALE)
            probs = expon / jnp.sum(expon, -1, keepdims=True)
            slopes = total[:, 128:]
            mixed = SCALE * probs * (slopes - jnp.sum(probs * slopes, -1, keepdims=True))
            pm[rows, 0:128] = probs.astype(BF16)
            pm[rows, 128:256] = mixed.astype(BF16)
            out = []
            for s in range(8):
                if s != place:
                    copy = remote(pm.at[rows, :], pm.at[rows, :], sq_s.at[s], sq_r.at[o], over_z(s))
                    copy.start()
                    out.append(copy)
            for copy in out:
                copy.wait_send()

    turn(1)
    for o, place in enumerate(OWNERS):
        rows = pl.ds(pl.multiple_of(48 * e + 16 * o, 16), 16)

        @pl.when(ze != place)
        def _():
            remote(pm.at[rows, :], pm.at[rows, :], sq_s.at[0], sq_r.at[o], over_z(place)).wait_recv()

    def chunk(ee):
        return pm.at[pl.ds(pl.multiple_of(48 * ee, 16), 48), :]

    for d in range(1, 8):
        copy = remote(chunk(e), chunk(e), sp_s.at[d], sp_r.at[d], over_e(ahead(e, d)))
        copy.start()
        sends.append(copy)
    keeps = jnp.concatenate([jnp.broadcast_to(cover(k), (READS, 128)) for k in range(4)], axis=1)
    from_core(1)
    from_far(1)
    for half in range(2):
        rows = to_columns[half * 256 : (half + 1) * 256, :]
        gp[2 * half : 2 * half + 2] = nn(rows, fg[1].reshape(512, D)).astype(BF16).reshape(2, READS, D)
    for d in range(1, 8):
        ee = behind(e, d)
        remote(chunk(ee), chunk(ee), sp_s.at[d], sp_r.at[d], over_e(ee)).wait_recv()

    eye = hot(ro == co)
    made = []
    for h, (t, _) in enumerate(plan):
        probs_b = pm[h * 128 : (h + 1) * 128, 0:128]
        mixed = pm[h * 128 : (h + 1) * 128, 128:256]
        made.append(
            (
                nn(mixed, heads[1, t]),
                nn(nt(eye, mixed).astype(BF16), heads[0, t]),
                nn(nt(eye, probs_b).astype(BF16), heads[3, t]),
                nn(probs_b, heads[2, t]),
            )
        )
    def lanes(v, k):
        return v[:, k * 128 : (k + 1) * 128]

    spare = []
    for j in range(4):
        tile0 = made[0][j] * high + made[2][j] * (low * (1.0 - par_f))
        tile1 = made[1][j] * low + made[2][j] * (high * par_f)
        if j < 3:
            tile0, tile1 = tile0 * keeps, tile1 * keeps
            full = (tile0 * (1.0 - par_f) + tile1 * par_f).astype(BF16)
            spare.append(tile1 * (1.0 - par_f) + tile0 * par_f)
        for k in range(4):
            for t, tile in ((0, tile0), (1, tile1)):
                if j < 3:
                    gr[j, k, :, t * 128 : (t + 1) * 128] = lanes(tile, k).astype(BF16)
                else:
                    ob[k, :, t * 128 : (t + 1) * 128] = lanes(tile, k).astype(BF16)
            if j < 3:
                gpk[k, :, j * 128 : (j + 1) * 128] = lanes(full, k)
    for k in range(4):
        gpk[k, :, 384:512] = (lanes(spare[0], k) + pltpu.roll(lanes(spare[1], k), 64, axis=1)).astype(BF16)
        gpk[k, :, 512:640] = lanes(spare[2], k).astype(BF16)

    def rows_of(mm):
        return pl.ds(pl.multiple_of(32 * mm, 32), 32)

    for d, mm in ((1, side_m), (2, far_m), (3, core_m)):
        copy = remote(gr.at[:, :, rows_of(mm), :], rg.at[m], sg_s.at[d], sg_r.at[d], mate(mm))
        copy.start()
        sends.append(copy)
    rg[m] = gr[:, :, rows_of(m), :]

    def left_parts(p):
        first_lane, count = PARTS[p]
        right = gpk[:, :, first_lane : first_lane + count].reshape(512, count)
        for half in range(2):
            part = nn(nbt[half * 384 : (half + 1) * 384, :], right).astype(BF16)
            for q in range(4):
                wa[p][(half * 4 + q + 1) % 8] = part[q * 96 : (q + 1) * 96, :]
            for q in range(4):
                d = (half * 4 + q + 1) % 8
                if d > 0:
                    copy = remote(wa[p].at[d], ra[p].at[d], sd_s.at[p, d], sd_r.at[p, d], over_e(ahead(e, d)))
                    copy.start()
                    sends.append(copy)

    left_parts(0)
    left_parts(1)
    ow, cw = iota((256, 256), 0), iota((256, 256), 1)
    u, zz = ow & 31, ((ow >> 5) + ze) & 7
    xi2, xx, yy = (zz >> 1) & 1, u & 1, (u >> 1) & 3
    local = 64 * par + (xi2 + xx * (3 - 2 * xi2)) * 48 + (zz & 1) * 24 + yy * 6 + (zz >> 2) * 3 + (u >> 3)
    obt[...] = nt(hot(jnp.where(u < 24, local, -1) == cw), ob[...].reshape(512, WIN)).astype(BF16)
    wb[...] = nn(obt[...], gp[...].reshape(512, D)).astype(BF16).reshape(8, 32, D)
    for d in range(1, 8):
        copy = remote(wb.at[d], rb.at[d], sb_s.at[d], sb_r.at[d], over_z(ahead(ze, d)))
        copy.start()
        sends.append(copy)

    def second_parts(p):
        count = PARTS[p][1]
        total = wa[p][0].astype(F32)
        for d in range(1, 8):
            remote(ra[p].at[d], ra[p].at[d], sd_s.at[p, d], sd_r.at[p, d], over_e(behind(e, d))).wait_recv()
            total = total + ra[p][d].astype(F32)
        ra_row, ra_col = iota((128, 96), 0), iota((128, 96), 1)
        v, zz = ra_row & 15, ((ra_row >> 4) + ze) & 7
        src = jnp.where(v < 12, (v >> 2) * 32 + (zz & 3) * 8 + (zz >> 2) * 4 + (v & 3), -1)
        za[p][...] = nn(hot(ra_col == src), total.astype(BF16)).astype(BF16).reshape(8, 16, count)
        for d in range(1, 8):
            copy = remote(za[p].at[d], rza[p].at[d], se_s.at[p, d], se_r.at[p, d], over_z(ahead(ze, d)))
            copy.start()
            sends.append(copy)

    for copy in full_copies:
        copy.wait()
    grad_norm = jnp.zeros((128, D), F32)
    for d, mm in ((0, m), (3, core_m), (1, side_m), (2, far_m)):
        if d > 0:
            remote(gr.at[:, :, rows_of(mm), :], rg.at[mm], sg_s.at[d], sg_r.at[d], mate(mm)).wait_recv()
        lane = pl.multiple_of(128 * lax.div(3 * mm, 2), 128)
        for j in range(3):
            grad_norm = grad_norm + nt(rg[mm, j].reshape(128, WIN), wv[j, :, pl.ds(lane, WIN)])
    own_feat = mine[...].astype(F32)
    inverse = lax.rsqrt(jnp.mean(own_feat * own_feat, -1, keepdims=True) + EPS)
    normed = own_feat * inverse
    result = (inverse * (grad_norm - normed * jnp.mean(grad_norm * normed, -1, keepdims=True))).astype(BF16)
    to_sources = hot(co == (ro & 3) * 32 + (ro >> 2))
    gi[...] = nn(to_sources, result).astype(BF16).reshape(8, 16, D)
    for d in FAR + NEAR:
        gg = twin(d)
        copy = remote(gi.at[gg], ogi.at[g], si_s.at[d], si_r.at[d], over_g(gg))
        copy.start()
        sends.append(copy)
    ogi[g] = gi[g]

    second_parts(0)
    total = wb[0].astype(F32)
    for d in range(1, 8):
        remote(rb.at[d], rb.at[d], sb_s.at[d], sb_r.at[d], over_z(behind(ze, d))).wait_recv()
        total = total + rb[d].astype(F32)
    rb_row, rb_col = iota((128, 32), 0), iota((128, 32), 1)
    v = rb_row & 15
    src = jnp.where(v < 3, v * 8 + (((rb_row >> 4) + e) & 7), -1)
    yb[...] = nn(hot(rb_col == src), total.astype(BF16)).astype(BF16).reshape(8, 16, D)
    for d in range(1, 8):
        copy = remote(yb.at[d], ryb.at[d], sy_s.at[d], sy_r.at[d], over_e(ahead(e, d)))
        copy.start()
        sends.append(copy)

    second_parts(1)

    for d in range(1, 8):
        slot = ogi.at[twin(d)]
        remote(slot, slot, si_s.at[d], si_r.at[d], over_g(twin(d))).wait_recv()
    from_groups = hot(co == ((ro >> 2) & 7) * 16 + (ro >> 5) * 4 + (ro & 3))
    gin[...] = nn(from_groups, ogi[...].reshape(128, D)).astype(BF16).reshape(4, 32, D)

    total = yb[0].astype(F32)
    for d in range(1, 8):
        remote(ryb.at[d], ryb.at[d], sy_s.at[d], sy_r.at[d], over_e(behind(e, d))).wait_recv()
        total = total + ryb[d].astype(F32)
    f3[...] = total[0:8, :]
    last = remote(f3, r3, s3_s.at[0], s3_r.at[0], turned)

    @pl.when(zl != m)
    def _():
        last.start()

    @pl.when(zl == m)
    def _():
        r3[...] = f3[...]

    for p, (lane, count) in enumerate(PARTS):
        total = za[p][0].astype(F32)
        for d in range(1, 8):
            remote(rza[p].at[d], rza[p].at[d], se_s.at[p, d], se_r.at[p, d], over_z(behind(ze, d))).wait_recv()
            total = total + rza[p][d].astype(F32)
        for mm in range(4):
            for t in range(3):
                fd[mm, t : t + 1, lane : lane + count] = total[t * 4 + mm : t * 4 + mm + 1, :]
            fd[mm, 3:8, lane : lane + count] = jnp.zeros((5, count), F32)
    for d, mm in ((1, side_m), (2, far_m), (3, core_m)):
        copy = remote(fd.at[mm], rj.at[m], sj_s.at[d], sj_r.at[d], mate(mm))
        copy.start()
        sends.append(copy)
    rj[m] = fd[m]

    @pl.when(zl != m)
    def _():
        last.wait()

    for d, mm in ((1, side_m), (2, far_m), (3, core_m)):
        remote(fd.at[mm], rj.at[mm], sj_s.at[d], sj_r.at[d], mate(mm)).wait_recv()
    for j in range(3):
        tiles = [jnp.zeros((3, 128), F32)] * 6
        for mm in range(4):
            side = (low, high)[mm % 2][:, :128]
            full = rj[mm, :, j * 128 : (j + 1) * 128]
            rest = rj[mm, :, (512 if j == 2 else 384) : (640 if j == 2 else 512)]
            if j == 1:
                rest = pltpu.roll(rest, 64, axis=1)
            pair = (full, rest * side) if mm % 2 == 0 else (rest * side, full)
            for at in range(2):
                tiles[(3 * mm) // 2 + at] = tiles[(3 * mm) // 2 + at] + pair[at][0:3]
        for tile in range(6):
            wsum[:, j * D + tile * 128 : j * D + (tile + 1) * 128] = tiles[tile]
    wsum[:, 3 * D : 4 * D] = r3[0:3, :]

    for copy in sends:
        copy.wait_send()
    for place, copy in late:

        @pl.when(ze != place)
        def _():
            copy.wait_send()


def hand_over(gin, wgrad, gin_out, wgrad_out, sem):
    copies = [pltpu.make_async_copy(gin, gin_out, sem.at[0]), pltpu.make_async_copy(wgrad, wgrad_out, sem.at[1])]
    for copy in copies:
        copy.start()
    for copy in copies:
        copy.wait()


def shards(features, grad_out, weights, read_start, read_end):
    hbm = pl.BlockSpec(memory_space=pl.ANY)
    vm = pl.BlockSpec(memory_space=pltpu.VMEM)
    dma = pltpu.SemaphoreType.DMA
    results = pl.pallas_call(
        kernel,
        name="tied_rows",
        out_shape=(
            pltpu.VMEM((4, 32, D), BF16),
            pltpu.VMEM((3, 4 * D), F32),
        ),
        in_specs=[hbm] * 5,
        out_specs=(vm, vm),
        scratch_shapes=[
            pltpu.VMEM((4, 32, D), BF16),
            pltpu.VMEM((4, 32, D), BF16),
            pltpu.VMEM((1, READS), I32),
            pltpu.VMEM((1, READS), I32),
            pltpu.VMEM((3, D, D), BF16),
            pltpu.VMEM((3, D, WIN), BF16),
            pltpu.VMEM((D, D), BF16),
            pltpu.VMEM((3, 8, 16, D), BF16),
            pltpu.VMEM((2, 4, 8, 16, D), BF16),
            pltpu.VMEM((512, 512), BF16),
            pltpu.VMEM((8, 16, D), BF16),
            pltpu.VMEM((4, 8, 16, WIN), BF16),
            pltpu.VMEM((3, 4, READS, WIN), BF16),
            pltpu.VMEM((4, READS, D), BF16),
            pltpu.VMEM((READS, D), BF16),
            pltpu.VMEM((4, READS, D), BF16),
            pltpu.VMEM((4, READS, D), BF16),
            pltpu.VMEM((4, 2, READS, 512), BF16),
            pltpu.VMEM((2, 384, 128), F32),
            pltpu.VMEM((2, 8, 48, 128), F32),
            pltpu.VMEM((48, 256), F32),
            pltpu.VMEM((8, 16, 256), F32),
            pltpu.VMEM((384, 256), BF16),
            pltpu.VMEM((3, 4, READS, WIN), BF16),
            pltpu.VMEM((4, READS, PACK), BF16),
            pltpu.VMEM((4, READS, WIN), BF16),
            pltpu.VMEM((4, 3, 4, 32, WIN), BF16),
            pltpu.VMEM((D, 512), BF16),
            pltpu.VMEM((WIN, 512), BF16),
            pltpu.VMEM((8, 96, PARTS[0][1]), BF16),
            pltpu.VMEM((8, 96, PARTS[1][1]), BF16),
            pltpu.VMEM((8, 96, PARTS[0][1]), BF16),
            pltpu.VMEM((8, 96, PARTS[1][1]), BF16),
            pltpu.VMEM((8, 32, D), BF16),
            pltpu.VMEM((8, 32, D), BF16),
            pltpu.VMEM((8, 16, PARTS[0][1]), BF16),
            pltpu.VMEM((8, 16, PARTS[1][1]), BF16),
            pltpu.VMEM((8, 16, PARTS[0][1]), BF16),
            pltpu.VMEM((8, 16, PARTS[1][1]), BF16),
            pltpu.VMEM((8, 16, D), BF16),
            pltpu.VMEM((8, 16, D), BF16),
            pltpu.VMEM((4, 8, PACK), F32),
            pltpu.VMEM((4, 8, PACK), F32),
            pltpu.VMEM((8, D), F32),
            pltpu.VMEM((8, D), F32),
            pltpu.VMEM((8, 16, D), BF16),
            pltpu.VMEM((8, 16, D), BF16),
            dma((4,)), dma((7,)),
            dma((3, 8)), dma((3, 8)), dma((2, 4)), dma((2, 4)),
            dma((2, 2)), dma((2, 2)), dma((2, 2)), dma((2, 2)), dma((2, 2)), dma((2, 2)),
            dma((2, 8)), dma((2, 8)),
            dma((3,)), dma((8,)),
            dma((8,)), dma((3,)),
            dma((8,)), dma((8,)),
            dma((4,)), dma((4,)),
            dma((2, 8)), dma((2, 8)),
            dma((2, 8)), dma((2, 8)),
            dma((8,)), dma((8,)),
            dma((8,)), dma((8,)),
            dma((4,)), dma((4,)),
            dma((1,)), dma((1,)),
            dma((8,)), dma((8,)),
        ],
        compiler_params=pltpu.CompilerParams(
            collective_id=0, has_side_effects=True, vmem_limit_bytes=56 * 1024 * 1024
        ),
    )(features, grad_out, read_start.reshape(1, READS), read_end.reshape(1, READS), weights)
    return pl.pallas_call(
        hand_over,
        name="hand_over",
        out_shape=tuple(jax.ShapeDtypeStruct(r.shape, r.dtype) for r in results),
        in_specs=[vm, vm],
        out_specs=(hbm, hbm),
        scratch_shapes=[dma((2,))],
        compiler_params=pltpu.CompilerParams(vmem_limit_bytes=4 * 1024 * 1024),
    )(*results)


def solution(mesh):
    in_specs = (P("read", "pos", None), P("read", "pos", None), P(), P(), P())
    out_specs = (P("read", "pos", None), P(("read", "pos"), None))
    return jax.shard_map(shards, mesh=mesh, in_specs=in_specs, out_specs=out_specs, check_vma=False)
```

```python
import math

import jax
import jax.numpy as jnp
from jax import lax
from jax.experimental import pallas as pl
from jax.experimental.pallas import tpu as pltpu
from jax.sharding import PartitionSpec as P

F32, BF16, I32 = jnp.float32, jnp.bfloat16, jnp.int32
D = 768
WIN = 256
PARTS = ((0, 384), (384, 256))
PACK = 640
READS = 128
SCALE = 1.0 / 128.0
EPS = 1e-05
OWNERS = (0, 3, 5)


def nt(a, b):
    return lax.dot_general(a, b, (((1,), (1,)), ((), ())), preferred_element_type=F32)


def nn(a, b):
    return jnp.dot(a, b, preferred_element_type=F32)


def iota(shape, dim):
    return lax.broadcasted_iota(I32, shape, dim)


def hot(cond):
    return jnp.where(cond, 1.0, 0.0).astype(BF16)


def read_of(g, m):
    zl, xp = lax.div(g, 2), lax.rem(g, 2)
    xi, c = lax.div(m, 2), lax.rem(m, 2)
    return zl * 8 + (xi + xp * (3 - 2 * xi)) * 2 + c


def kernel(
    feat_hbm, gout_hbm, starts_hbm, ends_hbm, w_hbm, gin, wsum,
    feat, gout, starts, ends, wv, ww, w3, a_buf, fg, to_columns, bg, bx, qa, na, mine, gp, nb, heads, lbuf, rl, acc, rz, pm,
    gr, gpk, ob, rg, nbt, obt, wa0, wa1, ra0, ra1, wb, rb, za0, za1, rza0, rza1, yb, ryb, fd, rj, f3, r3, gi, ogi,
    s_in, s_w, sa_s, sa_r, sh_s, sh_r, sc_s, sc_r, sx_s, sx_r, sf_s, sf_r, sl_s, sl_r, sz_s, sz_r,
    sq_s, sq_r, sp_s, sp_r, sg_s, sg_r, sd_s, sd_r, se_s, se_r, sb_s, sb_r, sy_s, sy_r, sj_s, sj_r, s3_s, s3_r, si_s, si_r,
):
    ri, pi = lax.axis_index("read"), lax.axis_index("pos")
    zl, x, c = lax.div(ri, 8), lax.rem(lax.div(ri, 2), 4), lax.rem(ri, 2)
    xp = lax.div(x, 2)
    xi = x + xp * (3 - 2 * x)
    y, zh = lax.div(pi, 2), lax.rem(pi, 2)
    g, m = zl * 2 + xp, xi * 2 + c
    e, ze = y * 2 + xp, zh * 4 + zl
    par = lax.rem(m, 2)
    off = pl.multiple_of(128 * lax.div(3 * m, 2), 128)
    core_m = xi * 2 + (1 - c)
    side_m = (1 - xi) * 2 + c
    far_m = (1 - xi) * 2 + (1 - c)

    def remote(src, dst, ss, rs, dev):
        return pltpu.make_async_remote_copy(
            src_ref=src, dst_ref=dst, send_sem=ss, recv_sem=rs,
            device_id=dev, device_id_type=pl.DeviceIdType.MESH,
        )

    def mate(mm):
        return (read_of(g, mm), pi)

    def over_g(gg):
        return (read_of(gg, m), pi)

    def over_e(ee):
        return (read_of(zl * 2 + lax.rem(ee, 2), m), lax.div(ee, 2) * 2 + zh)

    def over_z(zz):
        return (read_of(lax.rem(zz, 4) * 2 + xp, m), y * 2 + lax.div(zz, 4))

    def ahead(v, d):
        return lax.rem(v + d, 8)

    def behind(v, d):
        return lax.rem(v + 8 - d, 8)

    z1, z0 = lax.div(zl, 2), lax.rem(zl, 2)

    def twin(d):
        a, b, q = z1, z0, xp
        a = 1 - a if d & 4 else a
        b = 1 - b if d & 2 else b
        q = 1 - q if d & 1 else q
        return a * 4 + b * 2 + q

    NEAR, FAR = (1, 2, 3), (4, 5, 6, 7)

    def side_of(ref, far):
        return ref.at[pl.ds((1 - z1 if far else z1) * 4, 4)]

    turned = (read_of(m * 2 + xp, zl), pi)
    sends = []
    wa, ra, za, rza = (wa0, wa1), (ra0, ra1), (za0, za1), (rza0, rza1)

    in_copies = [
        pltpu.make_async_copy(src, dst, s_in.at[i])
        for i, (src, dst) in enumerate(
            ((feat_hbm, feat), (gout_hbm, gout), (starts_hbm, starts), (ends_hbm, ends))
        )
    ]
    for copy in in_copies:
        copy.start()

    barrier = pltpu.get_barrier_semaphore()

    def greet(dev):
        pl.semaphore_signal(barrier, inc=1, device_id=dev, device_id_type=pl.DeviceIdType.MESH)

    for d in range(1, 8):
        greet(over_g(twin(d)))
        greet(over_e(ahead(e, d)))
        greet(over_z(ahead(ze, d)))
    for mm in (core_m, side_m, far_m):
        greet(mate(mm))

    @pl.when(zl != m)
    def _():
        greet(turned)

    win_copies = [
        pltpu.make_async_copy(w_hbm.at[j, :, pl.ds(off, WIN)], ww.at[j], s_w.at[j]) for j in range(3)
    ]
    w3_copy = pltpu.make_async_copy(w_hbm.at[3], w3, s_w.at[3])
    full_copies = [pltpu.make_async_copy(w_hbm.at[j], wv.at[j], s_w.at[4 + j]) for j in range(3)]
    for copy in [w3_copy] + win_copies + full_copies:
        copy.start()

    ro, co = iota((128, 128), 0), iota((128, 128), 1)
    to_groups = hot(co == ((ro >> 2) & 3) * 32 + (ro >> 4) * 4 + (ro & 3))
    def by_group(ref):
        return nn(to_groups, ref[...].reshape(128, D)).astype(BF16)

    def spread(i, dst):
        dst[g] = a_buf[i, g]
        for d in FAR + NEAR:
            gg = twin(d)
            copy = remote(a_buf.at[i, gg], dst.at[g], sa_s.at[i, d], sa_r.at[i, d], over_g(gg))
            copy.start()
            sends.append(copy)

    def gathered(i, dst, far):
        for d in FAR if far else NEAR:
            slot = dst.at[twin(d)]
            remote(slot, slot, sa_s.at[i, d], sa_r.at[i, d], over_g(twin(d))).wait_recv()

    in_copies[0].wait()
    a_buf[0] = by_group(feat).reshape(8, 16, D)

    @pl.when(zl == m)
    def _():
        pl.semaphore_wait(barrier, 24)

    @pl.when(zl != m)
    def _():
        pl.semaphore_wait(barrier, 25)

    spread(0, fg.at[0, m])
    in_copies[1].wait()
    local_grad = by_group(gout)
    a_buf[1] = local_grad.reshape(8, 16, D)
    w3_copy.wait()
    a_buf[2] = nt(local_grad, w3[...]).astype(BF16).reshape(8, 16, D)
    spread(2, bg)

    def first(t, far):
        gathered(t, fg.at[t, m], far)
        slot = side_of(fg.at[t, m], far)
        for ss, rs, mm in ((sx_s, sx_r, side_m), (sc_s, sc_r, core_m)):
            copy = remote(slot, slot, ss.at[t, far], rs.at[t, far], mate(mm))
            copy.start()
            sends.append(copy)

    def second(t, far):
        slot = side_of(fg.at[t, side_m], far)
        remote(slot, slot, sx_s.at[t, far], sx_r.at[t, far], mate(side_m)).wait_recv()
        copy = remote(slot, slot, sf_s.at[t, far], sf_r.at[t, far], mate(core_m))
        copy.start()
        sends.append(copy)

    def from_core(t):
        for far in (0, 1):
            slot = side_of(fg.at[t, core_m], far)
            remote(slot, slot, sc_s.at[t, far], sc_r.at[t, far], mate(core_m)).wait_recv()

    def from_far(t):
        for far in (0, 1):
            slot = side_of(fg.at[t, far_m], far)
            remote(slot, slot, sf_s.at[t, far], sf_r.at[t, far], mate(core_m)).wait_recv()

    def project(mm):
        f32 = fg[0, mm].reshape(128, D).astype(F32)
        inverse = lax.rsqrt(jnp.mean(f32 * f32, -1, keepdims=True) + EPS)
        normed_b = (f32 * inverse).astype(BF16)
        na[mm] = normed_b
        for j in range(3):
            qa[j, mm] = nn(normed_b, ww[j]).astype(BF16)

    for k in range(4):
        pr, pc = iota((READS, 512), 0), iota((READS, 512), 1)
        to_columns[k * 128 : (k + 1) * 128, :] = hot(pc == pr * 4 + k)
    first(0, 0)
    for copy in in_copies[2:] + win_copies:
        copy.wait()
    first(0, 1)
    second(0, 0)
    project(m)
    from_core(0)
    project(core_m)

    def window(mm, far):
        lane = pl.multiple_of(128 * lax.div(3 * mm, 2), 128)
        return side_of(bg, far).at[:, :, pl.ds(lane, WIN)]

    def trade(far):
        gathered(2, bg, far)
        for d, mm in ((1, side_m), (2, far_m), (3, core_m)):
            copy = remote(window(mm, far), side_of(bx.at[m], far), sh_s.at[far, d], sh_r.at[far, d], mate(mm))
            copy.start()
            sends.append(copy)

    trade(0)
    second(0, 1)
    trade(1)
    spread(1, fg.at[1, m])
    nat = iota((READS, READS), 0)
    gs_v, ms_v, r_v = (nat >> 2) & 7, nat >> 5, nat & 3
    xi_v, xp_v = ms_v >> 1, gs_v & 1
    nat = 4 * ((gs_v >> 1) * 8 + (xi_v + xp_v * (3 - 2 * xi_v)) * 2 + (ms_v & 1)) + r_v
    pick = iota((READS, READS), 1) == nat
    begin = jnp.sum(jnp.where(pick, starts[...].astype(F32), 0.0), axis=1, keepdims=True)
    close = jnp.sum(jnp.where(pick, ends[...].astype(F32), 0.0), axis=1, keepdims=True)

    def cover(k):
        col = (32 * pi + 4 * g + k).astype(F32)
        return jnp.where(col >= begin, 1.0, 0.0) * jnp.where(col < close, 1.0, 0.0)

    project(side_m)
    bx[m] = bg[:, :, pl.ds(off, WIN)]
    def set_heads(j, part):
        for k in range(4):
            for t in range(2):
                heads[j, t, :, k * 128 : (k + 1) * 128] = part[k * 128 : (k + 1) * 128, t * 128 : (t + 1) * 128]

    keep = jnp.concatenate([cover(k) for k in range(4)], axis=0)
    from_far(0)
    project(far_m)
    for j in range(3):
        set_heads(j, (nn(to_columns[...], qa[j].reshape(512, WIN)) * keep).astype(BF16))

    low = jnp.where((iota((1, 512), 1) & 127) < 64, 1.0, 0.0)
    high = 1.0 - low
    par_f = par.astype(F32)
    own = low * (1.0 - par_f) + high * par_f
    plan = ((0, high), (1, low), (par, own))

    def scores(which, left, right):
        for h, (t, mask) in enumerate(plan):
            lbuf[which, h * 128 : (h + 1) * 128, :] = nt(heads[left, t] * mask.astype(BF16), heads[right, t])
        for d in range(1, 8):
            ee = ahead(e, d)
            copy = remote(
                lbuf.at[which, pl.ds(pl.multiple_of(48 * ee, 16), 48), :], rl.at[which, d],
                sl_s.at[which, d], sl_r.at[which, d], over_e(ee),
            )
            copy.start()
            sends.append(copy)

    scores(0, 0, 1)
    for far in (0, 1):
        for d, mm in ((1, side_m), (2, far_m), (3, core_m)):
            slot = side_of(bx.at[mm], far)
            remote(slot, slot, sh_s.at[far, d], sh_r.at[far, d], mate(mm)).wait_recv()
    set_heads(3, nn(to_columns[...], bx[...].reshape(512, WIN)).astype(BF16))
    scores(1, 3, 2)

    first(1, 0)
    for half in range(2):
        rows = to_columns[half * 256 : (half + 1) * 256, :]
        nb[2 * half : 2 * half + 2] = nn(rows, na[...].reshape(512, D)).astype(BF16).reshape(2, READS, D)
    mine[...] = nn(hot(co == (ro & 31) * 4 + (ro >> 5)), fg[0, m].reshape(128, D)).astype(BF16)

    first(1, 1)

    def turn(half):
        w, col = iota((96, D), 0), iota((96, D), 1)
        xi2 = (w >> 1) & 1
        picks = []
        for q in range(4):
            ee = ahead(e, half * 4 + q + 1)
            yy, xx = lax.div(ee, 2), lax.rem(ee, 2)
            row = (
                ((w >> 3) & 3) * 192 + (xi2 + xx * (3 - 2 * xi2)) * 48 + (w & 1) * 24
                + yy * 6 + ((w >> 2) & 1) * 3 + (w >> 5)
            )
            picks.append(hot(col == row))
        pick = jnp.concatenate(picks, axis=0)
        nbt[half * 384 : (half + 1) * 384, :] = nt(pick, nb[...].reshape(512, D)).astype(BF16)

    for which in range(2):
        total = lbuf[which, pl.ds(pl.multiple_of(48 * e, 16), 48), :]
        for d in range(1, 8):
            remote(
                rl.at[which, d], rl.at[which, d], sl_s.at[which, d], sl_r.at[which, d], over_e(behind(e, d))
            ).wait_recv()
            total = total + rl[which, d]
        acc[:, which * 128 : (which + 1) * 128] = total

    late = []
    for o, place in enumerate(OWNERS):
        dev = over_z(place)
        copy = remote(acc.at[pl.ds(16 * o, 16), :], rz.at[ze], sz_s.at[o], sz_r.at[ze], dev)

        @pl.when(ze != place)
        def _():
            copy.start()

        late.append((place, copy))

    second(1, 0)
    second(1, 1)
    turn(0)
    for o, place in enumerate(OWNERS):
        rows = pl.ds(pl.multiple_of(48 * e + 16 * o, 16), 16)

        @pl.when(ze == place)
        def _():
            total = acc[16 * o : 16 * o + 16, :]
            for s in range(8):
                if s != place:
                    remote(rz.at[s], rz.at[s], sz_s.at[o], sz_r.at[s], over_z(s)).wait_recv()
                    total = total + rz[s]
            expon = jnp.exp(total[:, :128] * SCALE)
            probs = expon / jnp.sum(expon, -1, keepdims=True)
            slopes = total[:, 128:]
            mixed = SCALE * probs * (slopes - jnp.sum(probs * slopes, -1, keepdims=True))
            pm[rows, 0:128] = probs.astype(BF16)
            pm[rows, 128:256] = mixed.astype(BF16)
            out = []
            for s in range(8):
                if s != place:
                    copy = remote(pm.at[rows, :], pm.at[rows, :], sq_s.at[s], sq_r.at[o], over_z(s))
                    copy.start()
                    out.append(copy)
            for copy in out:
                copy.wait_send()

    turn(1)
    for o, place in enumerate(OWNERS):
        rows = pl.ds(pl.multiple_of(48 * e + 16 * o, 16), 16)

        @pl.when(ze != place)
        def _():
            remote(pm.at[rows, :], pm.at[rows, :], sq_s.at[0], sq_r.at[o], over_z(place)).wait_recv()

    def chunk(ee):
        return pm.at[pl.ds(pl.multiple_of(48 * ee, 16), 48), :]

    for d in range(1, 8):
        copy = remote(chunk(e), chunk(e), sp_s.at[d], sp_r.at[d], over_e(ahead(e, d)))
        copy.start()
        sends.append(copy)
    keeps = jnp.concatenate([jnp.broadcast_to(cover(k), (READS, 128)) for k in range(4)], axis=1)
    from_core(1)
    from_far(1)
    for half in range(2):
        rows = to_columns[half * 256 : (half + 1) * 256, :]
        gp[2 * half : 2 * half + 2] = nn(rows, fg[1].reshape(512, D)).astype(BF16).reshape(2, READS, D)
    for d in range(1, 8):
        ee = behind(e, d)
        remote(chunk(ee), chunk(ee), sp_s.at[d], sp_r.at[d], over_e(ee)).wait_recv()

    eye = hot(ro == co)
    made = []
    for h, (t, _) in enumerate(plan):
        probs_b = pm[h * 128 : (h + 1) * 128, 0:128]
        mixed = pm[h * 128 : (h + 1) * 128, 128:256]
        made.append(
            (
                nn(mixed, heads[1, t]),
                nn(nt(eye, mixed).astype(BF16), heads[0, t]),
                nn(nt(eye, probs_b).astype(BF16), heads[3, t]),
                nn(probs_b, heads[2, t]),
            )
        )
    def lanes(v, k):
        return v[:, k * 128 : (k + 1) * 128]

    spare = []
    for j in range(4):
        tile0 = made[0][j] * high + made[2][j] * (low * (1.0 - par_f))
        tile1 = made[1][j] * low + made[2][j] * (high * par_f)
        if j < 3:
            tile0, tile1 = tile0 * keeps, tile1 * keeps
            full = (tile0 * (1.0 - par_f) + tile1 * par_f).astype(BF16)
            spare.append(tile1 * (1.0 - par_f) + tile0 * par_f)
        for k in range(4):
            for t, tile in ((0, tile0), (1, tile1)):
                if j < 3:
                    gr[j, k, :, t * 128 : (t + 1) * 128] = lanes(tile, k).astype(BF16)
                else:
                    ob[k, :, t * 128 : (t + 1) * 128] = lanes(tile, k).astype(BF16)
            if j < 3:
                gpk[k, :, j * 128 : (j + 1) * 128] = lanes(full, k)
    for k in range(4):
        gpk[k, :, 384:512] = (lanes(spare[0], k) + pltpu.roll(lanes(spare[1], k), 64, axis=1)).astype(BF16)
        gpk[k, :, 512:640] = lanes(spare[2], k).astype(BF16)

    def rows_of(mm):
        return pl.ds(pl.multiple_of(32 * mm, 32), 32)

    for d, mm in ((1, side_m), (2, far_m), (3, core_m)):
        copy = remote(gr.at[:, :, rows_of(mm), :], rg.at[m], sg_s.at[d], sg_r.at[d], mate(mm))
        copy.start()
        sends.append(copy)
    rg[m] = gr[:, :, rows_of(m), :]

    def left_parts(p):
        first_lane, count = PARTS[p]
        right = gpk[:, :, first_lane : first_lane + count].reshape(512, count)
        for half in range(2):
            part = nn(nbt[half * 384 : (half + 1) * 384, :], right).astype(BF16)
            for q in range(4):
                wa[p][(half * 4 + q + 1) % 8] = part[q * 96 : (q + 1) * 96, :]
            for q in range(4):
                d = (half * 4 + q + 1) % 8
                if d > 0:
                    copy = remote(wa[p].at[d], ra[p].at[d], sd_s.at[p, d], sd_r.at[p, d], over_e(ahead(e, d)))
                    copy.start()
                    sends.append(copy)

    left_parts(0)
    left_parts(1)
    ow, cw = iota((256, 256), 0), iota((256, 256), 1)
    u, zz = ow & 31, ((ow >> 5) + ze) & 7
    xi2, xx, yy = (zz >> 1) & 1, u & 1, (u >> 1) & 3
    local = 64 * par + (xi2 + xx * (3 - 2 * xi2)) * 48 + (zz & 1) * 24 + yy * 6 + (zz >> 2) * 3 + (u >> 3)
    obt[...] = nt(hot(jnp.where(u < 24, local, -1) == cw), ob[...].reshape(512, WIN)).astype(BF16)
    wb[...] = nn(obt[...], gp[...].reshape(512, D)).astype(BF16).reshape(8, 32, D)
    for d in range(1, 8):
        copy = remote(wb.at[d], rb.at[d], sb_s.at[d], sb_r.at[d], over_z(ahead(ze, d)))
        copy.start()
        sends.append(copy)

    def second_parts(p):
        count = PARTS[p][1]
        total = wa[p][0].astype(F32)
        for d in range(1, 8):
            remote(ra[p].at[d], ra[p].at[d], sd_s.at[p, d], sd_r.at[p, d], over_e(behind(e, d))).wait_recv()
            total = total + ra[p][d].astype(F32)
        ra_row, ra_col = iota((128, 96), 0), iota((128, 96), 1)
        v, zz = ra_row & 15, ((ra_row >> 4) + ze) & 7
        src = jnp.where(v < 12, (v >> 2) * 32 + (zz & 3) * 8 + (zz >> 2) * 4 + (v & 3), -1)
        za[p][...] = nn(hot(ra_col == src), total.astype(BF16)).astype(BF16).reshape(8, 16, count)
        for d in range(1, 8):
            copy = remote(za[p].at[d], rza[p].at[d], se_s.at[p, d], se_r.at[p, d], over_z(ahead(ze, d)))
            copy.start()
            sends.append(copy)

    for copy in full_copies:
        copy.wait()
    grad_norm = jnp.zeros((128, D), F32)
    for d, mm in ((0, m), (3, core_m), (1, side_m), (2, far_m)):
        if d > 0:
            remote(gr.at[:, :, rows_of(mm), :], rg.at[mm], sg_s.at[d], sg_r.at[d], mate(mm)).wait_recv()
        lane = pl.multiple_of(128 * lax.div(3 * mm, 2), 128)
        for j in range(3):
            grad_norm = grad_norm + nt(rg[mm, j].reshape(128, WIN), wv[j, :, pl.ds(lane, WIN)])
    own_feat = mine[...].astype(F32)
    inverse = lax.rsqrt(jnp.mean(own_feat * own_feat, -1, keepdims=True) + EPS)
    normed = own_feat * inverse
    result = (inverse * (grad_norm - normed * jnp.mean(grad_norm * normed, -1, keepdims=True))).astype(BF16)
    to_sources = hot(co == (ro & 3) * 32 + (ro >> 2))
    gi[...] = nn(to_sources, result).astype(BF16).reshape(8, 16, D)
    for d in FAR + NEAR:
        gg = twin(d)
        copy = remote(gi.at[gg], ogi.at[g], si_s.at[d], si_r.at[d], over_g(gg))
        copy.start()
        sends.append(copy)
    ogi[g] = gi[g]

    second_parts(0)
    total = wb[0].astype(F32)
    for d in range(1, 8):
        remote(rb.at[d], rb.at[d], sb_s.at[d], sb_r.at[d], over_z(behind(ze, d))).wait_recv()
        total = total + rb[d].astype(F32)
    rb_row, rb_col = iota((128, 32), 0), iota((128, 32), 1)
    v = rb_row & 15
    src = jnp.where(v < 3, v * 8 + (((rb_row >> 4) + e) & 7), -1)
    yb[...] = nn(hot(rb_col == src), total.astype(BF16)).astype(BF16).reshape(8, 16, D)
    for d in range(1, 8):
        copy = remote(yb.at[d], ryb.at[d], sy_s.at[d], sy_r.at[d], over_e(ahead(e, d)))
        copy.start()
        sends.append(copy)

    second_parts(1)

    for d in range(1, 8):
        slot = ogi.at[twin(d)]
        remote(slot, slot, si_s.at[d], si_r.at[d], over_g(twin(d))).wait_recv()
    from_groups = hot(co == ((ro >> 2) & 7) * 16 + (ro >> 5) * 4 + (ro & 3))
    gin[...] = nn(from_groups, ogi[...].reshape(128, D)).astype(BF16).reshape(4, 32, D)

    total = yb[0].astype(F32)
    for d in range(1, 8):
        remote(ryb.at[d], ryb.at[d], sy_s.at[d], sy_r.at[d], over_e(behind(e, d))).wait_recv()
        total = total + ryb[d].astype(F32)
    f3[...] = total[0:8, :]
    last = remote(f3, r3, s3_s.at[0], s3_r.at[0], turned)

    @pl.when(zl != m)
    def _():
        last.start()

    @pl.when(zl == m)
    def _():
        r3[...] = f3[...]

    for p, (lane, count) in enumerate(PARTS):
        total = za[p][0].astype(F32)
        for d in range(1, 8):
            remote(rza[p].at[d], rza[p].at[d], se_s.at[p, d], se_r.at[p, d], over_z(behind(ze, d))).wait_recv()
            total = total + rza[p][d].astype(F32)
        for mm in range(4):
            for t in range(3):
                fd[mm, t : t + 1, lane : lane + count] = total[t * 4 + mm : t * 4 + mm + 1, :]
            fd[mm, 3:8, lane : lane + count] = jnp.zeros((5, count), F32)
    for d, mm in ((1, side_m), (2, far_m), (3, core_m)):
        copy = remote(fd.at[mm], rj.at[m], sj_s.at[d], sj_r.at[d], mate(mm))
        copy.start()
        sends.append(copy)
    rj[m] = fd[m]

    @pl.when(zl != m)
    def _():
        last.wait()

    for d, mm in ((1, side_m), (2, far_m), (3, core_m)):
        remote(fd.at[mm], rj.at[mm], sj_s.at[d], sj_r.at[d], mate(mm)).wait_recv()
    for j in range(3):
        tiles = [jnp.zeros((3, 128), F32)] * 6
        for mm in range(4):
            side = (low, high)[mm % 2][:, :128]
            full = rj[mm, :, j * 128 : (j + 1) * 128]
            rest = rj[mm, :, (512 if j == 2 else 384) : (640 if j == 2 else 512)]
            if j == 1:
                rest = pltpu.roll(rest, 64, axis=1)
            pair = (full, rest * side) if mm % 2 == 0 else (rest * side, full)
            for at in range(2):
                tiles[(3 * mm) // 2 + at] = tiles[(3 * mm) // 2 + at] + pair[at][0:3]
        for tile in range(6):
            wsum[:, j * D + tile * 128 : j * D + (tile + 1) * 128] = tiles[tile]
    wsum[:, 3 * D : 4 * D] = r3[0:3, :]

    for copy in sends:
        copy.wait_send()
    for place, copy in late:

        @pl.when(ze != place)
        def _():
            copy.wait_send()


def hand_over(gin, wgrad, gin_out, wgrad_out, sem):
    copies = [pltpu.make_async_copy(gin, gin_out, sem.at[0]), pltpu.make_async_copy(wgrad, wgrad_out, sem.at[1])]
    for copy in copies:
        copy.start()
    for copy in copies:
        copy.wait()


def shards(features, grad_out, weights, read_start, read_end):
    hbm = pl.BlockSpec(memory_space=pl.ANY)
    vm = pl.BlockSpec(memory_space=pltpu.VMEM)
    dma = pltpu.SemaphoreType.DMA
    results = pl.pallas_call(
        kernel,
        name="tied_rows",
        out_shape=(
            pltpu.VMEM((4, 32, D), BF16),
            pltpu.VMEM((3, 4 * D), F32),
        ),
        in_specs=[hbm] * 5,
        out_specs=(vm, vm),
        scratch_shapes=[
            pltpu.VMEM((4, 32, D), BF16),
            pltpu.VMEM((4, 32, D), BF16),
            pltpu.VMEM((1, READS), I32),
            pltpu.VMEM((1, READS), I32),
            pltpu.VMEM((3, D, D), BF16),
            pltpu.VMEM((3, D, WIN), BF16),
            pltpu.VMEM((D, D), BF16),
            pltpu.VMEM((3, 8, 16, D), BF16),
            pltpu.VMEM((2, 4, 8, 16, D), BF16),
            pltpu.VMEM((512, 512), BF16),
            pltpu.VMEM((8, 16, D), BF16),
            pltpu.VMEM((4, 8, 16, WIN), BF16),
            pltpu.VMEM((3, 4, READS, WIN), BF16),
            pltpu.VMEM((4, READS, D), BF16),
            pltpu.VMEM((READS, D), BF16),
            pltpu.VMEM((4, READS, D), BF16),
            pltpu.VMEM((4, READS, D), BF16),
            pltpu.VMEM((4, 2, READS, 512), BF16),
            pltpu.VMEM((2, 384, 128), F32),
            pltpu.VMEM((2, 8, 48, 128), F32),
            pltpu.VMEM((48, 256), F32),
            pltpu.VMEM((8, 16, 256), F32),
            pltpu.VMEM((384, 256), BF16),
            pltpu.VMEM((3, 4, READS, WIN), BF16),
            pltpu.VMEM((4, READS, PACK), BF16),
            pltpu.VMEM((4, READS, WIN), BF16),
            pltpu.VMEM((4, 3, 4, 32, WIN), BF16),
            pltpu.VMEM((D, 512), BF16),
            pltpu.VMEM((WIN, 512), BF16),
            pltpu.VMEM((8, 96, PARTS[0][1]), BF16),
            pltpu.VMEM((8, 96, PARTS[1][1]), BF16),
            pltpu.VMEM((8, 96, PARTS[0][1]), BF16),
            pltpu.VMEM((8, 96, PARTS[1][1]), BF16),
            pltpu.VMEM((8, 32, D), BF16),
            pltpu.VMEM((8, 32, D), BF16),
            pltpu.VMEM((8, 16, PARTS[0][1]), BF16),
            pltpu.VMEM((8, 16, PARTS[1][1]), BF16),
            pltpu.VMEM((8, 16, PARTS[0][1]), BF16),
            pltpu.VMEM((8, 16, PARTS[1][1]), BF16),
            pltpu.VMEM((8, 16, D), BF16),
            pltpu.VMEM((8, 16, D), BF16),
            pltpu.VMEM((4, 8, PACK), F32),
            pltpu.VMEM((4, 8, PACK), F32),
            pltpu.VMEM((8, D), F32),
            pltpu.VMEM((8, D), F32),
            pltpu.VMEM((8, 16, D), BF16),
            pltpu.VMEM((8, 16, D), BF16),
            dma((4,)), dma((7,)),
            dma((3, 8)), dma((3, 8)), dma((2, 4)), dma((2, 4)),
            dma((2, 2)), dma((2, 2)), dma((2, 2)), dma((2, 2)), dma((2, 2)), dma((2, 2)),
            dma((2, 8)), dma((2, 8)),
            dma((3,)), dma((8,)),
            dma((8,)), dma((3,)),
            dma((8,)), dma((8,)),
            dma((4,)), dma((4,)),
            dma((2, 8)), dma((2, 8)),
            dma((2, 8)), dma((2, 8)),
            dma((8,)), dma((8,)),
            dma((8,)), dma((8,)),
            dma((4,)), dma((4,)),
            dma((1,)), dma((1,)),
            dma((8,)), dma((8,)),
        ],
        compiler_params=pltpu.CompilerParams(
            collective_id=0, has_side_effects=True, vmem_limit_bytes=56 * 1024 * 1024
        ),
    )(features, grad_out, read_start.reshape(1, READS), read_end.reshape(1, READS), weights)
    return pl.pallas_call(
        hand_over,
        name="hand_over",
        out_shape=tuple(jax.ShapeDtypeStruct(r.shape, r.dtype) for r in results),
        in_specs=[vm, vm],
        out_specs=(hbm, hbm),
        scratch_shapes=[dma((2,))],
        compiler_params=pltpu.CompilerParams(vmem_limit_bytes=4 * 1024 * 1024),
    )(*results)


def solution(mesh):
    in_specs = (P("read", "pos", None), P("read", "pos", None), P(), P(), P())
    out_specs = (P("read", "pos", None), P(("read", "pos"), None))
    return jax.shard_map(shards, mesh=mesh, in_specs=in_specs, out_specs=out_specs, check_vma=False)
```
